32 devices in a mesh: dp: 2 (over z_hi), expert: 8 (over y, x, core), tensor: 2 (over z_lo).
Axes of the slice: x: 2, y: 2, z: 4 (z_hi: 2, z_lo: 2; z = z_hi * 2 + z_lo), core: 2. Of those that a mesh axis runs over, the one named last changes fastest.
Arguments:
- tokens: bfloat16 [15760, 768], P(('dp', 'expert')), may hold values from -6 to 6
- cotangent: bfloat16 [15760, 768], P(('dp', 'expert')), may hold values from -6 to 6
- ln1_gain: float32 [768], P(('dp', 'expert')), may hold values from 0.5 to 1.5
- ln1_bias: float32 [768], P(('dp', 'expert')), may hold values from -0.625 to 0.625
- ln2_gain: float32 [768], P(('dp', 'expert')), may hold values from 0.5 to 1.5
- ln2_bias: float32 [768], P(('dp', 'expert')), may hold values from -0.625 to 0.625
- w_query: float32 [768, 768], P(('dp', 'expert'), 'tensor'), may hold values from -0.3125 to 0.3125
- w_key: float32 [768, 768], P(('dp', 'expert'), 'tensor'), may hold values from -0.3125 to 0.3125
- w_value: float32 [768, 768], P(('dp', 'expert'), 'tensor'), may hold values from -0.21875 to 0.21875
- w_out: float32 [768, 768], P('tensor', ('dp', 'expert')), may hold values from -1.5 to 1.5
- w_router: float32 [768, 8], P(('dp', 'expert')), may hold values from -0.15625 to 0.15625
- w_in: float32 [8, 768, 3072], P('expert', 'dp', 'tensor'), may hold values from -0.21875 to 0.21875
- w_back: float32 [8, 3072, 768], P('expert', 'tensor', 'dp'), may hold values from -0.875 to 0.875
- expert_ids: int32 [15760, 2], P(('dp', 'expert')), may hold values from 0 to 7, all different within a row; in each aligned block of 985 rows (0 to 984, 985 to 1969, ...) at most 312 rows name the same one
Outputs:
- block_out: bfloat16 [15760, 768], P(('dp', 'expert'))
- grad_tokens: float32 [15760, 768], P(('dp', 'expert'))
- grad_ln1_gain: float32 [768], P(('dp', 'expert'))
- grad_ln1_bias: float32 [768], P(('dp', 'expert'))
- grad_ln2_gain: float32 [768], P(('dp', 'expert'))
- grad_ln2_bias: float32 [768], P(('dp', 'expert'))
- grad_query: float32 [768, 768], P(('dp', 'expert'), 'tensor')
- grad_key: float32 [768, 768], P(('dp', 'expert'), 'tensor')
- grad_value: float32 [768, 768], P(('dp', 'expert'), 'tensor')
- grad_out: float32 [768, 768], P('tensor', ('dp', 'expert'))
- grad_router: float32 [768, 8], P(('dp', 'expert'))
- grad_in: float32 [8, 768, 3072], P('expert', 'dp', 'tensor')
- grad_back: float32 [8, 3072, 768], P('expert', 'tensor', 'dp')
The draws below stay inside these ranges and needn't reach their ends.
Inputs may be any that keep to these rules, and one draw needn't show every extreme that they name: `expert_ids`: each row names two different experts; in each aligned block of 985 rows (the tokens of one group) no expert is named more than 312 times, and in every draw some expert is named exactly 312 times in some block.
All inputs are finite; a program needn't handle non-finite values.
Results may differ from the reference program's by a relative error of at most 0.014.
The reference program's roundings to bfloat16 on the way count: a program that leaves them out, or rounds other values in their place, can miss the bound.
Values may be sent and summed in bfloat16 or wider, within the bound.
No kernel may reach another device: no remote copies, remote signals or barrier semaphores. Data moves between devices by JAX's collectives and lax.ppermute only.
A program may use at most 192 MiB of HBM per device.

```python
import math
import jax
import jax.numpy as jnp
import numpy as np
from jax import lax

D = 768
HEADS = 12
FF = 3072
SEQ = 197
IMG_DEV = 5
EXPERTS = 8
GROUPS = 16
TOK_DEV = 985
IMAGES = 80
TOKENS = 15760
CAP = 312
N_DP = 2
N_EXPERT = 8


def shard_levels(stream_key, dims, shards, smallest, high):
    level = 1.0
    for dim, parts in shards:
        heights = jax.random.uniform(jax.random.fold_in(jax.random.fold_in(stream_key, 6), dim), (parts,), jnp.float32, smallest / len(shards), high / len(shards))
        level = level * jnp.repeat(jnp.exp(heights), dims[dim] // parts).reshape((-1,) + (1,) * (len(dims) - 1 - dim))
    return level


def assign_block(rng, own, number, rows, count, top, bound, slope):
    order = jax.random.permutation(rng, count)
    crowded, usual = load_shares(count, rows * top, bound, slope, True), load_shares(count, rows * top, bound, slope, False)
    places = jnp.arange(count)

    def named(tallies, turn):
        used = int((tallies > 0).sum())
        fixed = max(1, used // 4)
        passed = fixed + (places - fixed + turn * (used - fixed)) % max(1, count - fixed)
        return jnp.zeros((count,), jnp.int32).at[order[jnp.where(places < fixed, places, passed)]].set(jnp.asarray(tallies, jnp.int32))

    tallies = jnp.where(number % 4 == 0, named(crowded, number // 4), named(usual, number - number // 4 - 1))
    mixed = jax.random.permutation(jax.random.fold_in(own, 3), count)
    source_of, receiver = mixed[0:count // 2 * 2:2], mixed[1:count // 2 * 2:2]
    room = jnp.minimum(tallies[source_of] - 1, bound - tallies[receiver]) // 2
    room = jnp.where((source_of == order[0]) | (receiver == order[0]) | (tallies[receiver] == 0), 0, jnp.maximum(room, 0))
    passed = jax.random.randint(jax.random.fold_in(own, 4), (count // 2,), 0, 1 << 20) % (room + 1)
    tallies = tallies.at[source_of].add(-passed).at[receiver].add(passed)
    members = jnp.searchsorted(jnp.cumsum(tallies), jnp.arange(rows * top), side="right").astype(jnp.int32)
    listing = members.reshape(top, rows).T
    listing = listing[jax.random.permutation(jax.random.fold_in(own, 1), rows)]
    turn = jax.random.randint(jax.random.fold_in(own, 2), (rows, 1), 0, top)
    return jnp.take_along_axis(listing, (jnp.arange(top)[None, :] + turn) % top, axis=1)


def load_shares(number_of, total, bound, slope, full):
    portions = [(1 << 20) // math.isqrt(rank ** slope) + 1 for rank in range(1, number_of + 1)]
    largest = bound if full else min(bound, max(-(-total // number_of), total * portions[0] // sum(portions)))
    least = 1 if total - largest >= number_of - 1 else 0
    holding, rest = [largest] + [least] * (number_of - 1), total - largest - least * (number_of - 1)
    while rest > 0:
        candidates = [i for i in range(1, number_of) if holding[i] < largest] or [i for i in range(1, number_of) if holding[i] < bound]
        pool, budget = sum([portions[i] for i in candidates]), rest
        for i in candidates:
            extra = min(bound - holding[i], max(1, budget * portions[i] // pool), rest)
            holding[i] = holding[i] + extra
            rest = rest - extra
    return np.array(holding)


def scatter_about(own_key, dims, width, most, cuts=(), kind=jnp.bfloat16):
    result = width * jax.random.normal(own_key, dims, jnp.float32)
    if cuts:
        result = result * shard_levels(own_key, dims, cuts, -0.22, 0.18)
    return jnp.clip(result, -most, most).astype(kind)


def setup_inputs(seed: int = 0) -> dict:
    streams_of = jax.random.split(jax.random.key(seed), 15)
    tokens = scatter_about(streams_of[0], (TOKENS, D), 1.0, 6.0, ((0, 16),))
    cotangent = scatter_about(streams_of[1], (TOKENS, D), 1.0, 6.0, ((0, 16),))
    ln1_gain = jnp.clip(1.0 + 0.1 * jax.random.normal(streams_of[2], (D,), jnp.float32), 0.5, 1.5)
    ln1_bias = scatter_about(streams_of[3], (D,), 0.1, 0.625, ((0, 16),), jnp.float32)
    ln2_gain = jnp.clip(1.0 + 0.1 * jax.random.normal(streams_of[4], (D,), jnp.float32), 0.5, 1.5)
    ln2_bias = scatter_about(streams_of[5], (D,), 0.1, 0.625, ((0, 16),), jnp.float32)
    w_query = scatter_about(streams_of[6], (D, D), (D // 2) ** -0.5, 0.3125, ((0, 16), (1, 2)), jnp.float32)
    w_key = scatter_about(streams_of[7], (D, D), (D // 2) ** -0.5, 0.3125, ((0, 16), (1, 2)), jnp.float32)
    w_value = scatter_about(streams_of[8], (D, D), D ** -0.5, 0.21875, ((0, 16), (1, 2)), jnp.float32)
    w_out = scatter_about(streams_of[9], (D, D), (max(1, 4 * D // SEQ)) ** -0.5, 1.5, ((0, 2), (1, 16)), jnp.float32)
    w_router = scatter_about(streams_of[10], (D, EXPERTS), (2 * D) ** -0.5, 0.15625, ((0, 16),), jnp.float32)
    w_in = scatter_about(streams_of[11], (EXPERTS, D, FF), D ** -0.5, 0.21875, ((0, 8), (1, 2), (2, 2)), jnp.float32)
    w_back = scatter_about(streams_of[12], (EXPERTS, FF, D), (max(1, FF // (EXPERTS * EXPERTS))) ** -0.5, 0.875, ((0, 8), (1, 2), (2, 2)), jnp.float32)
    expert_ids_keys = jax.random.split(jax.random.fold_in(streams_of[13], 1), TOKENS // TOK_DEV)
    expert_ids_turns = jax.random.permutation(jax.random.fold_in(streams_of[13], 3), TOKENS // TOK_DEV)
    expert_ids = jax.vmap(lambda own, number: assign_block(jax.random.fold_in(streams_of[13], 2), own, number, TOK_DEV, EXPERTS, 2, CAP, 1))(expert_ids_keys, expert_ids_turns).reshape((TOKENS, 2))
    return {"tokens": tokens, "cotangent": cotangent, "ln1_gain": ln1_gain, "ln1_bias": ln1_bias, "ln2_gain": ln2_gain, "ln2_bias": ln2_bias, "w_query": w_query, "w_key": w_key, "w_value": w_value, "w_out": w_out, "w_router": w_router, "w_in": w_in, "w_back": w_back, "expert_ids": expert_ids}


@jax.custom_vjp
def low(v):
    return lax.optimization_barrier(v.astype(jnp.bfloat16)).astype(jnp.float32)

@jax.custom_vjp
def low_back(v):
    return v

def low_keep(v):
    return (low(v), None)

def low_pass(kept, grad):
    return (grad,)

def back_keep(v):
    return (v, None)

def back_low(kept, grad):
    return (low(grad),)
low.defvjp(low_keep, low_pass)
low_back.defvjp(back_keep, back_low)
EPSILON = 1e-06
HIGH = lax.Precision.HIGHEST

def norm_rows(values, gain, bias):
    average = lax.optimization_barrier(jnp.mean(values, axis=-1, keepdims=True))
    centred = values - average
    variance = lax.optimization_barrier(jnp.mean(centred * centred, axis=-1, keepdims=True))
    return centred * lax.rsqrt(variance + EPSILON) * gain + bias

def slot_table(routes, expert_count):
    total = routes.shape[0]
    sequence = jnp.transpose(routes).reshape(-1)
    onehot = (sequence[:, None] == jnp.arange(expert_count, dtype=jnp.int32)[None, :]).astype(jnp.int32)
    before = jnp.cumsum(onehot, axis=0) - onehot
    placed = lax.optimization_barrier(jnp.sum(before * onehot, axis=1)).reshape(2, total)
    return jnp.transpose(placed)

def attend_block(triple):
    query_b, key_b, value_b = triple
    score_scale = (D // HEADS) ** (-0.5)
    scores = jnp.einsum('bqhd,bkhd->bhqk', query_b, key_b, precision=HIGH) * score_scale
    scores = low_back(scores)
    weights = jax.nn.softmax(scores, axis=-1)
    return jnp.einsum('bhqk,bkhd->bqhd', low(weights), value_b, precision=HIGH)

def reference(tokens, cotangent, ln1_gain, ln1_bias, ln2_gain, ln2_bias, w_query, w_key, w_value, w_out, w_router, w_in, w_back, expert_ids):
    grouped = expert_ids.reshape(GROUPS, TOK_DEV, 2)
    slots = jax.vmap(lambda routes: slot_table(routes, EXPERTS))(grouped)
    group_ids = jnp.arange(GROUPS, dtype=jnp.int32)
    replica = group_ids // N_EXPERT
    source = group_ids % N_EXPERT
    slot_index = (replica[:, None, None] * (EXPERTS * N_EXPERT * CAP) + grouped * (N_EXPERT * CAP) + source[:, None, None] * CAP + slots).reshape(-1)
    route_flat = expert_ids

    def forward(inputs, gain_one, bias_one, gain_two, bias_two, query_w, key_w, value_w, out_w, router_w, first_w, second_w):
        gain_one, bias_one, gain_two, bias_two = (low(gain_one), low(bias_one), low(gain_two), low(bias_two))
        query_w, key_w, value_w, out_w = (low(query_w), low(key_w), low(value_w), low(out_w))
        router_w, first_w, second_w = (low(router_w), low(first_w), low(second_w))
        a_rows = low(norm_rows(inputs, gain_one, bias_one))
        query = low(low_back(jnp.dot(a_rows, query_w, precision=HIGH)))
        keys = low(low_back(jnp.dot(a_rows, key_w, precision=HIGH)))
        values = low(low_back(jnp.dot(a_rows, value_w, precision=HIGH)))
        shape_five = (IMAGES // IMG_DEV, IMG_DEV, SEQ, HEADS, D // HEADS)
        attended = lax.map(jax.checkpoint(attend_block), (query.reshape(shape_five), keys.reshape(shape_five), values.reshape(shape_five)))
        attended = low(low_back(attended.reshape(TOKENS, D)))
        middle = inputs + low_back(jnp.dot(attended, out_w, precision=HIGH))
        h_rows = low(norm_rows(middle, gain_two, bias_two))
        router_probs = jax.nn.softmax(jnp.dot(h_rows, router_w, precision=HIGH), axis=-1)
        gate_values = jnp.take_along_axis(router_probs, route_flat, axis=1)
        buffer = jnp.zeros((N_DP * EXPERTS * N_EXPERT * CAP, D), jnp.float32).at[slot_index].set(jnp.repeat(h_rows, 2, axis=0))
        rows_in = low_back(buffer).reshape(N_DP * EXPERTS, N_EXPERT * CAP, D)

        def expert_block(item):
            block, owner = item
            first = lax.dynamic_index_in_dim(first_w, owner, 0, False)
            second = lax.dynamic_index_in_dim(second_w, owner, 0, False)
            pre_act = low_back(jnp.dot(block, first, precision=HIGH))
            hidden = low(jax.nn.gelu(pre_act, approximate=False))
            return low(low_back(jnp.dot(hidden, second, precision=HIGH)))
        owners = jnp.arange(N_DP * EXPERTS, dtype=jnp.int32) % EXPERTS
        expert_rows = lax.map(jax.checkpoint(expert_block), (rows_in, owners))
        picked = jnp.take(expert_rows.reshape(-1, D), slot_index, axis=0).reshape(TOKENS, 2, D)
        return middle + lax.optimization_barrier(jnp.sum(gate_values[:, :, None] * picked, axis=1))
    primal, pullback = jax.vjp(forward, tokens.astype(jnp.float32), ln1_gain, ln1_bias, ln2_gain, ln2_bias, w_query, w_key, w_value, w_out, w_router, w_in, w_back)
    grads = pullback(cotangent.astype(jnp.float32))
    return (primal.astype(jnp.bfloat16), grads[0], grads[1], grads[2], grads[3], grads[4], grads[5], grads[6], grads[7], grads[8], grads[9], grads[10], grads[11])
```

```python
import functools

import jax
import jax.numpy as jnp
from jax import lax
from jax.experimental import pallas as pl
from jax.experimental.pallas import tpu as pltpu
from jax.sharding import PartitionSpec as P

D = 768
HEADS = 12
SEQ = 197
HEAD = D // HEADS
SCALE = HEAD ** (-0.5)
EPSILON = 1e-06
HIGH = lax.Precision.HIGHEST
BF = jnp.bfloat16
F32 = jnp.float32


def norm_rows(values, gain, bias):
    average = jnp.mean(values, axis=-1, keepdims=True)
    centred = values - average
    variance = jnp.mean(centred * centred, axis=-1, keepdims=True)
    return centred * lax.rsqrt(variance + EPSILON) * gain + bias


def gelu_exact(values):
    return jax.nn.gelu(values, approximate=False)


def slot_table(routes, expert_count):
    total = routes.shape[0]
    sequence = jnp.transpose(routes).reshape(-1)
    onehot = (sequence[:, None] == jnp.arange(expert_count, dtype=jnp.int32)[None, :]).astype(
        jnp.int32
    )
    before = jnp.cumsum(onehot, axis=0) - onehot
    return jnp.sum(before * onehot, axis=1).reshape(2, total)


def hop(value, axis, offset):
    count = lax.axis_size(axis)
    return lax.ppermute(value, axis, [(i, i ^ offset) for i in range(count)])


def after(value, *others):
    return lax.optimization_barrier((value,) + others)[0]


def in_order(first, own, other, axis):
    return jnp.where(
        first, jnp.concatenate([own, other], axis), jnp.concatenate([other, own], axis)
    )


def gather_rows(shard):
    count = lax.axis_size("expert")
    here_dp = lax.axis_index("dp")
    here = lax.axis_index("expert")
    across = hop(shard, "dp", 1)
    pair = jnp.where(here_dp == 0, jnp.stack([shard, across]), jnp.stack([across, shard]))
    same = [pair] + [hop(pair, "expert", k) for k in range(2, count, 2)]
    flipped = [hop(p, "expert", 1) for p in same]
    buffer = jnp.zeros((2, count) + shard.shape, shard.dtype)
    for j in range(count // 2):
        buffer = lax.dynamic_update_slice(buffer, same[j][:, None], (0, here ^ (2 * j), 0, 0))
        buffer = lax.dynamic_update_slice(
            buffer, flipped[j][:, None], (0, here ^ (2 * j + 1), 0, 0)
        )
    return buffer.reshape(-1, shard.shape[1]), across


def scatter_sum(grad, wide):
    count = lax.axis_size("expert")
    here_dp = lax.axis_index("dp")
    here = lax.axis_index("expert")
    core = here & 1
    chip = here >> 1
    blocks = grad.reshape((2, count // 2, 2, -1) + grad.shape[1:])
    pick = lambda array, index, axis: lax.dynamic_index_in_dim(array, index, axis, False)
    total = pick(blocks, core, 2) + hop(
        pick(blocks, 1 - core, 2).astype(wide), "expert", 1
    ).astype(F32)
    summed = pick(total, chip, 1)
    for k in range(1, count // 2):
        summed = summed + hop(pick(total, chip ^ k, 1).astype(wide), "expert", 2 * k).astype(F32)
    return pick(summed, here_dp, 0) + hop(
        pick(summed, 1 - here_dp, 0).astype(wide), "dp", 1
    ).astype(F32)


def trade_blocks(blocks):
    return [blocks[0]] + [hop(blocks[k], "expert", k) for k in range(1, len(blocks))]


def send_kernel(rows_ref, values_ref, gates_ref, out_ref, *, gated):
    capacity = out_ref.shape[1]
    base = pl.program_id(0) * capacity
    places = lax.broadcasted_iota(jnp.int32, (capacity, 1), 0) + base
    first = places == rows_ref[0:1, :]
    second = places == rows_ref[1:2, :]
    chosen = jnp.where(first | second, 1.0, 0.0).astype(BF)
    picked = jnp.dot(chosen, values_ref[...], preferred_element_type=F32)
    if gated:
        weight = jnp.where(first, gates_ref[0:1, :], 0.0) + jnp.where(
            second, gates_ref[1:2, :], 0.0
        )
        picked = picked * jnp.sum(weight, axis=1, keepdims=True)
    out_ref[0] = picked.astype(BF)


def send_rows(rows, values, gates, count, capacity, gated):
    total = values.shape[0]
    return pl.pallas_call(
        functools.partial(send_kernel, gated=gated),
        grid=(count,),
        in_specs=[
            pl.BlockSpec((2, total), lambda i: (0, 0)),
            pl.BlockSpec((total, D), lambda i: (0, 0)),
            pl.BlockSpec((2, total), lambda i: (0, 0)),
        ],
        out_specs=pl.BlockSpec((1, capacity, D), lambda i: (i, 0, 0)),
        out_shape=jax.ShapeDtypeStruct((count, capacity, D), BF),
        name="send_gated" if gated else "send_rows",
        cost_estimate=pl.CostEstimate(
            flops=2 * count * capacity * total * D, bytes_accessed=8_000_000, transcendentals=0
        ),
    )(rows, values, gates)


TILE = 200


def home_kernel(rows_ref, back_ref, middle_ref, grad_ref, gates_ref, out_ref, dgate_ref):
    total = back_ref.shape[0]
    places = lax.broadcasted_iota(jnp.int32, (1, total), 1)
    value = middle_ref[...]
    columns = lax.broadcasted_iota(jnp.int32, (TILE, 128), 1)
    found = jnp.zeros((TILE, 128), F32)
    for c in range(2):
        chosen = jnp.where(rows_ref[:, c : c + 1] == places, 1.0, 0.0).astype(BF)
        picked = jnp.dot(chosen, back_ref[...], preferred_element_type=F32)
        value = value + gates_ref[:, c : c + 1] * picked
        dgate = jnp.sum(picked * grad_ref[...].astype(F32), axis=1, keepdims=True)
        found = jnp.where(columns == c, dgate, found)
    out_ref[...] = value.astype(BF)
    dgate_ref[...] = found


def bring_home(rows, back, middle, grad, gates):
    total, width = middle.shape
    count = back.shape[0]
    tile = lambda w: pl.BlockSpec((TILE, w), lambda i: (i, 0))
    return pl.pallas_call(
        home_kernel,
        grid=(pl.cdiv(total, TILE),),
        in_specs=[
            tile(2),
            pl.BlockSpec((count, width), lambda i: (0, 0)),
            tile(width),
            tile(width),
            tile(2),
        ],
        out_specs=[tile(width), tile(128)],
        out_shape=[
            jax.ShapeDtypeStruct((total, width), BF),
            jax.ShapeDtypeStruct((total, 128), F32),
        ],
        name="bring_home",
        cost_estimate=pl.CostEstimate(
            flops=4 * count * total * width, bytes_accessed=8_000_000, transcendentals=0
        ),
    )(rows, back, middle, grad, gates)


def sum_kernel(rows_ref, back_ref, out_ref):
    places = lax.broadcasted_iota(jnp.int32, (1, back_ref.shape[0]), 1)
    chosen = (rows_ref[:, 0:1] == places) | (rows_ref[:, 1:2] == places)
    out_ref[...] = jnp.dot(
        jnp.where(chosen, 1.0, 0.0).astype(BF), back_ref[...], preferred_element_type=F32
    ).astype(BF)


def sum_home(rows, back):
    total = rows.shape[0]
    count, width = back.shape
    tile = lambda w: pl.BlockSpec((TILE, w), lambda i: (i, 0))
    return pl.pallas_call(
        sum_kernel,
        grid=(pl.cdiv(total, TILE),),
        in_specs=[tile(2), pl.BlockSpec((count, width), lambda i: (0, 0))],
        out_specs=tile(width),
        out_shape=jax.ShapeDtypeStruct((total, width), BF),
        name="sum_home",
        cost_estimate=pl.CostEstimate(
            flops=2 * count * total * width, bytes_accessed=6_000_000, transcendentals=0
        ),
    )(rows, back)


def on_device(
    tokens,
    cotangent,
    ln1_gain,
    ln1_bias,
    ln2_gain,
    ln2_bias,
    w_query,
    w_key,
    w_value,
    w_out,
    w_router,
    w_in,
    w_back,
    expert_ids,
):
    count = lax.axis_size("expert")
    tok = tokens.shape[0]
    capacity = (10 * tok + 32 * count - 1) // (32 * count) * 8
    images = tok // SEQ
    here = lax.axis_index("expert")
    here_dp = lax.axis_index("dp")
    here_t = lax.axis_index("tensor")
    half = D // 2

    small = jnp.stack([ln1_gain, ln1_bias, ln2_gain, ln2_bias], axis=1)
    narrow = jnp.concatenate([small, w_router], axis=1)
    narrow = jnp.pad(narrow, ((0, 0), (0, 128 - narrow.shape[1])))
    first_pack = jnp.concatenate([w_query, w_key, w_value, narrow], axis=1).astype(BF)
    packed, crossed = gather_rows(first_pack)
    query_w = packed[:, :half]
    key_w = packed[:, half : 2 * half]
    value_w = packed[:, 2 * half : 3 * half]
    vectors = packed[:, 3 * half : 3 * half + 4].astype(F32)
    gain_a, bias_a, gain_b, bias_b = (vectors[:, i] for i in range(4))
    router_w = packed[:, 3 * half + 4 : 3 * half + 4 + count]
    out_own = jnp.transpose(w_out).astype(BF)
    out_pair = in_order(here_t == 0, out_own, hop(after(out_own, crossed), "tensor", 1), 1)
    out_t, crossed_out = gather_rows(out_pair)
    out_here = lax.dynamic_slice_in_dim(out_t, here_t * half, half, 1)

    in_own = w_in[0].astype(BF)
    back_own = w_back[0].astype(BF)
    first_w = in_order(here_dp == 0, in_own, hop(after(in_own, crossed_out), "dp", 1), 0)
    second_w = in_order(here_dp == 0, back_own, hop(after(back_own, first_w[:8]), "dp", 1), 1)

    slots = slot_table(expert_ids, count)
    ids = jnp.transpose(expert_ids)
    rows_lane = (ids ^ here) * capacity + slots
    rows = jnp.transpose(rows_lane)

    inputs = tokens.astype(F32)
    a_rows = norm_rows(inputs, gain_a, bias_a).astype(BF)
    dot = functools.partial(jnp.dot, preferred_element_type=F32)
    ein = functools.partial(jnp.einsum, preferred_element_type=F32)
    heads_here = half // HEAD
    shape = (images, SEQ, heads_here, HEAD)
    query = dot(a_rows, query_w).astype(BF).reshape(shape)
    keys = dot(a_rows, key_w).astype(BF).reshape(shape)
    values = dot(a_rows, value_w).astype(BF).reshape(shape)
    scores = ein("bqhd,bkhd->bhqk", query, keys) * SCALE
    log_total = jax.nn.logsumexp(scores, axis=-1, keepdims=True)
    weights = jnp.exp(scores - log_total)
    attended = ein("bhqk,bkhd->bqhd", weights.astype(BF), values).astype(BF).reshape(tok, -1)
    attended_all = in_order(here_t == 0, attended, hop(attended, "tensor", 1), 1)
    middle = inputs + ein("tc,dc->td", attended_all, out_t)

    h_rows = norm_rows(middle, gain_b, bias_b).astype(BF)
    router_probs = jax.nn.softmax(dot(h_rows, router_w), axis=-1)
    lanes = jnp.arange(count, dtype=jnp.int32)[None, :]
    chosen = [(expert_ids[:, c : c + 1] == lanes).astype(F32) for c in range(2)]
    gates = jnp.stack([jnp.sum(router_probs * chosen[c], axis=1) for c in range(2)], axis=1)
    gates_lane = jnp.transpose(gates)
    outgoing = send_rows(rows_lane, h_rows, gates_lane, count, capacity, False)
    arrived = jnp.concatenate(trade_blocks([outgoing[k] for k in range(count)]), axis=0)
    grad_out_rows = send_rows(
        rows_lane, cotangent, after(gates_lane, outgoing[0, :8]), count, capacity, True
    )
    grad_arrived = jnp.concatenate(trade_blocks([grad_out_rows[k] for k in range(count)]), axis=0)

    pre_act = dot(arrived, first_w)
    hidden = gelu_exact(pre_act).astype(BF)
    second_there = lax.dynamic_slice_in_dim(second_w, (1 - here_t) * half, half, 1)
    second_here = lax.dynamic_slice_in_dim(second_w, here_t * half, half, 1)
    part_there = dot(hidden, second_there).astype(BF)
    part_here = dot(hidden, second_here)
    returned = (part_here + hop(part_there, "tensor", 1).astype(F32)).astype(BF)
    returned = returned.reshape(count, capacity, half)
    came_back = jnp.concatenate(trade_blocks([returned[k] for k in range(count)]), axis=0)

    grad_second = ein("rf,rd->fd", hidden, grad_arrived)
    grad_hidden = ein("rd,fd->rf", grad_arrived, second_w)
    _, gelu_pull = jax.vjp(gelu_exact, pre_act)
    grad_pre = gelu_pull(grad_hidden)[0].astype(BF)
    first_there = lax.dynamic_slice_in_dim(first_w, (1 - here_t) * half, half, 0)
    first_here = lax.dynamic_slice_in_dim(first_w, here_t * half, half, 0)
    input_there = ein("rf,df->rd", grad_pre, first_there).astype(BF)
    input_here = ein("rf,df->rd", grad_pre, first_here)
    grad_rows = (input_here + hop(input_there, "tensor", 1).astype(F32)).astype(BF)
    grad_rows = grad_rows.reshape(count, capacity, half)
    grad_home = jnp.concatenate(trade_blocks([grad_rows[k] for k in range(count)]), axis=0)
    grad_first = ein("rd,rf->df", arrived, grad_pre)

    def share(grad, axis):
        size = grad.shape[axis] // 2
        there = lax.dynamic_slice_in_dim(grad, (1 - here_dp) * size, size, axis).astype(BF)
        own = lax.dynamic_slice_in_dim(grad, here_dp * size, size, axis)
        return own + hop(there, "dp", 1).astype(F32)

    grad_back = share(grad_second, 1)[None]
    grad_in = share(grad_first, 0)[None]

    middle_half = lax.dynamic_slice_in_dim(middle, here_t * half, half, 1)
    cot_half = lax.dynamic_slice_in_dim(cotangent, here_t * half, half, 1)
    out_half, dgate_part = bring_home(rows, came_back, middle_half, cot_half, gates)
    block_out = in_order(here_t == 0, out_half, hop(out_half, "tensor", 1), 1)
    dgate_part = jnp.transpose(dgate_part[:, :2])
    grad_gates = jnp.transpose(dgate_part + hop(dgate_part, "tensor", 1))
    grad_probs = sum(chosen[c] * grad_gates[:, c : c + 1] for c in range(2))
    grad_logits = router_probs * (
        grad_probs - jnp.sum(router_probs * grad_probs, axis=-1, keepdims=True)
    )
    h_float = h_rows.astype(F32)
    grad_router = jnp.dot(jnp.transpose(h_float), grad_logits, precision=HIGH)
    grad_h_router = jnp.dot(grad_logits, jnp.transpose(router_w.astype(F32)), precision=HIGH)

    moe_half = sum_home(rows, grad_home)
    moe_all = in_order(here_t == 0, moe_half, hop(moe_half, "tensor", 1), 1)
    grad_h = moe_all.astype(F32) + grad_h_router
    _, norm_two_pull = jax.vjp(norm_rows, middle, gain_b, bias_b)
    grad_mid_norm, grad_gain_two, grad_bias_two = norm_two_pull(grad_h)
    grad_middle = cotangent.astype(F32) + grad_mid_norm

    grad_branch = grad_middle.astype(BF)
    grad_outw = ein("td,tc->dc", grad_branch, attended)
    grad_att = dot(grad_branch, out_here).astype(BF).reshape(shape)
    again = ein("bqhd,bkhd->bhqk", query, keys) * SCALE
    weights_again = jnp.exp(again - log_total)
    grad_value = ein("bhqk,bqhd->bkhd", weights_again.astype(BF), grad_att).astype(BF)
    grad_weights = ein("bqhd,bkhd->bhqk", grad_att, values)
    grad_scores = (
        weights_again
        * (grad_weights - jnp.sum(weights_again * grad_weights, axis=-1, keepdims=True))
    ).astype(BF)
    grad_query = (ein("bhqk,bkhd->bqhd", grad_scores, keys) * SCALE).astype(BF)
    grad_key = (ein("bhqk,bqhd->bkhd", grad_scores, query) * SCALE).astype(BF)
    grad_qkv = jnp.concatenate(
        [g.reshape(tok, half) for g in (grad_query, grad_key, grad_value)], axis=1
    )
    qkv_w = packed[:, : 3 * half]
    norm_part = ein("tc,dc->td", grad_qkv, qkv_w).astype(BF)
    grad_normed = norm_part.astype(F32) + hop(norm_part, "tensor", 1).astype(F32)
    grad_wqkv = ein("td,tc->dc", a_rows, grad_qkv)
    _, norm_one_pull = jax.vjp(norm_rows, inputs, gain_a, bias_a)
    grad_in_norm, grad_gain_one, grad_bias_one = norm_one_pull(grad_normed)
    grad_tokens = grad_middle + grad_in_norm

    shard_outw = jnp.transpose(scatter_sum(grad_outw, BF))
    shard_qkv = scatter_sum(grad_wqkv, BF)
    tiny = jnp.concatenate(
        [
            jnp.transpose(grad_router),
            jnp.stack([grad_gain_one, grad_bias_one, grad_gain_two, grad_bias_two]),
        ],
        axis=0,
    )
    for offset in [1 << b for b in range(count.bit_length() - 1)]:
        tiny = tiny + hop(tiny, "expert", offset)
    tiny = tiny + hop(tiny, "dp", 1)
    width = ln1_gain.shape[0]
    tiny = tiny.reshape(-1, 2 * count, width)
    tiny = lax.dynamic_index_in_dim(tiny, here_dp * count + here, 1, False)
    return (
        block_out,
        grad_tokens,
        tiny[count],
        tiny[count + 1],
        tiny[count + 2],
        tiny[count + 3],
        shard_qkv[:, :half],
        shard_qkv[:, half : 2 * half],
        shard_qkv[:, 2 * half :],
        shard_outw,
        jnp.transpose(tiny[:count]),
        grad_in,
        grad_back,
    )


def solution(mesh):
    rows = ("dp", "expert")
    in_specs = (
        P(rows, None),
        P(rows, None),
        P(rows),
        P(rows),
        P(rows),
        P(rows),
        P(rows, "tensor"),
        P(rows, "tensor"),
        P(rows, "tensor"),
        P("tensor", rows),
        P(rows, None),
        P("expert", "dp", "tensor"),
        P("expert", "tensor", "dp"),
        P(rows, None),
    )
    out_specs = (
        P(rows, None),
        P(rows, None),
        P(rows),
        P(rows),
        P(rows),
        P(rows),
        P(rows, "tensor"),
        P(rows, "tensor"),
        P(rows, "tensor"),
        P("tensor", rows),
        P(rows, None),
        P("expert", "dp", "tensor"),
        P("expert", "tensor", "dp"),
    )
    return jax.shard_map(
        on_device, mesh=mesh, in_specs=in_specs, out_specs=out_specs, check_vma=False
    )
```

```python
import functools

import jax
import jax.numpy as jnp
from jax import lax
from jax.experimental import pallas as pl
from jax.experimental.pallas import tpu as pltpu
from jax.sharding import PartitionSpec as P

D = 768
HALF = 384
HEADS = 12
SEQ = 197
ROWS = 208
HEAD = D // HEADS
SCALE = HEAD ** (-0.5)
EPSILON = 1e-06
HIGH = lax.Precision.HIGHEST
BF = jnp.bfloat16
F32 = jnp.float32
LANES = 128
TILE = 512
CHUNKS = 4
TAIL_RATE = 0.305
TAIL = (
    0.12163973686996697,
    0.12246675128071258,
    0.10342128505066615,
    0.12102026121907625,
    -0.03797407148483761,
    0.1857138128109823,
    -0.15298645906475614,
    0.03669873020693663,
)
DENSITY = 0.3989422804014327


def hop(value, axis, offset):
    count = lax.axis_size(axis)
    return lax.ppermute(value, axis, [(i, i ^ offset) for i in range(count)])


class Order:
    def __init__(self):
        self.token = lax.create_token()

    def after(self, value):
        return lax.optimization_barrier((self.token, value))[1]

    def wait(self, value):
        self.token, value = lax.optimization_barrier((self.token, value))
        return value

    def run(self, function, *operands):
        return self.wait(function(*self.after(operands)))


def follow(value, first):
    token = lax.optimization_barrier((lax.create_token(), first))[0]
    return lax.optimization_barrier((token, value))[1]


def dot_nn(a, b):
    return lax.dot_general(a, b, (((1,), (0,)), ((), ())), preferred_element_type=F32)


def dot_nt(a, b):
    return lax.dot_general(a, b, (((1,), (1,)), ((), ())), preferred_element_type=F32)


def dot_tn(a, b):
    return lax.dot_general(a, b, (((0,), (0,)), ((), ())), preferred_element_type=F32)


def cost(flops=1000):
    return pl.CostEstimate(flops=flops, bytes_accessed=1000, transcendentals=0)


def image(width, lo=0):
    return pl.BlockSpec((1, ROWS, width), lambda i, *_: (i + lo, 0, 0))


def images(count, width, kind):
    return jax.ShapeDtypeStruct((count, ROWS, width), kind)


ANY = pl.BlockSpec(memory_space=pl.ANY)


def whole(shape):
    zeros = (0,) * len(shape)
    return pl.BlockSpec(shape, lambda *_: zeros)


def cross(shard):
    across = hop(shard, "dp", 1)
    mine = lax.axis_index("dp") == 0
    return jnp.where(mine, jnp.stack([shard, across]), jnp.stack([across, shard]))


def assemble_kernel(here_ref, same_ref, flip_ref, *out_refs):
    chips, _, rows, _ = same_ref.shape
    for chip in range(chips):
        for b, ref in enumerate((same_ref, flip_ref)):
            place = here_ref[0] ^ (2 * chip + b)
            for d in range(2):
                at = pl.ds(pl.multiple_of((d * 2 * chips + place) * rows, 16), rows)
                lo = 0
                for out_ref in out_refs:
                    out_ref[at, :] = ref[chip, d, :, lo : lo + out_ref.shape[1]]
                    lo += out_ref.shape[1]


def assemble(same, flipped, widths):
    chips, _, rows, columns = same.shape
    here = lax.axis_index("expert").astype(jnp.int32)
    if rows % 16 == 0:
        return pl.pallas_call(
            assemble_kernel,
            grid_spec=pltpu.PrefetchScalarGridSpec(
                num_scalar_prefetch=1,
                grid=(1,),
                in_specs=[whole(same.shape), whole(same.shape)],
                out_specs=[whole((4 * chips * rows, w)) for w in widths],
            ),
            out_shape=[jax.ShapeDtypeStruct((4 * chips * rows, w), same.dtype) for w in widths],
            name="assemble",
            cost_estimate=cost(),
        )(here.reshape(1), same, flipped)
    buffer = jnp.zeros((2, 2 * chips, rows, columns), same.dtype)
    for j in range(chips):
        for b, both in enumerate((same, flipped)):
            buffer = lax.dynamic_update_slice(buffer, both[j][:, None], (0, here ^ (2 * j + b), 0, 0))
    buffer = buffer.reshape(-1, columns)
    cuts = [sum(widths[:n]) for n in range(len(widths) + 1)]
    return [buffer[:, cuts[n] : cuts[n + 1]] for n in range(len(widths))]


def chip_copies(pair):
    count = lax.axis_size("expert")
    return [pair] + [hop(pair, "expert", k) for k in range(2, count, 2)]


def scatter_sum(grad, wide):
    count = lax.axis_size("expert")
    here_dp = lax.axis_index("dp")
    here = lax.axis_index("expert")
    core = here & 1
    chip = here >> 1
    blocks = grad.reshape((2, count // 2, 2, -1) + grad.shape[1:])
    pick = lambda array, index, axis: lax.dynamic_index_in_dim(array, index, axis, False)
    total = pick(blocks, core, 2) + hop(
        pick(blocks, 1 - core, 2).astype(wide), "expert", 1
    ).astype(F32)
    summed = pick(total, chip, 1)
    for k in range(1, count // 2):
        summed = summed + hop(pick(total, chip ^ k, 1).astype(wide), "expert", 2 * k).astype(F32)
    return pick(summed, here_dp, 0), pick(summed, 1 - here_dp, 0).astype(wide)


def normed(values):
    average = jnp.mean(values, axis=-1, keepdims=True)
    centred = values - average
    variance = jnp.mean(centred * centred, axis=-1, keepdims=True)
    scale = lax.rsqrt(variance + EPSILON)
    return centred * scale, scale


def attend_kernel(x_ref, vec_ref, w_ref, *refs):
    a_ref, qkv_ref, o_ref, lse_ref, part_ref = refs[-5:]
    hat, _ = normed(x_ref[0].astype(F32))
    a = (hat * vec_ref[0:1, :] + vec_ref[1:2, :]).astype(BF)
    a_ref[0] = a
    qkv_ref[0] = dot_nn(a, w_ref[...]).astype(BF)
    keys_in = lax.broadcasted_iota(jnp.int32, (ROWS, ROWS), 1) < SEQ
    lane = lax.broadcasted_iota(jnp.int32, (ROWS, LANES), 1)
    lse = jnp.zeros((ROWS, LANES), F32)
    for h in range(HALF // HEAD):
        at = h * HEAD
        q = qkv_ref[0, :, at : at + HEAD]
        k = qkv_ref[0, :, HALF + at : HALF + at + HEAD]
        v = qkv_ref[0, :, 2 * HALF + at : 2 * HALF + at + HEAD]
        s = jnp.where(keys_in, dot_nt(q, k) * SCALE, -1e30)
        top = jnp.max(s, axis=1, keepdims=True)
        total = top + jnp.log(jnp.sum(jnp.exp(s - top), axis=1, keepdims=True))
        weights = jnp.exp(s - total).astype(BF)
        part_ref[0, :, at : at + HEAD] = dot_nn(weights, v).astype(BF)
        lse = jnp.where(lane == h, total, lse)
    lse_ref[0] = lse
    o_ref[0] = part_ref[0]


def attend(x, vectors, weight, lo, hi, held):
    total = x.shape[0]
    return pl.pallas_call(
        attend_kernel,
        grid=(hi - lo,),
        in_specs=[image(D, lo), whole(vectors.shape), whole(weight.shape)] + [ANY] * len(held),
        out_specs=[image(D, lo), image(3 * HALF, lo), image(HALF, lo), image(LANES, lo), image(HALF)],
        out_shape=[
            images(total, D, BF),
            images(total, 3 * HALF, BF),
            images(total, HALF, BF),
            images(total, LANES, F32),
            images(hi - lo, HALF, BF),
        ],
        input_output_aliases={3 + n: n for n in range(len(held))},
        name="attend",
        cost_estimate=cost(),
    )(x, vectors, weight, *held)


def route_kernel(
    which_ref, x_ref, own_ref, got_ref, vec_ref, out_w_ref, router_ref, ids_ref, *refs, count
):
    y_ref, r_ref, g_ref, h_ref = refs[-4:]
    y = x_ref[0].astype(F32) + (
        dot_nt(own_ref[0], out_w_ref[:, :HALF]) + dot_nt(got_ref[0], out_w_ref[:, HALF:])
    )
    y_ref[0] = y
    hat, _ = normed(y)
    h = (hat * vec_ref[2:3, :] + vec_ref[3:4, :]).astype(BF)
    first = which_ref[0] == 0
    h_ref[0, :, :HALF] = jnp.where(first, h[:, :HALF], h[:, HALF:])
    h_ref[0, :, HALF:] = jnp.where(first, h[:, HALF:], h[:, :HALF])
    lane = lax.broadcasted_iota(jnp.int32, (ROWS, LANES), 1)
    logits = jnp.where(lane < count, dot_nn(h, router_ref[...]), -1e30)
    logits = jnp.exp(logits - jnp.max(logits, axis=1, keepdims=True))
    probs = logits / jnp.sum(logits, axis=1, keepdims=True)
    r_ref[0] = probs
    gates = jnp.zeros((ROWS, LANES), F32)
    for c in range(2):
        gate = jnp.sum(jnp.where(lane == ids_ref[0, :, c : c + 1], probs, 0.0), axis=1, keepdims=True)
        gates = jnp.where(lane == c, gate, gates)
    g_ref[0] = gates


def route(which, x, own, got, vectors, out_w, router, ids, count, lo, hi, held):
    total = x.shape[0]
    return pl.pallas_call(
        functools.partial(route_kernel, count=count),
        grid_spec=pltpu.PrefetchScalarGridSpec(
            num_scalar_prefetch=1,
            grid=(hi - lo,),
            in_specs=[
                image(D, lo),
                image(HALF),
                image(HALF),
                whole(vectors.shape),
                whole(out_w.shape),
                whole(router.shape),
                image(2, lo),
            ]
            + [ANY] * len(held),
            out_specs=[image(D, lo), image(LANES, lo), image(LANES, lo), image(D)],
        ),
        out_shape=[
            images(total, D, F32),
            images(total, LANES, F32),
            images(total, LANES, F32),
            images(hi - lo, D, BF),
        ],
        input_output_aliases={8 + n: n for n in range(len(held))},
        name="route",
        cost_estimate=cost(),
    )(which, x, own, got, vectors, out_w, router, ids, *held)


def send_kernel(*refs, parts, chips, gated):
    per = 3 if gated else 2
    groups = [refs[n * per * parts : (n + 1) * per * parts] for n in range(2)]
    out_refs = refs[2 * per * parts :]
    capacity = out_refs[0].shape[1]
    for out_ref, chip in zip(out_refs, chips):
        for r in range(2):
            rows, values, gates = (groups[r][n * parts : (n + 1) * parts] for n in range(3))
            places = lax.broadcasted_iota(jnp.int32, (capacity, 1), 0) + (2 * chip + r) * capacity
            picked = jnp.zeros((capacity, D), F32)
            weight = jnp.zeros((capacity, 1), F32)
            for n in range(parts):
                first = places == rows[n][0:1, :]
                second = places == rows[n][1:2, :]
                chosen = jnp.where(first | second, 1.0, 0.0).astype(BF)
                picked = picked + dot_nn(chosen, values[n][...])
                if gated:
                    each = jnp.where(
                        first, gates[n][0:1, :], jnp.where(second, gates[n][1:2, :], 0.0)
                    )
                    weight = weight + jnp.sum(each, axis=1, keepdims=True)
            if gated:
                picked = picked * weight
            out_ref[r] = picked.astype(BF)


def send_rows(own, other, capacity, chips, gated):
    operands = [part for group in (own, other) for kind in group for part in kind]
    return pl.pallas_call(
        functools.partial(send_kernel, parts=len(own[0]), chips=chips, gated=gated),
        grid=(1,),
        in_specs=[whole(o.shape) for o in operands],
        out_specs=[whole((2, capacity, D))] * len(chips),
        out_shape=[jax.ShapeDtypeStruct((2, capacity, D), BF)] * len(chips),
        name="send_gated" if gated else "send_rows",
        cost_estimate=cost(),
    )(*operands)


def home_kernel(which_ref, rows_ref, middle_ref, grad_ref, gates_ref, own_ref, other_ref, out_ref, dgate_ref):
    value = middle_ref[0]
    grad = grad_ref[0].astype(F32)
    lane = lax.broadcasted_iota(jnp.int32, (ROWS, LANES), 1)
    found = jnp.zeros((ROWS, LANES), F32)
    chips, capacity = own_ref.shape[:2]
    places = lax.broadcasted_iota(jnp.int32, (1, capacity), 1)
    for c in range(2):
        picked = jnp.zeros((ROWS, HALF), F32)
        for chip in range(chips):
            for r, back_ref in enumerate((own_ref, other_ref)):
                at = rows_ref[0, :, c : c + 1] - (2 * chip + r) * capacity
                chosen = jnp.where(at == places, 1.0, 0.0)
                picked = picked + dot_nn(chosen.astype(BF), back_ref[chip])
        value = value + gates_ref[0, :, c : c + 1] * picked
        dgate = jnp.sum(picked * grad, axis=1, keepdims=True)
        found = jnp.where(lane == c, dgate, found)
    out_ref[0] = value.astype(BF)
    dgate_ref[0] = found


def bring_home(which, rows, middle, grad, gates, own, other):
    total = middle.shape[0]
    part = pl.BlockSpec((1, ROWS, HALF), lambda i, s: (i, 0, s[0]))
    return pl.pallas_call(
        home_kernel,
        grid_spec=pltpu.PrefetchScalarGridSpec(
            num_scalar_prefetch=1,
            grid=(total,),
            in_specs=[image(2), part, part, image(LANES), whole(own.shape), whole(other.shape)],
            out_specs=[image(HALF), image(LANES)],
        ),
        out_shape=[images(total, HALF, BF), images(total, LANES, F32)],
        name="bring_home",
        cost_estimate=cost(),
    )(which, rows, middle, grad, gates, own, other)


def sum_kernel(rows_ref, own_ref, other_ref, out_ref):
    chips, capacity = own_ref.shape[:2]
    places = lax.broadcasted_iota(jnp.int32, (1, capacity), 1)
    total = jnp.zeros((ROWS, HALF), F32)
    for chip in range(chips):
        for r, back_ref in enumerate((own_ref, other_ref)):
            base = (2 * chip + r) * capacity
            chosen = (rows_ref[0, :, 0:1] - base == places) | (rows_ref[0, :, 1:2] - base == places)
            total = total + dot_nn(jnp.where(chosen, 1.0, 0.0).astype(BF), back_ref[chip])
    out_ref[0] = total.astype(BF)


def sum_home(rows, own, other, lo, hi):
    return pl.pallas_call(
        sum_kernel,
        grid=(hi - lo,),
        in_specs=[image(2, lo), whole(own.shape), whole(other.shape)],
        out_specs=image(HALF),
        out_shape=images(hi - lo, HALF, BF),
        name="sum_home",
        cost_estimate=cost(),
    )(rows, own, other)


def gelu_parts(u):
    size = jnp.abs(u)
    t = 1.0 / (1.0 + TAIL_RATE * size)
    poly = jnp.full_like(t, TAIL[-1])
    for c in TAIL[-2::-1]:
        poly = poly * t + c
    bell = jnp.exp(-0.5 * (u * u))
    tail = bell * (t * poly)
    normal = jnp.where(u >= 0.0, 1.0 - tail, tail)
    return u * normal, normal + u * (DENSITY * bell)


def forward_kernel(m_ref, w1h, w1t, w2h, w2t, g_ref, s_ref, zt_ref, zh_ref, acc):
    step = pl.program_id(0)
    last = pl.num_programs(0) - 1
    for b in range(m_ref.shape[0]):
        u = dot_nn(m_ref[b, :, :HALF], w1h[...]) + dot_nn(m_ref[b, :, HALF:], w1t[...])
        g, slope = gelu_parts(u)
        g = g.astype(BF)
        g_ref[b] = g
        s_ref[b] = slope.astype(BF)
        away = dot_nn(g, w2t[...])
        near = dot_nn(g, w2h[...])

        @pl.when(step == 0)
        def _():
            acc[b] = away
            zh_ref[b] = near

        @pl.when(step > 0)
        def _():
            acc[b] += away
            zh_ref[b] += near

        @pl.when(step == last)
        def _():
            zt_ref[b] = acc[b].astype(BF)


def expert_forward(rows, w1h, w1t, w2h, w2t):
    blocks, capacity, _ = rows.shape
    hidden = w1h.shape[1]
    across = pl.BlockSpec((HALF, TILE), lambda i: (0, i))
    down = pl.BlockSpec((TILE, HALF), lambda i: (i, 0))
    wide = pl.BlockSpec((blocks, capacity, TILE), lambda i: (0, 0, i))
    make = lambda w, t: jax.ShapeDtypeStruct((blocks, capacity, w), t)
    return pl.pallas_call(
        forward_kernel,
        grid=(hidden // TILE,),
        in_specs=[whole(rows.shape), across, across, down, down],
        out_specs=[wide, wide] + [whole((blocks, capacity, HALF))] * 2,
        out_shape=[make(hidden, BF), make(hidden, BF), make(HALF, BF), make(HALF, F32)],
        scratch_shapes=[pltpu.VMEM((blocks, capacity, HALF), F32)],
        name="expert_forward",
        cost_estimate=cost(),
    )(rows, w1h, w1t, w2h, w2t)


def backward_kernel(z_ref, s_ref, w1h, w1t, w2h, w2t, u_ref, mt_ref, mh_ref, acc):
    step = pl.program_id(0)
    last = pl.num_programs(0) - 1
    for b in range(z_ref.shape[0]):
        grad = dot_nt(z_ref[b, :, :HALF], w2h[...]) + dot_nt(z_ref[b, :, HALF:], w2t[...])
        grad = (grad * s_ref[b].astype(F32)).astype(BF)
        u_ref[b] = grad
        away = dot_nt(grad, w1t[...])
        near = dot_nt(grad, w1h[...])

        @pl.when(step == 0)
        def _():
            acc[b] = away
            mh_ref[b] = near

        @pl.when(step > 0)
        def _():
            acc[b] += away
            mh_ref[b] += near

        @pl.when(step == last)
        def _():
            mt_ref[b] = acc[b].astype(BF)


def expert_backward(rows, slope, w1h, w1t, w2h, w2t):
    blocks, capacity, _ = rows.shape
    hidden = w1h.shape[1]
    across = pl.BlockSpec((HALF, TILE), lambda i: (0, i))
    down = pl.BlockSpec((TILE, HALF), lambda i: (i, 0))
    wide = pl.BlockSpec((blocks, capacity, TILE), lambda i: (0, 0, i))
    make = lambda w, t: jax.ShapeDtypeStruct((blocks, capacity, w), t)
    return pl.pallas_call(
        backward_kernel,
        grid=(hidden // TILE,),
        in_specs=[whole(rows.shape), wide, across, across, down, down],
        out_specs=[wide] + [whole((blocks, capacity, HALF))] * 2,
        out_shape=[make(hidden, BF), make(HALF, BF), make(HALF, F32)],
        scratch_shapes=[pltpu.VMEM((blocks, capacity, HALF), F32)],
        name="expert_backward",
        cost_estimate=cost(),
    )(rows, slope, w1h, w1t, w2h, w2t)


def outer_kernel(which_ref, *refs, chunks, hidden_first, added):
    wides = refs[:chunks]
    narrows = refs[chunks : 2 * chunks]
    out_ref = refs[-1]
    total = None
    for wide_ref, slim_ref in zip(wides, narrows):
        for b in range(wide_ref.shape[0]):
            slim = slim_ref[b]
            term = dot_tn(wide_ref[b], slim) if hidden_first else dot_tn(slim, wide_ref[b])
            total = term if total is None else total + term
    if added:
        total = total + refs[-2][...].astype(F32)
    out_ref[...] = total.astype(out_ref.dtype)


def outer(which, wides, narrows, hidden_first, extra=None):
    per, capacity, hidden = wides[0].shape
    slim = pl.BlockSpec((per, capacity, HALF), lambda i, s: (0, 0, s[0]))
    if hidden_first:
        shape, out = (hidden, HALF), pl.BlockSpec((TILE, HALF), lambda i, s: (i, 0))
    else:
        shape, out = (HALF, hidden), pl.BlockSpec((HALF, TILE), lambda i, s: (0, i))
    specs = [pl.BlockSpec((per, capacity, TILE), lambda i, s: (0, 0, i))] * len(wides)
    specs += [slim] * len(narrows)
    operands = list(wides) + list(narrows)
    if extra is not None:
        specs.append(out)
        operands.append(extra)
    return pl.pallas_call(
        functools.partial(
            outer_kernel,
            chunks=len(wides),
            hidden_first=hidden_first,
            added=extra is not None,
        ),
        grid_spec=pltpu.PrefetchScalarGridSpec(
            num_scalar_prefetch=1, grid=(hidden // TILE,), in_specs=specs, out_specs=out
        ),
        out_shape=jax.ShapeDtypeStruct(shape, BF if extra is None else F32),
        name="outer_send" if extra is None else "outer_keep",
        cost_estimate=cost(),
    )(which, *operands)


def norm_back(grad, hat, scale, gain):
    inner = grad * gain
    return scale * (
        inner
        - jnp.mean(inner, axis=-1, keepdims=True)
        - hat * jnp.mean(inner * hat, axis=-1, keepdims=True)
    )


def add_sums(ref, grad, hat, first):
    sums = [jnp.sum(grad * hat, axis=0, keepdims=True), jnp.sum(grad, axis=0, keepdims=True)]

    @pl.when(first)
    def _():
        ref[...] = jnp.zeros_like(ref)

    ref[0:1, :] += sums[0]
    ref[1:2, :] += sums[1]


def attend_back_kernel(
    which_ref,
    x_ref,
    y_ref,
    near_ref,
    away_ref,
    rout_ref,
    cot_ref,
    vec_ref,
    out_w_ref,
    qkv_ref,
    lse_ref,
    w_ref,
    *refs,
):
    dy_ref, dyb_ref, dqkv_ref, part_ref, sums2_ref, sums1_ref, att_ref = refs[-7:]
    first = which_ref[0] == 0
    start = pl.program_id(0) == 0
    near = near_ref[0].astype(F32)
    away = away_ref[0].astype(F32)
    grad = rout_ref[0] + jnp.concatenate(
        [jnp.where(first, near, away), jnp.where(first, away, near)], axis=1
    )
    hat, scale = normed(y_ref[0])
    add_sums(sums2_ref, grad, hat, start)
    dy = cot_ref[0].astype(F32) + norm_back(grad, hat, scale, vec_ref[2:3, :])
    dy_ref[0] = dy
    dyb = dy.astype(BF)
    dyb_ref[0] = dyb
    att_ref[...] = dot_nn(dyb, out_w_ref[:, :HALF]).astype(BF)
    keys_in = lax.broadcasted_iota(jnp.int32, (ROWS, ROWS), 1) < SEQ
    for h in range(HALF // HEAD):
        at = h * HEAD
        q = qkv_ref[0, :, at : at + HEAD]
        k = qkv_ref[0, :, HALF + at : HALF + at + HEAD]
        v = qkv_ref[0, :, 2 * HALF + at : 2 * HALF + at + HEAD]
        do = att_ref[:, at : at + HEAD]
        s = jnp.where(keys_in, dot_nt(q, k) * SCALE, -1e30)
        weights = jnp.exp(s - lse_ref[0, :, h : h + 1])
        dv = dot_tn(weights.astype(BF), do)
        dp = dot_nt(do, v)
        ds = (weights * (dp - jnp.sum(weights * dp, axis=1, keepdims=True))).astype(BF)
        dqkv_ref[0, :, at : at + HEAD] = (dot_nn(ds, k) * SCALE).astype(BF)
        dqkv_ref[0, :, HALF + at : HALF + at + HEAD] = (dot_tn(ds, q) * SCALE).astype(BF)
        dqkv_ref[0, :, 2 * HALF + at : 2 * HALF + at + HEAD] = dv.astype(BF)
    part = dot_nt(dqkv_ref[0], w_ref[...])
    part_ref[0] = part.astype(BF)
    hat, _ = normed(x_ref[0].astype(F32))
    add_sums(sums1_ref, part, hat, start)


def attend_back(which, x, y, near, away, rout, cot, vectors, out_w, qkv, lse, weight, lo, hi, held):
    total = y.shape[0]
    return pl.pallas_call(
        attend_back_kernel,
        grid_spec=pltpu.PrefetchScalarGridSpec(
            num_scalar_prefetch=1,
            grid=(hi - lo,),
            in_specs=[
                image(D, lo),
                image(D, lo),
                image(HALF),
                image(HALF),
                image(D, lo),
                image(D, lo),
                whole(vectors.shape),
                whole(out_w.shape),
                image(3 * HALF, lo),
                image(LANES, lo),
                whole(weight.shape),
            ]
            + [ANY] * len(held),
            out_specs=[
                image(D, lo),
                image(D, lo),
                image(3 * HALF, lo),
                image(D),
                whole((8, D)),
                whole((8, D)),
            ],
            scratch_shapes=[pltpu.VMEM((ROWS, HALF), BF)],
        ),
        out_shape=[
            images(total, D, F32),
            images(total, D, BF),
            images(total, 3 * HALF, BF),
            images(hi - lo, D, BF),
            jax.ShapeDtypeStruct((8, D), F32),
            jax.ShapeDtypeStruct((8, D), F32),
        ],
        input_output_aliases={12 + n: n for n in range(len(held))},
        name="attend_back",
        cost_estimate=cost(),
    )(which, x, y, near, away, rout, cot, vectors, out_w, qkv, lse, weight, *held)


def token_kernel(x_ref, own_ref, got_ref, dy_ref, vec_ref, *refs):
    out_ref = refs[-1]
    grad = own_ref[0].astype(F32) + got_ref[0].astype(F32)
    hat, scale = normed(x_ref[0].astype(F32))
    out_ref[0] = dy_ref[0] + norm_back(grad, hat, scale, vec_ref[0:1, :])


def token_back(x, own, got, dy, vectors, lo, hi, held):
    total = x.shape[0]
    return pl.pallas_call(
        token_kernel,
        grid=(hi - lo,),
        in_specs=[image(D, lo), image(D), image(D), image(D, lo), whole(vectors.shape)]
        + [ANY] * len(held),
        out_specs=image(D, lo),
        out_shape=images(total, D, F32),
        input_output_aliases={5 + n: n for n in range(len(held))},
        name="token_back",
        cost_estimate=cost(),
    )(x, own, got, dy, vectors, *held)


def slot_table(routes, expert_count):
    total = routes.shape[0]
    sequence = jnp.transpose(routes).reshape(-1)
    onehot = (sequence[:, None] == jnp.arange(expert_count, dtype=jnp.int32)[None, :]).astype(
        jnp.int32
    )
    before = jnp.cumsum(onehot, axis=0) - onehot
    return jnp.sum(before * onehot, axis=1).reshape(2, total)


def images_of(value, fill=0):
    value = value.reshape(-1, SEQ, value.shape[-1])
    return jnp.pad(value, ((0, 0), (0, ROWS - SEQ), (0, 0)), constant_values=fill)


def on_device(
    tokens,
    cotangent,
    ln1_gain,
    ln1_bias,
    ln2_gain,
    ln2_bias,
    w_query,
    w_key,
    w_value,
    w_out,
    w_router,
    w_in,
    w_back,
    expert_ids,
):
    count = lax.axis_size("expert")
    chips = count // 2
    tok = tokens.shape[0]
    capacity = (10 * tok + 32 * count - 1) // (32 * count) * 8
    pictures = tok // SEQ
    rows_all = pictures * ROWS
    here = lax.axis_index("expert")
    here_dp = lax.axis_index("dp")
    here_t = lax.axis_index("tensor")
    which = here_t.astype(jnp.int32).reshape(1)
    same = here_t == here_dp

    order = Order()

    small = jnp.stack([ln1_gain, ln1_bias, ln2_gain, ln2_bias], axis=1)
    narrow = jnp.concatenate([small, w_router], axis=1)
    narrow = jnp.pad(narrow, ((0, 0), (0, LANES - narrow.shape[1])))
    first_pack = jnp.concatenate([w_query, w_key, w_value, narrow], axis=1).astype(BF)
    out_own = jnp.transpose(w_out).astype(BF)
    pair = cross(first_pack)
    out_both = jnp.concatenate([out_own, hop(follow(out_own, first_pack), "tensor", 1)], axis=1)

    slots = slot_table(follow(expert_ids, out_own), count)
    rows = images_of(jnp.transpose((jnp.transpose(expert_ids) ^ here) * capacity + slots), -1)
    rows_lane = jnp.transpose(rows.reshape(-1, 2))
    ids_pad = images_of(expert_ids, -1)
    x = images_of(follow(tokens, out_own))
    cot = images_of(follow(cotangent, out_own))
    cot_flat = cot.reshape(rows_all, D)
    cot_here = jnp.where(
        here_t == 0, cot_flat, jnp.concatenate([cot_flat[:, HALF:], cot_flat[:, :HALF]], axis=1)
    )
    in_own = follow(w_in, out_own)[0].astype(BF)
    back_own = follow(w_back, out_own)[0].astype(BF)

    pair, out_both = order.wait((pair, out_both))
    out_pair = cross(out_both)
    same_chips = jnp.stack(chip_copies(pair))
    same_chips, x, rows_lane, cot_here = order.wait((same_chips, x, rows_lane, cot_here))
    flipped = hop(same_chips, "expert", 1)
    out_pair = order.wait(out_pair)
    in_other = hop(order.after(in_own), "dp", 1)
    qkv_w, narrow_all = order.run(
        lambda *v: assemble(*v, (3 * HALF, LANES)), same_chips, flipped
    )
    vectors = jnp.pad(jnp.transpose(narrow_all[:, :4]).astype(F32), ((0, 4), (0, 0)))
    router_w = narrow_all[:, 4 : 4 + count]
    router_pad = jnp.pad(router_w, ((0, 0), (0, LANES - count)))
    out_same = jnp.stack(chip_copies(order.after(out_pair)))

    cut = (pictures + 1) // 2
    groups = [(0, cut), (cut, pictures)] if pictures > 1 else [(0, pictures)]
    held, o_parts, got_parts = [], [], []
    for n, (lo, hi) in enumerate(groups):
        *held, o_part = order.run(
            lambda x, v, w, *h: attend(x, v, w, lo, hi, h), x, vectors, qkv_w, *held
        )
        o_parts.append(o_part)
        got_parts.append(hop(o_part, "tensor", 1))
        if n == 0:
            out_same = order.wait(out_same)
            out_flip = hop(out_same, "expert", 1)
    a_rows, qkv, o_rows, lse = held
    (out_w,) = order.run(lambda *v: assemble(*v, (D,)), out_same, out_flip)
    rows_next = hop(order.after(rows_lane), "expert", 1)
    cot_next = hop(order.after(cot_here), "expert", 1)
    rows_next, cot_next = order.wait((rows_next, cot_next))
    in_other = order.wait(in_other)
    back_other = hop(order.after(back_own), "dp", 1)
    w1h, w1t = jnp.where(same, in_own, in_other), jnp.where(same, in_other, in_own)
    held, h_parts, h_next = [], [], []
    for n, (lo, hi) in enumerate(groups):
        *held, h_part = order.run(
            lambda x, o, g, v, w, r, i, *h: route(which, x, o, g, v, w, r, i, count, lo, hi, h),
            x, o_parts[n], got_parts[n], vectors, out_w, router_pad, ids_pad, *held,
        )
        h_parts.append(h_part.reshape(-1, D))
        h_next.append(hop(h_parts[-1], "expert", 1))
    y, probs, gates = held
    probs = probs.reshape(rows_all, LANES)[:, :count]
    gates_lane = jnp.transpose(gates.reshape(rows_all, LANES)[:, :2])
    gates_next = hop(gates_lane, "expert", 1)

    lanes_of = lambda value: [value[:, lo * ROWS : hi * ROWS] for lo, hi in groups]
    own = (lanes_of(rows_lane), h_parts)
    other = (lanes_of(rows_next), h_next)
    far = list(range(1, chips))
    outgoing = order.run(lambda *v: send_rows(*v, capacity, far, False), own, other)
    arrived = [None] + [hop(o, "expert", 2 * c) for o, c in zip(outgoing, far)]
    (arrived[0],) = order.run(lambda *v: send_rows(*v, capacity, [0], False), own, other)
    own = ([rows_lane], [cot_here], [gates_lane])
    other = ([rows_next], [cot_next], [gates_next])
    grad_outgoing = order.run(lambda *v: send_rows(*v, capacity, far, True), own, other)
    grad_arrived = [None] + [hop(o, "expert", 2 * c) for o, c in zip(grad_outgoing, far)]
    (grad_arrived[0],) = order.run(lambda *v: send_rows(*v, capacity, [0], True), own, other)
    w2h, w2t = jnp.where(same, back_own, back_other), jnp.where(same, back_other, back_own)

    hidden, slopes, grads, came_back, grad_home = [], [], [], [], []

    def return_rows(away, near, c):
        value = (near + hop(away, "tensor", 1).astype(F32)).astype(BF)
        return hop(value, "expert", 2 * c) if c else value

    for c in range(chips):
        g, s, zt, zh = order.run(expert_forward, arrived[c], w1h, w1t, w2h, w2t)
        hidden.append(g)
        slopes.append(s)
        came_back.append(return_rows(zt, zh, c))
    for c in range(chips):
        u, mt, mh = order.run(
            expert_backward, grad_arrived[c], slopes[c], w1h, w1t, w2h, w2t
        )
        grads.append(u)
        grad_home.append(return_rows(mt, mh, c))
    send_half = jnp.where(same, 1, 0).astype(jnp.int32).reshape(1)
    back_send = order.run(lambda h, g: outer(send_half, h, g, True), hidden, grad_arrived)
    back_got = hop(back_send, "dp", 1)
    in_send = order.run(lambda g, a: outer(send_half, g, a, False), grads, arrived)
    in_got = hop(follow(in_send, back_got), "dp", 1)

    def settle(parts):
        mine = jnp.stack([p[0] for p in parts])
        return mine, hop(jnp.stack([p[1] for p in parts]), "expert", 1)

    out_half, dgate = order.run(
        lambda *v: bring_home(which, *v), rows, y, cot, gates, *settle(came_back)
    )
    out_other = hop(out_half, "tensor", 1)
    dgate = jnp.transpose(dgate.reshape(rows_all, LANES)[:, :2])
    dgate = jnp.transpose(dgate + hop(dgate, "tensor", 1))
    ids_flat = ids_pad.reshape(rows_all, 2)
    lanes = jnp.arange(count, dtype=jnp.int32)[None, :]
    grad_probs = sum(
        jnp.where(ids_flat[:, c : c + 1] == lanes, dgate[:, c : c + 1], 0.0) for c in range(2)
    )
    grad_logits = probs * (grad_probs - jnp.sum(probs * grad_probs, axis=-1, keepdims=True))
    grad_rout = jnp.dot(grad_logits, jnp.transpose(router_w.astype(F32)), precision=HIGH)
    grad_rout = grad_rout.reshape(pictures, ROWS, D)

    back = settle(grad_home)
    near_parts = []
    for lo, hi in groups:
        near = order.run(lambda *v: sum_home(*v, lo, hi), rows, *back)
        near_parts.append((near, hop(near, "tensor", 1)))
    held, parts, sums, got = [], [], [], []
    for n, (lo, hi) in enumerate(groups):
        *held, part, sums2, sums1 = order.run(
            lambda *v: attend_back(which, *v[:11], lo, hi, v[11:]),
            x, y, *near_parts[n], grad_rout, cot, vectors, out_w, qkv, lse, qkv_w, *held,
        )
        parts.append(part)
        got.append(hop(part, "tensor", 1))
        sums.append(jnp.concatenate([sums1[:2], 0.5 * sums2[:2]], axis=0))
    dy, dyb, dqkv = held
    out_other = order.wait(out_other)

    flat = lambda value: value.reshape(rows_all, -1)
    grad_outw = dot_tn(flat(dyb), flat(o_rows))
    grad_wqkv = dot_tn(flat(a_rows), flat(dqkv))
    shards, leaving = scatter_sum(jnp.concatenate([grad_wqkv, grad_outw], axis=1), BF)
    grad_router = sum(
        jnp.dot(part, h.astype(F32), precision=HIGH)
        for part, h in zip(lanes_of(jnp.transpose(grad_logits)), h_parts)
    )
    grad_router = jnp.where(
        here_t == 0,
        grad_router,
        jnp.concatenate([grad_router[:, HALF:], grad_router[:, :HALF]], axis=1),
    )
    tiny = jnp.concatenate([0.5 * grad_router, sum(sums)], axis=0)
    tiny = tiny + hop(tiny, "tensor", 1)
    for offset in [1 << b for b in range(count.bit_length() - 1)]:
        tiny = tiny + hop(tiny, "expert", offset)
    tiny = tiny + hop(tiny, "dp", 1)
    tiny = tiny.reshape(tiny.shape[0], 2 * count, -1)
    tiny = lax.dynamic_index_in_dim(tiny, here_dp * count + here, 1, False)

    grad_tokens = []
    for n, (lo, hi) in enumerate(groups):
        if n == len(groups) - 1:
            leaving = order.wait(leaving)
            shards = shards + hop(leaving, "dp", 1).astype(F32)
        grad_tokens = [
            order.run(
                lambda *v: token_back(*v[:5], lo, hi, v[5:]),
                x, parts[n], got[n], dy, vectors, *grad_tokens,
            )
        ]
    grad_tokens = grad_tokens[0][:, :SEQ].reshape(tok, D)
    block_out = jnp.where(
        here_t == 0,
        jnp.concatenate([out_half, out_other], axis=2),
        jnp.concatenate([out_other, out_half], axis=2),
    )
    block_out = block_out[:, :SEQ].reshape(tok, D)

    keep_half = 1 - send_half
    grad_back = order.run(lambda h, g, b: outer(keep_half, h, g, True, b), hidden, grad_arrived, back_got)[None]
    grad_in = order.run(lambda g, a, b: outer(keep_half, g, a, False, b), grads, arrived, in_got)[None]
    return (
        block_out,
        grad_tokens,
        tiny[count],
        tiny[count + 1],
        tiny[count + 2],
        tiny[count + 3],
        shards[:, :HALF],
        shards[:, HALF : 2 * HALF],
        shards[:, 2 * HALF : 3 * HALF],
        jnp.transpose(shards[:, 3 * HALF :]),
        jnp.transpose(tiny[:count]),
        grad_in,
        grad_back,
    )


def solution(mesh):
    rows = ("dp", "expert")
    in_specs = (
        P(rows, None),
        P(rows, None),
        P(rows),
        P(rows),
        P(rows),
        P(rows),
        P(rows, "tensor"),
        P(rows, "tensor"),
        P(rows, "tensor"),
        P("tensor", rows),
        P(rows, None),
        P("expert", "dp", "tensor"),
        P("expert", "tensor", "dp"),
        P(rows, None),
    )
    out_specs = (
        P(rows, None),
        P(rows, None),
        P(rows),
        P(rows),
        P(rows),
        P(rows),
        P(rows, "tensor"),
        P(rows, "tensor"),
        P(rows, "tensor"),
        P("tensor", rows),
        P(rows, None),
        P("expert", "dp", "tensor"),
        P("expert", "tensor", "dp"),
    )
    return jax.shard_map(
        on_device, mesh=mesh, in_specs=in_specs, out_specs=out_specs, check_vma=False
    )
```

```python
import functools

import jax
import jax.numpy as jnp
from jax import lax
from jax.experimental import pallas as pl
from jax.experimental.pallas import tpu as pltpu
from jax.sharding import PartitionSpec as P

D = 768
HALF = 384
HEADS = 12
SEQ = 197
ROWS = 208
HEAD = D // HEADS
SCALE = HEAD ** (-0.5)
EPSILON = 1e-06
HIGH = lax.Precision.HIGHEST
BF = jnp.bfloat16
F32 = jnp.float32
LANES = 128
TILE = 512
CHUNKS = 4
TAIL_RATE = 0.305
TAIL = (
    0.12163973686996697,
    0.12246675128071258,
    0.10342128505066615,
    0.12102026121907625,
    -0.03797407148483761,
    0.1857138128109823,
    -0.15298645906475614,
    0.03669873020693663,
)
DENSITY = 0.3989422804014327


def hop(value, axis, offset):
    count = lax.axis_size(axis)
    return lax.ppermute(value, axis, [(i, i ^ offset) for i in range(count)])


class Order:
    def __init__(self):
        self.token = lax.create_token()

    def after(self, value):
        return lax.optimization_barrier((self.token, value))[1]

    def wait(self, value):
        self.token, value = lax.optimization_barrier((self.token, value))
        return value

    def run(self, function, *operands):
        return self.wait(function(*self.after(operands)))


def follow(value, first):
    token = lax.optimization_barrier((lax.create_token(), first))[0]
    return lax.optimization_barrier((token, value))[1]


def dot_nn(a, b):
    return lax.dot_general(a, b, (((1,), (0,)), ((), ())), preferred_element_type=F32)


def dot_nt(a, b):
    return lax.dot_general(a, b, (((1,), (1,)), ((), ())), preferred_element_type=F32)


def dot_tn(a, b):
    return lax.dot_general(a, b, (((0,), (0,)), ((), ())), preferred_element_type=F32)


def cost(flops=1000):
    return pl.CostEstimate(flops=flops, bytes_accessed=1000, transcendentals=0)


def image(width, lo=0):
    return pl.BlockSpec((1, ROWS, width), lambda i, *_: (i + lo, 0, 0))


def images(count, width, kind):
    return jax.ShapeDtypeStruct((count, ROWS, width), kind)


ANY = pl.BlockSpec(memory_space=pl.ANY)


def whole(shape):
    zeros = (0,) * len(shape)
    return pl.BlockSpec(shape, lambda *_: zeros)


def flag(value):
    return value.astype(jnp.int32).reshape(1)


def cross_kernel(here_ref, own_ref, across_ref, out_ref):
    first = here_ref[0] == 0
    out_ref[0] = jnp.where(first, own_ref[...], across_ref[...])
    out_ref[1] = jnp.where(first, across_ref[...], own_ref[...])


def cross(shard):
    across = hop(shard, "dp", 1)
    return pl.pallas_call(
        cross_kernel,
        grid_spec=pltpu.PrefetchScalarGridSpec(
            num_scalar_prefetch=1,
            grid=(1,),
            in_specs=[whole(shard.shape)] * 2,
            out_specs=whole((2,) + shard.shape),
        ),
        out_shape=jax.ShapeDtypeStruct((2,) + shard.shape, shard.dtype),
        name="cross",
        cost_estimate=cost(),
    )(flag(lax.axis_index("dp")), shard, across)


def stack_kernel(*refs):
    for n, ref in enumerate(refs[:-1]):
        refs[-1][n] = ref[...]


def stacked(parts):
    shape = (len(parts),) + parts[0].shape
    return pl.pallas_call(
        stack_kernel,
        grid=(1,),
        in_specs=[whole(p.shape) for p in parts],
        out_specs=whole(shape),
        out_shape=jax.ShapeDtypeStruct(shape, parts[0].dtype),
        name="stacked",
        cost_estimate=cost(),
    )(*parts)


def sort_kernel(*refs):
    parts, (mine_ref, away_ref) = refs[:-2], refs[-2:]
    for n, ref in enumerate(parts):
        mine_ref[n] = ref[0]
        away_ref[n] = ref[1]


def sort_groups(parts):
    shape = (len(parts),) + parts[0].shape[1:]
    return pl.pallas_call(
        sort_kernel,
        grid=(1,),
        in_specs=[whole(p.shape) for p in parts],
        out_specs=[whole(shape)] * 2,
        out_shape=[jax.ShapeDtypeStruct(shape, parts[0].dtype)] * 2,
        name="sort_groups",
        cost_estimate=cost(),
    )(*parts)


def add_kernel(near_ref, away_ref, out_ref):
    out_ref[...] = (near_ref[...] + away_ref[...].astype(F32)).astype(BF)


def add_halves(near, away):
    part = pl.BlockSpec((1,) + near.shape[1:], lambda i: (i, 0, 0))
    return pl.pallas_call(
        add_kernel,
        grid=(near.shape[0],),
        in_specs=[part, part],
        out_specs=part,
        out_shape=jax.ShapeDtypeStruct(near.shape, BF),
        name="add_halves",
        cost_estimate=cost(),
    )(near, away)


def vector_kernel(narrow_ref, out_ref, *, start):
    row = lax.broadcasted_iota(jnp.int32, (8, LANES), 0)
    lane = lax.broadcasted_iota(jnp.int32, (8, LANES), 1)
    wanted = jnp.where((lane == row + start) & (row < 4), 1.0, 0.0).astype(BF)
    out_ref[...] = dot_nt(wanted, narrow_ref[...])


def vectors_of(narrow, start):
    return pl.pallas_call(
        functools.partial(vector_kernel, start=start),
        grid=(1,),
        in_specs=[whole(narrow.shape)],
        out_specs=whole((8, D)),
        out_shape=jax.ShapeDtypeStruct((8, D), F32),
        name="vectors",
        cost_estimate=cost(),
    )(narrow)


def assemble_kernel(here_ref, same_ref, flip_ref, *out_refs):
    chips, _, rows, _ = same_ref.shape
    for chip in range(chips):
        for b, ref in enumerate((same_ref, flip_ref)):
            place = here_ref[0] ^ (2 * chip + b)
            for d in range(2):
                at = pl.ds(pl.multiple_of((d * 2 * chips + place) * rows, 16), rows)
                lo = 0
                for out_ref in out_refs:
                    out_ref[at, :] = ref[chip, d, :, lo : lo + out_ref.shape[1]]
                    lo += out_ref.shape[1]


def assemble(same, flipped, widths):
    chips, _, rows, columns = same.shape
    here = lax.axis_index("expert").astype(jnp.int32)
    if rows % 16 == 0:
        return pl.pallas_call(
            assemble_kernel,
            grid_spec=pltpu.PrefetchScalarGridSpec(
                num_scalar_prefetch=1,
                grid=(1,),
                in_specs=[whole(same.shape), whole(same.shape)],
                out_specs=[whole((4 * chips * rows, w)) for w in widths],
            ),
            out_shape=[jax.ShapeDtypeStruct((4 * chips * rows, w), same.dtype) for w in widths],
            name="assemble",
            cost_estimate=cost(),
        )(here.reshape(1), same, flipped)
    buffer = jnp.zeros((2, 2 * chips, rows, columns), same.dtype)
    for j in range(chips):
        for b, both in enumerate((same, flipped)):
            buffer = lax.dynamic_update_slice(buffer, both[j][:, None], (0, here ^ (2 * j + b), 0, 0))
    buffer = buffer.reshape(-1, columns)
    cuts = [sum(widths[:n]) for n in range(len(widths) + 1)]
    return [buffer[:, cuts[n] : cuts[n + 1]] for n in range(len(widths))]


def chip_copies(pair):
    count = lax.axis_size("expert")
    return [pair] + [hop(pair, "expert", k) for k in range(2, count, 2)]


def pick(array, index, axis):
    return lax.dynamic_index_in_dim(array, index, axis, False)


def core_sum(grad, wide):
    count = lax.axis_size("expert")
    core = lax.axis_index("expert") & 1
    blocks = grad.reshape((2, count // 2, 2, -1) + grad.shape[1:])
    return pick(blocks, core, 2) + hop(
        pick(blocks, 1 - core, 2).astype(wide), "expert", 1
    ).astype(F32)


def chip_sum(total, wide):
    here_dp = lax.axis_index("dp")
    chip = lax.axis_index("expert") >> 1
    summed = pick(total, chip, 1)
    for k in range(1, total.shape[1]):
        summed = summed + hop(pick(total, chip ^ k, 1).astype(wide), "expert", 2 * k).astype(F32)
    return pick(summed, here_dp, 0), pick(summed, 1 - here_dp, 0).astype(wide)


def normed(values):
    average = jnp.mean(values, axis=-1, keepdims=True)
    centred = values - average
    variance = jnp.mean(centred * centred, axis=-1, keepdims=True)
    scale = lax.rsqrt(variance + EPSILON)
    return centred * scale, scale


def attend_kernel(x_ref, vec_ref, w_ref, *refs):
    a_ref, qkv_ref, o_ref, lse_ref, part_ref = refs[-5:]
    hat, _ = normed(x_ref[0].astype(F32))
    a = (hat * vec_ref[0:1, :] + vec_ref[1:2, :]).astype(BF)
    a_ref[0] = a
    qkv_ref[0] = dot_nn(a, w_ref[...]).astype(BF)
    keys_in = lax.broadcasted_iota(jnp.int32, (ROWS, ROWS), 1) < SEQ
    lane = lax.broadcasted_iota(jnp.int32, (ROWS, LANES), 1)
    lse = jnp.zeros((ROWS, LANES), F32)
    for h in range(HALF // HEAD):
        at = h * HEAD
        q = qkv_ref[0, :, at : at + HEAD]
        k = qkv_ref[0, :, HALF + at : HALF + at + HEAD]
        v = qkv_ref[0, :, 2 * HALF + at : 2 * HALF + at + HEAD]
        s = jnp.where(keys_in, dot_nt(q, k) * SCALE, -1e30)
        top = jnp.max(s, axis=1, keepdims=True)
        total = top + jnp.log(jnp.sum(jnp.exp(s - top), axis=1, keepdims=True))
        weights = jnp.exp(s - total).astype(BF)
        part_ref[0, :, at : at + HEAD] = dot_nn(weights, v).astype(BF)
        lse = jnp.where(lane == h, total, lse)
    lse_ref[0] = lse
    o_ref[0] = part_ref[0]


def attend(x, vectors, weight, lo, hi, held):
    total = x.shape[0]
    return pl.pallas_call(
        attend_kernel,
        grid=(hi - lo,),
        in_specs=[image(D, lo), whole(vectors.shape), whole(weight.shape)] + [ANY] * len(held),
        out_specs=[image(D, lo), image(3 * HALF, lo), image(HALF, lo), image(LANES, lo), image(HALF)],
        out_shape=[
            images(total, D, BF),
            images(total, 3 * HALF, BF),
            images(total, HALF, BF),
            images(total, LANES, F32),
            images(hi - lo, HALF, BF),
        ],
        input_output_aliases={3 + n: n for n in range(len(held))},
        name="attend",
        cost_estimate=cost(),
    )(x, vectors, weight, *held)


def route_kernel(
    which_ref, x_ref, own_ref, got_ref, vec_ref, here_ref, there_ref, router_ref, ids_ref, *refs, count
):
    y_ref, r_ref, g_ref, h_ref = refs[-4:]
    y = x_ref[0].astype(F32) + (
        dot_nt(own_ref[0], here_ref[...]) + dot_nt(got_ref[0], there_ref[...])
    )
    y_ref[0] = y
    hat, _ = normed(y)
    h = (hat * vec_ref[2:3, :] + vec_ref[3:4, :]).astype(BF)
    first = which_ref[0] == 0
    h_ref[0, :, :HALF] = jnp.where(first, h[:, :HALF], h[:, HALF:])
    h_ref[0, :, HALF:] = jnp.where(first, h[:, HALF:], h[:, :HALF])
    lane = lax.broadcasted_iota(jnp.int32, (ROWS, LANES), 1)
    logits = jnp.where(lane < count, dot_nn(h, router_ref[...]), -1e30)
    logits = jnp.exp(logits - jnp.max(logits, axis=1, keepdims=True))
    probs = logits / jnp.sum(logits, axis=1, keepdims=True)
    r_ref[0] = probs
    gates = jnp.zeros((ROWS, LANES), F32)
    for c in range(2):
        gate = jnp.sum(jnp.where(lane == ids_ref[0, :, c : c + 1], probs, 0.0), axis=1, keepdims=True)
        gates = jnp.where(lane == c, gate, gates)
    g_ref[0] = gates


def route(which, x, own, got, vectors, out_here, out_there, router, ids, count, lo, hi, held):
    total = x.shape[0]
    return pl.pallas_call(
        functools.partial(route_kernel, count=count),
        grid_spec=pltpu.PrefetchScalarGridSpec(
            num_scalar_prefetch=1,
            grid=(hi - lo,),
            in_specs=[
                image(D, lo),
                image(HALF),
                image(HALF),
                whole(vectors.shape),
                whole(out_here.shape),
                whole(out_there.shape),
                whole(router.shape),
                image(2, lo),
            ]
            + [ANY] * len(held),
            out_specs=[image(D, lo), image(LANES, lo), image(LANES, lo), image(D)],
        ),
        out_shape=[
            images(total, D, F32),
            images(total, LANES, F32),
            images(total, LANES, F32),
            images(hi - lo, D, BF),
        ],
        input_output_aliases={9 + n: n for n in range(len(held))},
        name="route",
        cost_estimate=cost(),
    )(which, x, own, got, vectors, out_here, out_there, router, ids, *held)


def send_kernel(*refs, parts, chips, gated):
    per = 3 if gated else 2
    groups = [refs[n * per * parts : (n + 1) * per * parts] for n in range(2)]
    out_refs = refs[2 * per * parts :]
    capacity = out_refs[0].shape[1]
    for out_ref, chip in zip(out_refs, chips):
        for r in range(2):
            rows, values, gates = (groups[r][n * parts : (n + 1) * parts] for n in range(3))
            places = lax.broadcasted_iota(jnp.int32, (capacity, 1), 0) + (2 * chip + r) * capacity
            picked = jnp.zeros((capacity, D), F32)
            weight = jnp.zeros((capacity, 1), F32)
            for n in range(parts):
                first = places == rows[n][0:1, :]
                second = places == rows[n][1:2, :]
                chosen = jnp.where(first | second, 1.0, 0.0).astype(BF)
                picked = picked + dot_nn(chosen, values[n][...])
                if gated:
                    each = jnp.where(
                        first, gates[n][0:1, :], jnp.where(second, gates[n][1:2, :], 0.0)
                    )
                    weight = weight + jnp.sum(each, axis=1, keepdims=True)
            if gated:
                picked = picked * weight
            out_ref[r] = picked.astype(BF)


def send_rows(own, other, capacity, chips, gated):
    operands = [part for group in (own, other) for kind in group for part in kind]
    return pl.pallas_call(
        functools.partial(send_kernel, parts=len(own[0]), chips=chips, gated=gated),
        grid=(1,),
        in_specs=[whole(o.shape) for o in operands],
        out_specs=[whole((2, capacity, D))] * len(chips),
        out_shape=[jax.ShapeDtypeStruct((2, capacity, D), BF)] * len(chips),
        name="send_gated" if gated else "send_rows",
        cost_estimate=cost(),
    )(*operands)


def first_lanes():
    row = lax.broadcasted_iota(jnp.int32, (8, LANES), 0)
    return jnp.where(row == lax.broadcasted_iota(jnp.int32, (8, LANES), 1), 1.0, 0.0)


def turn(columns):
    return lax.dot_general(
        first_lanes(), columns, (((1,), (1,)), ((), ())), precision=HIGH, preferred_element_type=F32
    )


def turn_back(rows):
    return lax.dot_general(
        rows, first_lanes(), (((0,), (0,)), ((), ())), precision=HIGH, preferred_element_type=F32
    )


def home_kernel(which_ref, rows_ref, middle_ref, grad_ref, gates_ref, own_ref, other_ref, out_ref, dgate_ref):
    value = middle_ref[0]
    grad = grad_ref[0].astype(F32)
    lane = lax.broadcasted_iota(jnp.int32, (ROWS, LANES), 1)
    found = jnp.zeros((ROWS, LANES), F32)
    chips, capacity = own_ref.shape[:2]
    places = lax.broadcasted_iota(jnp.int32, (1, capacity), 1)
    for c in range(2):
        picked = jnp.zeros((ROWS, HALF), F32)
        for chip in range(chips):
            for r, back_ref in enumerate((own_ref, other_ref)):
                at = rows_ref[0, :, c : c + 1] - (2 * chip + r) * capacity
                chosen = jnp.where(at == places, 1.0, 0.0)
                picked = picked + dot_nn(chosen.astype(BF), back_ref[chip])
        value = value + gates_ref[0, :, c : c + 1] * picked
        dgate = jnp.sum(picked * grad, axis=1, keepdims=True)
        found = jnp.where(lane == c, dgate, found)
    out_ref[0] = value.astype(BF)
    dgate_ref[0] = turn(found)


def bring_home(which, rows, middle, grad, gates, own, other):
    total = middle.shape[0]
    part = pl.BlockSpec((1, ROWS, HALF), lambda i, s: (i, 0, s[0]))
    return pl.pallas_call(
        home_kernel,
        grid_spec=pltpu.PrefetchScalarGridSpec(
            num_scalar_prefetch=1,
            grid=(total,),
            in_specs=[image(2), part, part, image(LANES), whole(own.shape), whole(other.shape)],
            out_specs=[image(HALF), pl.BlockSpec((1, 8, ROWS), lambda i, s: (i, 0, 0))],
        ),
        out_shape=[images(total, HALF, BF), jax.ShapeDtypeStruct((total, 8, ROWS), F32)],
        name="bring_home",
        cost_estimate=cost(),
    )(which, rows, middle, grad, gates, own, other)


def sum_kernel(rows_ref, own_ref, other_ref, out_ref):
    chips, capacity = own_ref.shape[:2]
    places = lax.broadcasted_iota(jnp.int32, (1, capacity), 1)
    total = jnp.zeros((ROWS, HALF), F32)
    for chip in range(chips):
        for r, back_ref in enumerate((own_ref, other_ref)):
            base = (2 * chip + r) * capacity
            chosen = (rows_ref[0, :, 0:1] - base == places) | (rows_ref[0, :, 1:2] - base == places)
            total = total + dot_nn(jnp.where(chosen, 1.0, 0.0).astype(BF), back_ref[chip])
    out_ref[0] = total.astype(BF)


def sum_home(rows, own, other, lo, hi):
    return pl.pallas_call(
        sum_kernel,
        grid=(hi - lo,),
        in_specs=[image(2, lo), whole(own.shape), whole(other.shape)],
        out_specs=image(HALF),
        out_shape=images(hi - lo, HALF, BF),
        name="sum_home",
        cost_estimate=cost(),
    )(rows, own, other)


def gelu_parts(u):
    size = jnp.abs(u)
    t = 1.0 / (1.0 + TAIL_RATE * size)
    poly = jnp.full_like(t, TAIL[-1])
    for c in TAIL[-2::-1]:
        poly = poly * t + c
    bell = jnp.exp(-0.5 * (u * u))
    tail = bell * (t * poly)
    normal = jnp.where(u >= 0.0, 1.0 - tail, tail)
    return u * normal, normal + u * (DENSITY * bell)


def in_order(same_ref, in_own, in_other, back_own, back_other):
    same = same_ref[0] == 1
    choose = lambda a, b: (jnp.where(same, a[...], b[...]), jnp.where(same, b[...], a[...]))
    return choose(in_own, in_other) + choose(back_own, back_other)


def forward_kernel(same_ref, m_ref, in_own, in_other, back_own, back_other, g_ref, s_ref, zt_ref, zh_ref, acc):
    w1h, w1t, w2h, w2t = in_order(same_ref, in_own, in_other, back_own, back_other)
    step = pl.program_id(0)
    last = pl.num_programs(0) - 1
    for b in range(m_ref.shape[0]):
        u = dot_nn(m_ref[b, :, :HALF], w1h) + dot_nn(m_ref[b, :, HALF:], w1t)
        g, slope = gelu_parts(u)
        g = g.astype(BF)
        g_ref[b] = g
        s_ref[b] = slope.astype(BF)
        away = dot_nn(g, w2t)
        near = dot_nn(g, w2h)

        @pl.when(step == 0)
        def _():
            acc[b] = away
            zh_ref[b] = near

        @pl.when(step > 0)
        def _():
            acc[b] += away
            zh_ref[b] += near

        @pl.when(step == last)
        def _():
            zt_ref[b] = acc[b].astype(BF)


def expert_forward(same, rows, *weights):
    blocks, capacity, _ = rows.shape
    hidden = weights[0].shape[1]
    across = pl.BlockSpec((HALF, TILE), lambda i, s: (0, i))
    down = pl.BlockSpec((TILE, HALF), lambda i, s: (i, 0))
    wide = pl.BlockSpec((blocks, capacity, TILE), lambda i, s: (0, 0, i))
    make = lambda w, t: jax.ShapeDtypeStruct((blocks, capacity, w), t)
    return pl.pallas_call(
        forward_kernel,
        grid_spec=pltpu.PrefetchScalarGridSpec(
            num_scalar_prefetch=1,
            grid=(hidden // TILE,),
            in_specs=[whole(rows.shape), across, across, down, down],
            out_specs=[wide, wide] + [whole((blocks, capacity, HALF))] * 2,
            scratch_shapes=[pltpu.VMEM((blocks, capacity, HALF), F32)],
        ),
        out_shape=[make(hidden, BF), make(hidden, BF), make(HALF, BF), make(HALF, F32)],
        name="expert_forward",
        cost_estimate=cost(),
    )(same, rows, *weights)


def backward_kernel(same_ref, z_ref, s_ref, in_own, in_other, back_own, back_other, u_ref, mt_ref, mh_ref, acc):
    w1h, w1t, w2h, w2t = in_order(same_ref, in_own, in_other, back_own, back_other)
    step = pl.program_id(0)
    last = pl.num_programs(0) - 1
    for b in range(z_ref.shape[0]):
        grad = dot_nt(z_ref[b, :, :HALF], w2h) + dot_nt(z_ref[b, :, HALF:], w2t)
        grad = (grad * s_ref[b].astype(F32)).astype(BF)
        u_ref[b] = grad
        away = dot_nt(grad, w1t)
        near = dot_nt(grad, w1h)

        @pl.when(step == 0)
        def _():
            acc[b] = away
            mh_ref[b] = near

        @pl.when(step > 0)
        def _():
            acc[b] += away
            mh_ref[b] += near

        @pl.when(step == last)
        def _():
            mt_ref[b] = acc[b].astype(BF)


def expert_backward(same, rows, slope, *weights):
    blocks, capacity, _ = rows.shape
    hidden = weights[0].shape[1]
    across = pl.BlockSpec((HALF, TILE), lambda i, s: (0, i))
    down = pl.BlockSpec((TILE, HALF), lambda i, s: (i, 0))
    wide = pl.BlockSpec((blocks, capacity, TILE), lambda i, s: (0, 0, i))
    make = lambda w, t: jax.ShapeDtypeStruct((blocks, capacity, w), t)
    return pl.pallas_call(
        backward_kernel,
        grid_spec=pltpu.PrefetchScalarGridSpec(
            num_scalar_prefetch=1,
            grid=(hidden // TILE,),
            in_specs=[whole(rows.shape), wide, across, across, down, down],
            out_specs=[wide] + [whole((blocks, capacity, HALF))] * 2,
            scratch_shapes=[pltpu.VMEM((blocks, capacity, HALF), F32)],
        ),
        out_shape=[make(hidden, BF), make(HALF, BF), make(HALF, F32)],
        name="expert_backward",
        cost_estimate=cost(),
    )(same, rows, slope, *weights)


def outer_kernel(which_ref, *refs, chunks, hidden_first, added):
    wides = refs[:chunks]
    narrows = refs[chunks : 2 * chunks]
    out_ref = refs[-1]
    total = None
    for wide_ref, slim_ref in zip(wides, narrows):
        for b in range(wide_ref.shape[0]):
            slim = slim_ref[b]
            term = dot_tn(wide_ref[b], slim) if hidden_first else dot_tn(slim, wide_ref[b])
            total = term if total is None else total + term
    if added:
        total = total + refs[-2][...].astype(F32)
    out_ref[...] = total.astype(out_ref.dtype)


def outer(which, wides, narrows, hidden_first, extra=None):
    per, capacity, hidden = wides[0].shape
    slim = pl.BlockSpec((per, capacity, HALF), lambda i, s: (0, 0, s[0]))
    if hidden_first:
        shape, out = (hidden, HALF), pl.BlockSpec((TILE, HALF), lambda i, s: (i, 0))
    else:
        shape, out = (HALF, hidden), pl.BlockSpec((HALF, TILE), lambda i, s: (0, i))
    specs = [pl.BlockSpec((per, capacity, TILE), lambda i, s: (0, 0, i))] * len(wides)
    specs += [slim] * len(narrows)
    operands = list(wides) + list(narrows)
    if extra is not None:
        specs.append(out)
        operands.append(extra)
    return pl.pallas_call(
        functools.partial(
            outer_kernel,
            chunks=len(wides),
            hidden_first=hidden_first,
            added=extra is not None,
        ),
        grid_spec=pltpu.PrefetchScalarGridSpec(
            num_scalar_prefetch=1, grid=(hidden // TILE,), in_specs=specs, out_specs=out
        ),
        out_shape=jax.ShapeDtypeStruct(shape, BF if extra is None else F32),
        name="outer_send" if extra is None else "outer_keep",
        cost_estimate=cost(),
    )(which, *operands)


def norm_back(grad, hat, scale, gain):
    inner = grad * gain
    return scale * (
        inner
        - jnp.mean(inner, axis=-1, keepdims=True)
        - hat * jnp.mean(inner * hat, axis=-1, keepdims=True)
    )


def add_sums(ref, grad, hat, first):
    sums = [jnp.sum(grad * hat, axis=0, keepdims=True), jnp.sum(grad, axis=0, keepdims=True)]

    @pl.when(first)
    def _():
        ref[...] = jnp.zeros_like(ref)

    ref[0:1, :] += sums[0]
    ref[1:2, :] += sums[1]


def attend_back_kernel(
    which_ref,
    x_ref,
    y_ref,
    near_ref,
    away_ref,
    dgate_ref,
    dgate2_ref,
    probs_ref,
    ids_ref,
    narrow_ref,
    cot_ref,
    vec_ref,
    out_w_ref,
    qkv_ref,
    lse_ref,
    w_ref,
    *refs,
):
    dy_ref, dyb_ref, dqkv_ref, part_ref, sums2_ref, sums1_ref, router_ref, att_ref = refs[-8:]
    first = which_ref[0] == 0
    start = pl.program_id(0) == 0
    near = near_ref[0].astype(F32)
    away = away_ref[0].astype(F32)
    dgate = turn_back(dgate_ref[0] + dgate2_ref[0])
    lane = lax.broadcasted_iota(jnp.int32, (ROWS, LANES), 1)
    probs = probs_ref[0]
    grad_probs = sum(
        jnp.where(lane == ids_ref[0, :, c : c + 1], dgate[:, c : c + 1], 0.0) for c in range(2)
    )
    grad_logits = probs * (grad_probs - jnp.sum(probs * grad_probs, axis=1, keepdims=True))
    grad = lax.dot_general(
        grad_logits, narrow_ref[...].astype(F32), (((1,), (1,)), ((), ())),
        precision=HIGH, preferred_element_type=F32,
    ) + jnp.concatenate(
        [jnp.where(first, near, away), jnp.where(first, away, near)], axis=1
    )
    hat, scale = normed(y_ref[0])
    h = (hat * vec_ref[2:3, :] + vec_ref[3:4, :]).astype(BF)
    grad_router = lax.dot_general(
        grad_logits, h.astype(F32), (((0,), (0,)), ((), ())),
        precision=HIGH, preferred_element_type=F32,
    )

    @pl.when(start)
    def _():
        router_ref[...] = grad_router

    @pl.when(jnp.logical_not(start))
    def _():
        router_ref[...] += grad_router

    add_sums(sums2_ref, grad, hat, start)
    dy = cot_ref[0].astype(F32) + norm_back(grad, hat, scale, vec_ref[2:3, :])
    dy_ref[0] = dy
    dyb = dy.astype(BF)
    dyb_ref[0] = dyb
    att_ref[...] = dot_nn(dyb, out_w_ref[...]).astype(BF)
    keys_in = lax.broadcasted_iota(jnp.int32, (ROWS, ROWS), 1) < SEQ
    for h in range(HALF // HEAD):
        at = h * HEAD
        q = qkv_ref[0, :, at : at + HEAD]
        k = qkv_ref[0, :, HALF + at : HALF + at + HEAD]
        v = qkv_ref[0, :, 2 * HALF + at : 2 * HALF + at + HEAD]
        do = att_ref[:, at : at + HEAD]
        s = jnp.where(keys_in, dot_nt(q, k) * SCALE, -1e30)
        weights = jnp.exp(s - lse_ref[0, :, h : h + 1])
        dv = dot_tn(weights.astype(BF), do)
        dp = dot_nt(do, v)
        ds = (weights * (dp - jnp.sum(weights * dp, axis=1, keepdims=True))).astype(BF)
        dqkv_ref[0, :, at : at + HEAD] = (dot_nn(ds, k) * SCALE).astype(BF)
        dqkv_ref[0, :, HALF + at : HALF + at + HEAD] = (dot_tn(ds, q) * SCALE).astype(BF)
        dqkv_ref[0, :, 2 * HALF + at : 2 * HALF + at + HEAD] = dv.astype(BF)
    part = dot_nt(dqkv_ref[0], w_ref[...])
    part_ref[0] = part.astype(BF)
    hat, _ = normed(x_ref[0].astype(F32))
    add_sums(sums1_ref, part, hat, start)


def attend_back(which, x, y, near, away, dgate, dgate2, probs, ids, narrow, cot, vectors, out_w, qkv, lse, weight, lo, hi, held):
    total = y.shape[0]
    turned = pl.BlockSpec((1, 8, ROWS), lambda i, s: (i + lo, 0, 0))
    return pl.pallas_call(
        attend_back_kernel,
        grid_spec=pltpu.PrefetchScalarGridSpec(
            num_scalar_prefetch=1,
            grid=(hi - lo,),
            in_specs=[
                image(D, lo),
                image(D, lo),
                image(HALF),
                image(HALF),
                turned,
                turned,
                image(LANES, lo),
                image(2, lo),
                whole(narrow.shape),
                image(D, lo),
                whole(vectors.shape),
                whole(out_w.shape),
                image(3 * HALF, lo),
                image(LANES, lo),
                whole(weight.shape),
            ]
            + [ANY] * len(held),
            out_specs=[
                image(D, lo),
                image(D, lo),
                image(3 * HALF, lo),
                image(D),
                whole((8, D)),
                whole((8, D)),
                whole((LANES, D)),
            ],
            scratch_shapes=[pltpu.VMEM((ROWS, HALF), BF)],
        ),
        out_shape=[
            images(total, D, F32),
            images(total, D, BF),
            images(total, 3 * HALF, BF),
            images(hi - lo, D, BF),
            jax.ShapeDtypeStruct((8, D), F32),
            jax.ShapeDtypeStruct((8, D), F32),
            jax.ShapeDtypeStruct((LANES, D), F32),
        ],
        input_output_aliases={16 + n: n for n in range(len(held))},
        name="attend_back",
        cost_estimate=cost(),
    )(which, x, y, near, away, dgate, dgate2, probs, ids, narrow, cot, vectors, out_w, qkv, lse, weight, *held)


def token_kernel(x_ref, own_ref, got_ref, dy_ref, vec_ref, *refs):
    out_ref = refs[-1]
    grad = own_ref[0].astype(F32) + got_ref[0].astype(F32)
    hat, scale = normed(x_ref[0].astype(F32))
    out_ref[0] = dy_ref[0] + norm_back(grad, hat, scale, vec_ref[0:1, :])


def token_back(x, own, got, dy, vectors, lo, hi, held):
    total = x.shape[0]
    return pl.pallas_call(
        token_kernel,
        grid=(hi - lo,),
        in_specs=[image(D, lo), image(D), image(D), image(D, lo), whole(vectors.shape)]
        + [ANY] * len(held),
        out_specs=image(D, lo),
        out_shape=images(total, D, F32),
        input_output_aliases={5 + n: n for n in range(len(held))},
        name="token_back",
        cost_estimate=cost(),
    )(x, own, got, dy, vectors, *held)


def slot_table(routes, expert_count):
    total = routes.shape[0]
    sequence = jnp.transpose(routes).reshape(-1)
    onehot = (sequence[:, None] == jnp.arange(expert_count, dtype=jnp.int32)[None, :]).astype(
        jnp.int32
    )
    before = jnp.cumsum(onehot, axis=0) - onehot
    return jnp.sum(before * onehot, axis=1).reshape(2, total)


def images_of(value, fill=0):
    value = value.reshape(-1, SEQ, value.shape[-1])
    return jnp.pad(value, ((0, 0), (0, ROWS - SEQ), (0, 0)), constant_values=fill)


def on_device(
    tokens,
    cotangent,
    ln1_gain,
    ln1_bias,
    ln2_gain,
    ln2_bias,
    w_query,
    w_key,
    w_value,
    w_out,
    w_router,
    w_in,
    w_back,
    expert_ids,
):
    count = lax.axis_size("expert")
    chips = count // 2
    tok = tokens.shape[0]
    capacity = (10 * tok + 32 * count - 1) // (32 * count) * 8
    pictures = tok // SEQ
    rows_all = pictures * ROWS
    here = lax.axis_index("expert")
    here_dp = lax.axis_index("dp")
    here_t = lax.axis_index("tensor")
    which = here_t.astype(jnp.int32).reshape(1)
    same = here_t == here_dp

    order = Order()

    small = jnp.stack([ln1_gain, ln1_bias, ln2_gain, ln2_bias], axis=1)
    narrow = jnp.concatenate([w_router, small], axis=1)
    narrow = jnp.pad(narrow, ((0, 0), (0, LANES - narrow.shape[1])))
    first_pack = jnp.concatenate(
        [w_query, w_key, w_value, narrow, jnp.transpose(w_out)], axis=1
    ).astype(BF)
    pair = cross(first_pack)
    in_own = follow(w_in, first_pack)[0].astype(BF)
    back_own = follow(w_back, first_pack)[0].astype(BF)
    ids_pad = images_of(follow(expert_ids, first_pack), -1)
    pair, in_own, back_own, ids_pad = order.wait((pair, in_own, back_own, ids_pad))

    same_chips = stacked(chip_copies(order.after(pair)))
    in_other = hop(order.after(in_own), "dp", 1)

    routes = order.after(expert_ids)
    slots = slot_table(routes, count)
    rows = images_of(jnp.transpose((jnp.transpose(routes) ^ here) * capacity + slots), -1)
    rows_lane = jnp.transpose(rows.reshape(-1, 2))
    x = images_of(order.after(tokens))
    cot = images_of(order.after(cotangent))
    cot_flat = cot.reshape(rows_all, D)
    cot_here = jnp.where(
        here_t == 0, cot_flat, jnp.concatenate([cot_flat[:, HALF:], cot_flat[:, :HALF]], axis=1)
    )
    cut = (pictures + 1) // 2
    groups = [(0, cut), (cut, pictures)] if pictures > 1 else [(0, pictures)]
    lanes_of = lambda value: [value[:, lo * ROWS : hi * ROWS] for lo, hi in groups]
    same_chips, x, rows, rows_lane, cot, cot_here, own_lanes = order.wait(
        (same_chips, x, rows, rows_lane, cot, cot_here, lanes_of(rows_lane))
    )
    flipped = order.wait(hop(order.after(same_chips), "expert", 1))
    qkv_w, narrow_all, out_here = order.run(
        lambda *v: assemble(*v, (3 * HALF, LANES, HALF)), same_chips, flipped
    )
    out_there = hop(order.after(out_here), "tensor", 1)
    vectors = order.run(lambda v: vectors_of(v, count), narrow_all)
    rows_next = hop(order.after(rows_lane), "expert", 1)
    cot_next = hop(order.after(cot_here), "expert", 1)

    held, o_parts, got_parts = [], [], []
    for n, (lo, hi) in enumerate(groups):
        *held, o_part = order.run(
            lambda x, v, w, *h: attend(x, v, w, lo, hi, h), x, vectors, qkv_w, *held
        )
        o_parts.append(o_part)
        got_parts.append(hop(o_part, "tensor", 1))
        if n == 0:
            rows_next, cot_next = order.wait((rows_next, cot_next))
    a_rows, qkv, o_rows, lse = held
    out_there = order.wait(out_there)
    got_parts = list(order.wait(tuple(got_parts)))
    next_lanes = order.wait(lanes_of(rows_next))
    held, h_parts, h_next = [], [], []
    for n, (lo, hi) in enumerate(groups):
        *held, h_part = order.run(
            lambda x, o, g, v, w, t, r, i, *h: route(which, x, o, g, v, w, t, r, i, count, lo, hi, h),
            x, o_parts[n], got_parts[n], vectors, out_here, out_there, narrow_all, ids_pad, *held,
        )
        h_parts.append(h_part.reshape(-1, D))
        h_next.append(hop(h_parts[-1], "expert", 1))
        if n == 0:
            in_other = order.wait(in_other)
            back_other = hop(order.after(back_own), "dp", 1)
    y, probs, gates = held
    gates_lane = jnp.transpose(gates.reshape(rows_all, LANES)[:, :2])
    gates_next = hop(gates_lane, "expert", 1)

    gates_next = order.wait(gates_next)
    own = (own_lanes, h_parts)
    other = (next_lanes, h_next)
    far = list(range(1, chips))
    outgoing = order.run(lambda *v: send_rows(*v, capacity, far, False), own, other)
    arrived = [None] + [hop(o, "expert", 2 * c) for o, c in zip(outgoing, far)]
    (arrived[0],) = order.run(lambda *v: send_rows(*v, capacity, [0], False), own, other)
    own = ([rows_lane], [cot_here], [gates_lane])
    other = ([rows_next], [cot_next], [gates_next])
    grad_outgoing = order.run(lambda *v: send_rows(*v, capacity, far, True), own, other)
    grad_arrived = [None] * chips
    (grad_arrived[0],) = order.run(lambda *v: send_rows(*v, capacity, [0], True), own, other)
    back_other = order.wait(back_other)
    weights = (in_own, in_other, back_own, back_other)
    same = flag(same)

    hidden, slopes, grads = [], [], []
    came_back, grad_home = [None] * chips, [None] * chips

    def back_to(chip, waiting):
        value = order.run(add_halves, *waiting)
        return hop(value, "expert", 2 * chip) if chip else value

    pending = None
    for c in range(chips):
        if c == 1:
            arrived[1:] = order.wait(arrived[1:])
            if chips <= 4:
                grad_arrived[1:] = [
                    hop(order.after(o), "expert", 2 * k) for o, k in zip(grad_outgoing, far)
                ]
        if c and chips > 4:
            grad_arrived[c] = hop(order.after(grad_outgoing[c - 1]), "expert", 2 * c)
        if c == chips - 1 and chips <= 4:
            grad_arrived[1:] = order.wait(grad_arrived[1:])
        g, s, zt, zh = order.run(lambda *v: expert_forward(same, *v), arrived[c], *weights)
        hidden.append(g)
        slopes.append(s)
        if pending is not None:
            came_back[c - 1] = back_to(c - 1, pending)
        pending = (zh, hop(order.after(zt), "tensor", 1))
    for c in range(chips):
        if c and chips > 4:
            grad_arrived[c] = order.wait(grad_arrived[c])
        u, mt, mh = order.run(
            lambda *v: expert_backward(same, *v), grad_arrived[c], slopes[c], *weights
        )
        grads.append(u)
        if c:
            grad_home[c - 1] = back_to(c - 1, pending)
        else:
            came_back[1] = order.wait(came_back[1])
            came_back[chips - 1] = back_to(chips - 1, pending)
        if c >= chips // 2:
            step = (chips - 2) * 2 // chips
            for k in range(2 + (c - chips // 2) * step, 2 + (c - chips // 2 + 1) * step):
                came_back[k] = order.wait(came_back[k])
        pending = (mh, hop(order.after(mt), "tensor", 1))
    z_here, z_there = order.run(lambda *v: sort_groups(v), *order.wait(tuple(came_back)))
    z_there = hop(z_there, "expert", 1)
    send_half = same
    back_send = order.run(lambda h, g: outer(send_half, h, g, True), hidden, grad_arrived)
    grad_home[chips - 1] = back_to(chips - 1, pending)
    back_got = hop(order.after(back_send), "dp", 1)
    in_send = order.run(lambda g, a: outer(send_half, g, a, False), grads, arrived)
    grad_home = list(order.wait(tuple(grad_home)))
    m_here, m_there = order.run(lambda *v: sort_groups(v), *grad_home)
    m_there = hop(m_there, "expert", 1)

    out_half, dgate = order.run(
        lambda *v: bring_home(which, *v), rows, y, cot, gates, z_here, z_there
    )
    dgate_next = hop(dgate, "tensor", 1)
    m_there = order.wait(m_there)
    near_parts = []
    for n, (lo, hi) in enumerate(groups):
        near = order.run(lambda *v: sum_home(*v, lo, hi), rows, m_here, m_there)
        near_parts.append((near, hop(near, "tensor", 1)))
    dgate_next = order.wait(dgate_next)
    held, parts, sums, got = [], [], [], []
    for n, (lo, hi) in enumerate(groups):
        if n == len(groups) - 1:
            near_parts[n], back_got = order.wait((near_parts[n], back_got))
            in_got = hop(order.after(in_send), "dp", 1)
        *held, part, sums2, sums1, grad_router = order.run(
            lambda *v: attend_back(which, *v[:15], lo, hi, v[15:]),
            x, y, *near_parts[n], dgate, dgate_next, probs, ids_pad, narrow_all, cot, vectors, out_here, qkv, lse, qkv_w, *held,
        )
        parts.append(part)
        got.append(hop(part, "tensor", 1))
        sums.append(
            jnp.concatenate([0.5 * grad_router[:count], sums1[:2], 0.5 * sums2[:2]], axis=0)
        )
    dy, dyb, dqkv = held

    flat = lambda value: value.reshape(rows_all, -1)
    grad_outw = dot_tn(flat(dyb), flat(o_rows))
    grad_wqkv = dot_tn(flat(a_rows), flat(dqkv))
    tiny = jnp.transpose(sum(sums))
    tiny = jnp.pad(tiny, ((0, 0), (0, -tiny.shape[1] % LANES)))
    all_grads = jnp.concatenate([grad_wqkv, grad_outw, tiny], axis=1)
    keep_half = 1 - send_half
    total = core_sum(order.after(all_grads), BF)
    grad_back = order.run(
        lambda h, g, b: outer(keep_half, h, g, True, b), hidden, grad_arrived, back_got
    )[None]
    shards, leaving = chip_sum(order.wait(total), BF)
    grad_tokens = []
    for n, (lo, hi) in enumerate(groups):
        grad_tokens = [
            order.run(
                lambda *v: token_back(*v[:5], lo, hi, v[5:]),
                x, parts[n], got[n], dy, vectors, *grad_tokens,
            )
        ]
        if n == 0:
            shards, leaving = order.wait((shards, leaving))
            entering = hop(leaving, "dp", 1)
    out_other = hop(order.after(out_half), "tensor", 1)
    shards = order.wait(shards + entering.astype(F32))
    tiny = shards[:, 4 * HALF :]
    tiny_next = hop(tiny, "tensor", 1)
    grad_in = order.run(
        lambda g, a, b: outer(keep_half, g, a, False, b), grads, arrived, in_got
    )[None]
    tiny = tiny + tiny_next
    grad_tokens = grad_tokens[0][:, :SEQ].reshape(tok, D)
    block_out = jnp.where(
        here_t == 0,
        jnp.concatenate([out_half, out_other], axis=2),
        jnp.concatenate([out_other, out_half], axis=2),
    )
    block_out = block_out[:, :SEQ].reshape(tok, D)
    return (
        block_out,
        grad_tokens,
        tiny[:, count],
        tiny[:, count + 1],
        tiny[:, count + 2],
        tiny[:, count + 3],
        shards[:, :HALF],
        shards[:, HALF : 2 * HALF],
        shards[:, 2 * HALF : 3 * HALF],
        jnp.transpose(shards[:, 3 * HALF : 4 * HALF]),
        tiny[:, :count],
        grad_in,
        grad_back,
    )


def solution(mesh):
    rows = ("dp", "expert")
    in_specs = (
        P(rows, None),
        P(rows, None),
        P(rows),
        P(rows),
        P(rows),
        P(rows),
        P(rows, "tensor"),
        P(rows, "tensor"),
        P(rows, "tensor"),
        P("tensor", rows),
        P(rows, None),
        P("expert", "dp", "tensor"),
        P("expert", "tensor", "dp"),
        P(rows, None),
    )
    out_specs = (
        P(rows, None),
        P(rows, None),
        P(rows),
        P(rows),
        P(rows),
        P(rows),
        P(rows, "tensor"),
        P(rows, "tensor"),
        P(rows, "tensor"),
        P("tensor", rows),
        P(rows, None),
        P("expert", "dp", "tensor"),
        P("expert", "tensor", "dp"),
    )
    return jax.shard_map(
        on_device, mesh=mesh, in_specs=in_specs, out_specs=out_specs, check_vma=False
    )
```

```python
import functools

import jax
import jax.numpy as jnp
from jax import lax
from jax.experimental import pallas as pl
from jax.experimental.pallas import tpu as pltpu
from jax.sharding import PartitionSpec as P

D = 768
HALF = 384
HEADS = 12
SEQ = 197
ROWS = 208
HEAD = D // HEADS
SCALE = HEAD ** (-0.5)
EPSILON = 1e-06
HIGH = lax.Precision.HIGHEST
BF = jnp.bfloat16
F32 = jnp.float32
LANES = 128
TILE = 512
IN_CUTS = ((0, 112), (112, 176), (176, 384))
BACK_CUTS = ((0, 128), (128, 384))
TAIL_RATE = 0.305
TAIL = (
    0.12163973686996697,
    0.12246675128071258,
    0.10342128505066615,
    0.12102026121907625,
    -0.03797407148483761,
    0.1857138128109823,
    -0.15298645906475614,
    0.03669873020693663,
)
DENSITY = 0.3989422804014327


def hop(value, axis, offset):
    count = lax.axis_size(axis)
    return lax.ppermute(value, axis, [(i, i ^ offset) for i in range(count)])


class Order:
    def __init__(self):
        self.token = lax.create_token()

    def after(self, value):
        return lax.optimization_barrier((self.token, value))[1]

    def wait(self, value):
        self.token, value = lax.optimization_barrier((self.token, value))
        return value

    def run(self, function, *operands):
        return self.wait(function(*self.after(operands)))


def follow(value, first):
    token = lax.optimization_barrier((lax.create_token(), first))[0]
    return lax.optimization_barrier((token, value))[1]


def dot_nn(a, b):
    return lax.dot_general(a, b, (((1,), (0,)), ((), ())), preferred_element_type=F32)


def dot_nt(a, b):
    return lax.dot_general(a, b, (((1,), (1,)), ((), ())), preferred_element_type=F32)


def dot_tn(a, b):
    return lax.dot_general(a, b, (((0,), (0,)), ((), ())), preferred_element_type=F32)


def cost(flops=1000):
    return pl.CostEstimate(flops=flops, bytes_accessed=1000, transcendentals=0)


def image(width, lo=0):
    return pl.BlockSpec((1, ROWS, width), lambda i, *_: (i + lo, 0, 0))


def images(count, width, kind):
    return jax.ShapeDtypeStruct((count, ROWS, width), kind)


ANY = pl.BlockSpec(memory_space=pl.ANY)


def whole(shape):
    zeros = (0,) * len(shape)
    return pl.BlockSpec(shape, lambda *_: zeros)


def flag(value):
    return value.astype(jnp.int32).reshape(1)


def cross_kernel(here_ref, own_ref, across_ref, out_ref):
    first = here_ref[0] == 0
    out_ref[0] = jnp.where(first, own_ref[...], across_ref[...])
    out_ref[1] = jnp.where(first, across_ref[...], own_ref[...])


def cross(shard):
    across = hop(shard, "dp", 1)
    return pl.pallas_call(
        cross_kernel,
        grid_spec=pltpu.PrefetchScalarGridSpec(
            num_scalar_prefetch=1,
            grid=(1,),
            in_specs=[whole(shard.shape)] * 2,
            out_specs=whole((2,) + shard.shape),
        ),
        out_shape=jax.ShapeDtypeStruct((2,) + shard.shape, shard.dtype),
        name="cross",
        cost_estimate=cost(),
    )(flag(lax.axis_index("dp")), shard, across)


def stack_kernel(*refs):
    for n, ref in enumerate(refs[:-1]):
        refs[-1][n] = ref[...]


def stacked(parts):
    shape = (len(parts),) + parts[0].shape
    return pl.pallas_call(
        stack_kernel,
        grid=(1,),
        in_specs=[whole(p.shape) for p in parts],
        out_specs=whole(shape),
        out_shape=jax.ShapeDtypeStruct(shape, parts[0].dtype),
        name="stacked",
        cost_estimate=cost(),
    )(*parts)


def sort_kernel(*refs):
    parts, (mine_ref, away_ref) = refs[:-2], refs[-2:]
    for n, ref in enumerate(parts):
        mine_ref[n] = ref[0]
        away_ref[n] = ref[1]


def sort_groups(parts):
    shape = (len(parts),) + parts[0].shape[1:]
    return pl.pallas_call(
        sort_kernel,
        grid=(1,),
        in_specs=[whole(p.shape) for p in parts],
        out_specs=[whole(shape)] * 2,
        out_shape=[jax.ShapeDtypeStruct(shape, parts[0].dtype)] * 2,
        name="sort_groups",
        cost_estimate=cost(),
    )(*parts)


def add_kernel(near_ref, away_ref, out_ref):
    out_ref[...] = (near_ref[...] + away_ref[...].astype(F32)).astype(BF)


def add_halves(near, away):
    part = pl.BlockSpec((1,) + near.shape[1:], lambda i: (i, 0, 0))
    return pl.pallas_call(
        add_kernel,
        grid=(near.shape[0],),
        in_specs=[part, part],
        out_specs=part,
        out_shape=jax.ShapeDtypeStruct(near.shape, BF),
        name="add_halves",
        cost_estimate=cost(),
    )(near, away)


def vector_kernel(narrow_ref, out_ref, *, start):
    row = lax.broadcasted_iota(jnp.int32, (8, LANES), 0)
    lane = lax.broadcasted_iota(jnp.int32, (8, LANES), 1)
    wanted = jnp.where((lane == row + start) & (row < 4), 1.0, 0.0).astype(BF)
    out_ref[...] = dot_nt(wanted, narrow_ref[...])


def vectors_of(narrow, start):
    return pl.pallas_call(
        functools.partial(vector_kernel, start=start),
        grid=(1,),
        in_specs=[whole(narrow.shape)],
        out_specs=whole((8, D)),
        out_shape=jax.ShapeDtypeStruct((8, D), F32),
        name="vectors",
        cost_estimate=cost(),
    )(narrow)


def assemble_kernel(here_ref, same_ref, flip_ref, *out_refs):
    chips, _, rows, _ = same_ref.shape
    for chip in range(chips):
        for b, ref in enumerate((same_ref, flip_ref)):
            place = here_ref[0] ^ (2 * chip + b)
            for d in range(2):
                at = pl.ds(pl.multiple_of((d * 2 * chips + place) * rows, 16), rows)
                lo = 0
                for out_ref in out_refs:
                    out_ref[at, :] = ref[chip, d, :, lo : lo + out_ref.shape[1]]
                    lo += out_ref.shape[1]


def assemble(same, flipped, widths):
    chips, _, rows, columns = same.shape
    here = lax.axis_index("expert").astype(jnp.int32)
    if rows % 16 == 0:
        return pl.pallas_call(
            assemble_kernel,
            grid_spec=pltpu.PrefetchScalarGridSpec(
                num_scalar_prefetch=1,
                grid=(1,),
                in_specs=[whole(same.shape), whole(same.shape)],
                out_specs=[whole((4 * chips * rows, w)) for w in widths],
            ),
            out_shape=[jax.ShapeDtypeStruct((4 * chips * rows, w), same.dtype) for w in widths],
            name="assemble",
            cost_estimate=cost(),
        )(here.reshape(1), same, flipped)
    buffer = jnp.zeros((2, 2 * chips, rows, columns), same.dtype)
    for j in range(chips):
        for b, both in enumerate((same, flipped)):
            buffer = lax.dynamic_update_slice(buffer, both[j][:, None], (0, here ^ (2 * j + b), 0, 0))
    buffer = buffer.reshape(-1, columns)
    cuts = [sum(widths[:n]) for n in range(len(widths) + 1)]
    return [buffer[:, cuts[n] : cuts[n + 1]] for n in range(len(widths))]


def chip_copies(pair):
    count = lax.axis_size("expert")
    return [pair] + [hop(pair, "expert", k) for k in range(2, count, 2)]


def pick(array, index, axis):
    return lax.dynamic_index_in_dim(array, index, axis, False)


def chip_sum(total, wide):
    here_dp = lax.axis_index("dp")
    chip = lax.axis_index("expert") >> 1
    summed = pick(total, chip, 1)
    for k in range(1, total.shape[1]):
        summed = summed + hop(pick(total, chip ^ k, 1).astype(wide), "expert", 2 * k).astype(F32)
    return pick(summed, here_dp, 0), pick(summed, 1 - here_dp, 0).astype(wide)


def normed(values):
    average = jnp.mean(values, axis=-1, keepdims=True)
    centred = values - average
    variance = jnp.mean(centred * centred, axis=-1, keepdims=True)
    scale = lax.rsqrt(variance + EPSILON)
    return centred * scale, scale


def attend_kernel(x_ref, vec_ref, w_ref, *refs):
    a_ref, qkv_ref, o_ref, lse_ref, part_ref = refs[-5:]
    hat, _ = normed(x_ref[0].astype(F32))
    a = (hat * vec_ref[0:1, :] + vec_ref[1:2, :]).astype(BF)
    a_ref[0] = a
    qkv_ref[0] = dot_nn(a, w_ref[...]).astype(BF)
    keys_in = lax.broadcasted_iota(jnp.int32, (ROWS, ROWS), 1) < SEQ
    lane = lax.broadcasted_iota(jnp.int32, (ROWS, LANES), 1)
    lse = jnp.zeros((ROWS, LANES), F32)
    for h in range(HALF // HEAD):
        at = h * HEAD
        q = qkv_ref[0, :, at : at + HEAD]
        k = qkv_ref[0, :, HALF + at : HALF + at + HEAD]
        v = qkv_ref[0, :, 2 * HALF + at : 2 * HALF + at + HEAD]
        s = jnp.where(keys_in, dot_nt(q, k) * SCALE, -1e30)
        top = jnp.max(s, axis=1, keepdims=True)
        total = top + jnp.log(jnp.sum(jnp.exp(s - top), axis=1, keepdims=True))
        weights = jnp.exp(s - total).astype(BF)
        part_ref[0, :, at : at + HEAD] = dot_nn(weights, v).astype(BF)
        lse = jnp.where(lane == h, total, lse)
    lse_ref[0] = lse
    o_ref[0] = part_ref[0]


def attend(x, vectors, weight, lo, hi, held):
    total = x.shape[0]
    return pl.pallas_call(
        attend_kernel,
        grid=(hi - lo,),
        in_specs=[image(D, lo), whole(vectors.shape), whole(weight.shape)] + [ANY] * len(held),
        out_specs=[image(D, lo), image(3 * HALF, lo), image(HALF, lo), image(LANES, lo), image(HALF)],
        out_shape=[
            images(total, D, BF),
            images(total, 3 * HALF, BF),
            images(total, HALF, BF),
            images(total, LANES, F32),
            images(hi - lo, HALF, BF),
        ],
        input_output_aliases={3 + n: n for n in range(len(held))},
        name="attend",
        cost_estimate=cost(),
    )(x, vectors, weight, *held)


def route_kernel(
    which_ref, x_ref, own_ref, got_ref, vec_ref, here_ref, there_ref, router_ref, ids_ref, *refs, count
):
    y_ref, r_ref, g_ref, h_ref = refs[-4:]
    y = x_ref[0].astype(F32) + (
        dot_nt(own_ref[0], here_ref[...]) + dot_nt(got_ref[0], there_ref[...])
    )
    y_ref[0] = y
    hat, _ = normed(y)
    h = (hat * vec_ref[2:3, :] + vec_ref[3:4, :]).astype(BF)
    first = which_ref[0] == 0
    h_ref[0, :, :HALF] = jnp.where(first, h[:, :HALF], h[:, HALF:])
    h_ref[0, :, HALF:] = jnp.where(first, h[:, HALF:], h[:, :HALF])
    lane = lax.broadcasted_iota(jnp.int32, (ROWS, LANES), 1)
    logits = jnp.where(lane < count, dot_nn(h, router_ref[...]), -1e30)
    logits = jnp.exp(logits - jnp.max(logits, axis=1, keepdims=True))
    probs = logits / jnp.sum(logits, axis=1, keepdims=True)
    r_ref[0] = probs
    gates = jnp.zeros((ROWS, LANES), F32)
    for c in range(2):
        gate = jnp.sum(jnp.where(lane == ids_ref[0, :, c : c + 1], probs, 0.0), axis=1, keepdims=True)
        gates = jnp.where(lane == c, gate, gates)
    g_ref[0] = gates


def route(which, x, own, got, vectors, out_here, out_there, router, ids, count, lo, hi, held):
    total = x.shape[0]
    return pl.pallas_call(
        functools.partial(route_kernel, count=count),
        grid_spec=pltpu.PrefetchScalarGridSpec(
            num_scalar_prefetch=1,
            grid=(hi - lo,),
            in_specs=[
                image(D, lo),
                image(HALF),
                image(HALF),
                whole(vectors.shape),
                whole(out_here.shape),
                whole(out_there.shape),
                whole(router.shape),
                image(2, lo),
            ]
            + [ANY] * len(held),
            out_specs=[image(D, lo), image(LANES, lo), image(LANES, lo), image(D)],
        ),
        out_shape=[
            images(total, D, F32),
            images(total, LANES, F32),
            images(total, LANES, F32),
            images(hi - lo, D, BF),
        ],
        input_output_aliases={9 + n: n for n in range(len(held))},
        name="route",
        cost_estimate=cost(),
    )(which, x, own, got, vectors, out_here, out_there, router, ids, *held)


def send_kernel(*refs, parts, chips, gated):
    per = 3 if gated else 2
    groups = [refs[n * per * parts : (n + 1) * per * parts] for n in range(2)]
    out_refs = refs[2 * per * parts :]
    capacity = out_refs[0].shape[1]
    for out_ref, chip in zip(out_refs, chips):
        for r in range(2):
            rows, values, gates = (groups[r][n * parts : (n + 1) * parts] for n in range(3))
            places = lax.broadcasted_iota(jnp.int32, (capacity, 1), 0) + (2 * chip + r) * capacity
            picked = jnp.zeros((capacity, D), F32)
            weight = jnp.zeros((capacity, 1), F32)
            for n in range(parts):
                first = places == rows[n][0:1, :]
                second = places == rows[n][1:2, :]
                chosen = jnp.where(first | second, 1.0, 0.0).astype(BF)
                picked = picked + dot_nn(chosen, values[n][...])
                if gated:
                    each = jnp.where(
                        first, gates[n][0:1, :], jnp.where(second, gates[n][1:2, :], 0.0)
                    )
                    weight = weight + jnp.sum(each, axis=1, keepdims=True)
            if gated:
                picked = picked * weight
            out_ref[r] = picked.astype(BF)


def send_rows(own, other, capacity, chips, gated):
    operands = [part for group in (own, other) for kind in group for part in kind]
    return pl.pallas_call(
        functools.partial(send_kernel, parts=len(own[0]), chips=chips, gated=gated),
        grid=(1,),
        in_specs=[whole(o.shape) for o in operands],
        out_specs=[whole((2, capacity, D))] * len(chips),
        out_shape=[jax.ShapeDtypeStruct((2, capacity, D), BF)] * len(chips),
        name="send_gated" if gated else "send_rows",
        cost_estimate=cost(),
    )(*operands)


def first_lanes():
    row = lax.broadcasted_iota(jnp.int32, (8, LANES), 0)
    return jnp.where(row == lax.broadcasted_iota(jnp.int32, (8, LANES), 1), 1.0, 0.0)


def turn(columns):
    return lax.dot_general(
        first_lanes(), columns, (((1,), (1,)), ((), ())), precision=HIGH, preferred_element_type=F32
    )


def turn_back(rows):
    return lax.dot_general(
        rows, first_lanes(), (((0,), (0,)), ((), ())), precision=HIGH, preferred_element_type=F32
    )


def home_kernel(which_ref, rows_ref, middle_ref, grad_ref, gates_ref, own_ref, other_ref, out_ref, dgate_ref):
    value = middle_ref[0]
    grad = grad_ref[0].astype(F32)
    lane = lax.broadcasted_iota(jnp.int32, (ROWS, LANES), 1)
    found = jnp.zeros((ROWS, LANES), F32)
    chips, capacity = own_ref.shape[:2]
    places = lax.broadcasted_iota(jnp.int32, (1, capacity), 1)
    for c in range(2):
        picked = jnp.zeros((ROWS, HALF), F32)
        for chip in range(chips):
            for r, back_ref in enumerate((own_ref, other_ref)):
                at = rows_ref[0, :, c : c + 1] - (2 * chip + r) * capacity
                chosen = jnp.where(at == places, 1.0, 0.0)
                picked = picked + dot_nn(chosen.astype(BF), back_ref[chip])
        value = value + gates_ref[0, :, c : c + 1] * picked
        dgate = jnp.sum(picked * grad, axis=1, keepdims=True)
        found = jnp.where(lane == c, dgate, found)
    out_ref[0] = value.astype(BF)
    dgate_ref[0] = turn(found)


def bring_home(which, rows, middle, grad, gates, own, other):
    total = middle.shape[0]
    part = pl.BlockSpec((1, ROWS, HALF), lambda i, s: (i, 0, s[0]))
    return pl.pallas_call(
        home_kernel,
        grid_spec=pltpu.PrefetchScalarGridSpec(
            num_scalar_prefetch=1,
            grid=(total,),
            in_specs=[image(2), part, part, image(LANES), whole(own.shape), whole(other.shape)],
            out_specs=[image(HALF), pl.BlockSpec((1, 8, ROWS), lambda i, s: (i, 0, 0))],
        ),
        out_shape=[images(total, HALF, BF), jax.ShapeDtypeStruct((total, 8, ROWS), F32)],
        name="bring_home",
        cost_estimate=cost(),
    )(which, rows, middle, grad, gates, own, other)


def sum_kernel(rows_ref, own_ref, other_ref, out_ref):
    chips, capacity = own_ref.shape[:2]
    places = lax.broadcasted_iota(jnp.int32, (1, capacity), 1)
    total = jnp.zeros((ROWS, HALF), F32)
    for chip in range(chips):
        for r, back_ref in enumerate((own_ref, other_ref)):
            base = (2 * chip + r) * capacity
            chosen = (rows_ref[0, :, 0:1] - base == places) | (rows_ref[0, :, 1:2] - base == places)
            total = total + dot_nn(jnp.where(chosen, 1.0, 0.0).astype(BF), back_ref[chip])
    out_ref[0] = total.astype(BF)


def sum_home(rows, own, other, lo, hi):
    return pl.pallas_call(
        sum_kernel,
        grid=(hi - lo,),
        in_specs=[image(2, lo), whole(own.shape), whole(other.shape)],
        out_specs=image(HALF),
        out_shape=images(hi - lo, HALF, BF),
        name="sum_home",
        cost_estimate=cost(),
    )(rows, own, other)


def gelu_parts(u):
    size = jnp.abs(u)
    t = 1.0 / (1.0 + TAIL_RATE * size)
    poly = jnp.full_like(t, TAIL[-1])
    for c in TAIL[-2::-1]:
        poly = poly * t + c
    bell = jnp.exp(-0.5 * (u * u))
    tail = bell * (t * poly)
    normal = jnp.where(u >= 0.0, 1.0 - tail, tail)
    return u * normal, normal + u * (DENSITY * bell)


def in_order(same_ref, refs):
    same = same_ref[0] == 1
    n, m = len(IN_CUTS), len(BACK_CUTS)
    join = lambda refs, axis: jnp.concatenate([ref[...] for ref in refs], axis=axis)
    pairs = [
        (join(refs[:n], 0), join(refs[n : 2 * n], 0)),
        (join(refs[2 * n : 2 * n + m], 1), join(refs[2 * n + m :], 1)),
    ]
    return [v for a, b in pairs for v in (jnp.where(same, a, b), jnp.where(same, b, a))]


def weight_specs():
    across = [pl.BlockSpec((hi - lo, TILE), lambda i, s: (0, i)) for lo, hi in IN_CUTS]
    down = [pl.BlockSpec((TILE, hi - lo), lambda i, s: (i, 0)) for lo, hi in BACK_CUTS]
    return across * 2 + down * 2


def forward_kernel(same_ref, m_ref, *refs):
    *weights, g_ref, s_ref, zt_ref, zh_ref, acc = refs
    w1h, w1t, w2h, w2t = in_order(same_ref, weights)
    step = pl.program_id(0)
    last = pl.num_programs(0) - 1
    for b in range(m_ref.shape[0]):
        u = dot_nn(m_ref[b, :, :HALF], w1h) + dot_nn(m_ref[b, :, HALF:], w1t)
        g, slope = gelu_parts(u)
        g = g.astype(BF)
        g_ref[b] = g
        s_ref[b] = slope.astype(BF)
        away = dot_nn(g, w2t)
        near = dot_nn(g, w2h)

        @pl.when(step == 0)
        def _():
            acc[b] = away
            zh_ref[b] = near

        @pl.when(step > 0)
        def _():
            acc[b] += away
            zh_ref[b] += near

        @pl.when(step == last)
        def _():
            zt_ref[b] = acc[b].astype(BF)


def expert_forward(same, rows, *weights):
    blocks, capacity, _ = rows.shape
    hidden = weights[0].shape[1]
    wide = pl.BlockSpec((blocks, capacity, TILE), lambda i, s: (0, 0, i))
    make = lambda w, t: jax.ShapeDtypeStruct((blocks, capacity, w), t)
    return pl.pallas_call(
        forward_kernel,
        grid_spec=pltpu.PrefetchScalarGridSpec(
            num_scalar_prefetch=1,
            grid=(hidden // TILE,),
            in_specs=[whole(rows.shape)] + weight_specs(),
            out_specs=[wide, wide] + [whole((blocks, capacity, HALF))] * 2,
            scratch_shapes=[pltpu.VMEM((blocks, capacity, HALF), F32)],
        ),
        out_shape=[make(hidden, BF), make(hidden, BF), make(HALF, BF), make(HALF, F32)],
        name="expert_forward",
        cost_estimate=cost(),
    )(same, rows, *weights)


def backward_kernel(same_ref, z_ref, s_ref, *refs):
    *weights, u_ref, mt_ref, mh_ref, acc = refs
    w1h, w1t, w2h, w2t = in_order(same_ref, weights)
    step = pl.program_id(0)
    last = pl.num_programs(0) - 1
    for b in range(z_ref.shape[0]):
        grad = dot_nt(z_ref[b, :, :HALF], w2h) + dot_nt(z_ref[b, :, HALF:], w2t)
        grad = (grad * s_ref[b].astype(F32)).astype(BF)
        u_ref[b] = grad
        away = dot_nt(grad, w1t)
        near = dot_nt(grad, w1h)

        @pl.when(step == 0)
        def _():
            acc[b] = away
            mh_ref[b] = near

        @pl.when(step > 0)
        def _():
            acc[b] += away
            mh_ref[b] += near

        @pl.when(step == last)
        def _():
            mt_ref[b] = acc[b].astype(BF)


def expert_backward(same, rows, slope, *weights):
    blocks, capacity, _ = rows.shape
    hidden = weights[0].shape[1]
    wide = pl.BlockSpec((blocks, capacity, TILE), lambda i, s: (0, 0, i))
    make = lambda w, t: jax.ShapeDtypeStruct((blocks, capacity, w), t)
    return pl.pallas_call(
        backward_kernel,
        grid_spec=pltpu.PrefetchScalarGridSpec(
            num_scalar_prefetch=1,
            grid=(hidden // TILE,),
            in_specs=[whole(rows.shape), wide] + weight_specs(),
            out_specs=[wide] + [whole((blocks, capacity, HALF))] * 2,
            scratch_shapes=[pltpu.VMEM((blocks, capacity, HALF), F32)],
        ),
        out_shape=[make(hidden, BF), make(HALF, BF), make(HALF, F32)],
        name="expert_backward",
        cost_estimate=cost(),
    )(same, rows, slope, *weights)


def outer_kernel(which_ref, *refs, chunks, hidden_first, added):
    wides = refs[:chunks]
    narrows = refs[chunks : 2 * chunks]
    out_ref = refs[-1]
    total = None
    for wide_ref, slim_ref in zip(wides, narrows):
        for b in range(wide_ref.shape[0]):
            slim = slim_ref[b]
            term = dot_tn(wide_ref[b], slim) if hidden_first else dot_tn(slim, wide_ref[b])
            total = term if total is None else total + term
    if added:
        total = total + refs[-2][...].astype(F32)
    out_ref[...] = total.astype(out_ref.dtype)


def outer(which, wides, narrows, hidden_first, extra=None):
    per, capacity, hidden = wides[0].shape
    slim = pl.BlockSpec((per, capacity, HALF), lambda i, s: (0, 0, s[0]))
    if hidden_first:
        shape, out = (hidden, HALF), pl.BlockSpec((TILE, HALF), lambda i, s: (i, 0))
    else:
        shape, out = (HALF, hidden), pl.BlockSpec((HALF, TILE), lambda i, s: (0, i))
    specs = [pl.BlockSpec((per, capacity, TILE), lambda i, s: (0, 0, i))] * len(wides)
    specs += [slim] * len(narrows)
    operands = list(wides) + list(narrows)
    if extra is not None:
        specs.append(out)
        operands.append(extra)
    return pl.pallas_call(
        functools.partial(
            outer_kernel,
            chunks=len(wides),
            hidden_first=hidden_first,
            added=extra is not None,
        ),
        grid_spec=pltpu.PrefetchScalarGridSpec(
            num_scalar_prefetch=1, grid=(hidden // TILE,), in_specs=specs, out_specs=out
        ),
        out_shape=jax.ShapeDtypeStruct(shape, BF if extra is None else F32),
        name="outer_send" if extra is None else "outer_keep",
        cost_estimate=cost(),
    )(which, *operands)


def norm_back(grad, hat, scale, gain):
    inner = grad * gain
    return scale * (
        inner
        - jnp.mean(inner, axis=-1, keepdims=True)
        - hat * jnp.mean(inner * hat, axis=-1, keepdims=True)
    )


def add_sums(ref, grad, hat, first):
    sums = [jnp.sum(grad * hat, axis=0, keepdims=True), jnp.sum(grad, axis=0, keepdims=True)]

    @pl.when(first)
    def _():
        ref[...] = jnp.zeros_like(ref)

    ref[0:1, :] += sums[0]
    ref[1:2, :] += sums[1]


def attend_back_kernel(
    which_ref,
    x_ref,
    y_ref,
    near_ref,
    away_ref,
    dgate_ref,
    dgate2_ref,
    probs_ref,
    ids_ref,
    narrow_ref,
    cot_ref,
    vec_ref,
    out_w_ref,
    qkv_ref,
    lse_ref,
    w_ref,
    *refs,
):
    dy_ref, dyb_ref, dqkv_ref, part_ref, sums2_ref, sums1_ref, router_ref, att_ref = refs[-8:]
    first = which_ref[0] == 0
    start = pl.program_id(0) == 0
    near = near_ref[0].astype(F32)
    away = away_ref[0].astype(F32)
    dgate = turn_back(dgate_ref[0] + dgate2_ref[0])
    lane = lax.broadcasted_iota(jnp.int32, (ROWS, LANES), 1)
    probs = probs_ref[0]
    grad_probs = sum(
        jnp.where(lane == ids_ref[0, :, c : c + 1], dgate[:, c : c + 1], 0.0) for c in range(2)
    )
    grad_logits = probs * (grad_probs - jnp.sum(probs * grad_probs, axis=1, keepdims=True))
    high = grad_logits.astype(BF)
    low = (grad_logits - high.astype(F32)).astype(BF)
    narrow = narrow_ref[...]
    grad = (dot_nt(high, narrow) + dot_nt(low, narrow)) + jnp.concatenate(
        [jnp.where(first, near, away), jnp.where(first, away, near)], axis=1
    )
    hat, scale = normed(y_ref[0])
    h = (hat * vec_ref[2:3, :] + vec_ref[3:4, :]).astype(BF)
    grad_router = dot_tn(high, h) + dot_tn(low, h)

    @pl.when(start)
    def _():
        router_ref[...] = grad_router

    @pl.when(jnp.logical_not(start))
    def _():
        router_ref[...] += grad_router

    add_sums(sums2_ref, grad, hat, start)
    dy = cot_ref[0].astype(F32) + norm_back(grad, hat, scale, vec_ref[2:3, :])
    dy_ref[0] = dy
    dyb = dy.astype(BF)
    dyb_ref[0] = dyb
    att_ref[...] = dot_nn(dyb, out_w_ref[...]).astype(BF)
    keys_in = lax.broadcasted_iota(jnp.int32, (ROWS, ROWS), 1) < SEQ
    for h in range(HALF // HEAD):
        at = h * HEAD
        q = qkv_ref[0, :, at : at + HEAD]
        k = qkv_ref[0, :, HALF + at : HALF + at + HEAD]
        v = qkv_ref[0, :, 2 * HALF + at : 2 * HALF + at + HEAD]
        do = att_ref[:, at : at + HEAD]
        s = jnp.where(keys_in, dot_nt(q, k) * SCALE, -1e30)
        weights = jnp.exp(s - lse_ref[0, :, h : h + 1])
        dv = dot_tn(weights.astype(BF), do)
        dp = dot_nt(do, v)
        ds = (weights * (dp - jnp.sum(weights * dp, axis=1, keepdims=True))).astype(BF)
        dqkv_ref[0, :, at : at + HEAD] = (dot_nn(ds, k) * SCALE).astype(BF)
        dqkv_ref[0, :, HALF + at : HALF + at + HEAD] = (dot_tn(ds, q) * SCALE).astype(BF)
        dqkv_ref[0, :, 2 * HALF + at : 2 * HALF + at + HEAD] = dv.astype(BF)
    part = dot_nt(dqkv_ref[0], w_ref[...])
    part_ref[0] = part.astype(BF)
    hat, _ = normed(x_ref[0].astype(F32))
    add_sums(sums1_ref, part, hat, start)


def attend_back(which, x, y, near, away, dgate, dgate2, probs, ids, narrow, cot, vectors, out_w, qkv, lse, weight, lo, hi, held):
    total = y.shape[0]
    turned = pl.BlockSpec((1, 8, ROWS), lambda i, s: (i + lo, 0, 0))
    return pl.pallas_call(
        attend_back_kernel,
        grid_spec=pltpu.PrefetchScalarGridSpec(
            num_scalar_prefetch=1,
            grid=(hi - lo,),
            in_specs=[
                image(D, lo),
                image(D, lo),
                image(HALF),
                image(HALF),
                turned,
                turned,
                image(LANES, lo),
                image(2, lo),
                whole(narrow.shape),
                image(D, lo),
                whole(vectors.shape),
                whole(out_w.shape),
                image(3 * HALF, lo),
                image(LANES, lo),
                whole(weight.shape),
            ]
            + [ANY] * len(held),
            out_specs=[
                image(D, lo),
                image(D, lo),
                image(3 * HALF, lo),
                image(D),
                whole((8, D)),
                whole((8, D)),
                whole((LANES, D)),
            ],
            scratch_shapes=[pltpu.VMEM((ROWS, HALF), BF)],
        ),
        out_shape=[
            images(total, D, F32),
            images(total, D, BF),
            images(total, 3 * HALF, BF),
            images(hi - lo, D, BF),
            jax.ShapeDtypeStruct((8, D), F32),
            jax.ShapeDtypeStruct((8, D), F32),
            jax.ShapeDtypeStruct((LANES, D), F32),
        ],
        input_output_aliases={16 + n: n for n in range(len(held))},
        name="attend_back",
        cost_estimate=cost(),
    )(which, x, y, near, away, dgate, dgate2, probs, ids, narrow, cot, vectors, out_w, qkv, lse, weight, *held)


def token_kernel(x_ref, own_ref, got_ref, dy_ref, vec_ref, *refs):
    out_ref = refs[-1]
    grad = own_ref[0].astype(F32) + got_ref[0].astype(F32)
    hat, scale = normed(x_ref[0].astype(F32))
    out_ref[0] = dy_ref[0] + norm_back(grad, hat, scale, vec_ref[0:1, :])


def token_back(x, own, got, dy, vectors, lo, hi, held):
    total = x.shape[0]
    return pl.pallas_call(
        token_kernel,
        grid=(hi - lo,),
        in_specs=[image(D, lo), image(D), image(D), image(D, lo), whole(vectors.shape)]
        + [ANY] * len(held),
        out_specs=image(D, lo),
        out_shape=images(total, D, F32),
        input_output_aliases={5 + n: n for n in range(len(held))},
        name="token_back",
        cost_estimate=cost(),
    )(x, own, got, dy, vectors, *held)


def exact(a, b, contract):
    return lax.dot_general(
        a, b, ((contract[:1], contract[1:]), ((), ())), precision=HIGH, preferred_element_type=F32
    )


def of_image(i, tok):
    row = lax.broadcasted_iota(jnp.int32, (ROWS, tok), 0)
    token = lax.broadcasted_iota(jnp.int32, (ROWS, tok), 1)
    return jnp.where((token == row + i * SEQ) & (row < SEQ), 1.0, 0.0)


def image_kernel(which_ref, tok_ref, cot_ref, x_ref, cot_out_ref, here_ref):
    mine = of_image(pl.program_id(0), tok_ref.shape[0]).astype(BF)
    x_ref[0] = dot_nn(mine, tok_ref[...]).astype(BF)
    cot = dot_nn(mine, cot_ref[...]).astype(BF)
    cot_out_ref[0] = cot
    first = which_ref[0] == 0
    here_ref[0, :, :HALF] = jnp.where(first, cot[:, :HALF], cot[:, HALF:])
    here_ref[0, :, HALF:] = jnp.where(first, cot[:, HALF:], cot[:, :HALF])


def image_rows(which, tokens, cotangent):
    pictures = tokens.shape[0] // SEQ
    return pl.pallas_call(
        image_kernel,
        grid_spec=pltpu.PrefetchScalarGridSpec(
            num_scalar_prefetch=1,
            grid=(pictures,),
            in_specs=[whole(tokens.shape)] * 2,
            out_specs=[image(D)] * 3,
        ),
        out_shape=[images(pictures, D, BF)] * 3,
        name="image_rows",
        cost_estimate=cost(),
    )(which, tokens, cotangent)


def slot_kernel(here_ref, ids_ref, rows_ref, lanes_ref, ids_out_ref, *, capacity):
    tok = ids_ref.shape[0]
    lane = lax.broadcasted_iota(jnp.int32, (tok, LANES), 1)
    earlier = jnp.where(
        lax.broadcasted_iota(jnp.int32, (tok, tok), 1) < lax.broadcasted_iota(jnp.int32, (tok, tok), 0),
        1.0, 0.0,
    ).astype(BF)
    ids = [ids_ref[:, c : c + 1] for c in range(2)]
    taken = jnp.zeros((1, LANES), F32)
    table = jnp.zeros((tok, LANES), F32)
    for c in range(2):
        onehot = jnp.where(lane == ids[c], 1.0, 0.0)
        before = dot_nn(earlier, onehot.astype(BF)) + taken
        slot = jnp.sum(before * onehot, axis=1, keepdims=True)
        taken = taken + jnp.sum(onehot, axis=0, keepdims=True)
        place = ((ids[c] ^ here_ref[0]) * capacity).astype(F32) + slot + 1.0
        table = jnp.where(lane == c, place, table)
        table = jnp.where(lane == 2 + c, ids[c].astype(F32) + 1.0, table)
    for i in range(rows_ref.shape[0]):
        part = exact(of_image(i, tok), table, (1, 0)) - 1.0
        whole_part = part.astype(jnp.int32)
        rows_ref[i] = whole_part[:, 0:2]
        ids_out_ref[i] = whole_part[:, 2:4]
        lanes_ref[:, i * ROWS : (i + 1) * ROWS] = exact(first_lanes(), part, (1, 1)).astype(jnp.int32)


def slot_rows(here, expert_ids, capacity):
    tok = expert_ids.shape[0]
    pictures = tok // SEQ
    shapes = [(pictures, ROWS, 2), (8, pictures * ROWS), (pictures, ROWS, 2)]
    rows, lanes, ids = pl.pallas_call(
        functools.partial(slot_kernel, capacity=capacity),
        grid_spec=pltpu.PrefetchScalarGridSpec(
            num_scalar_prefetch=1,
            grid=(1,),
            in_specs=[whole(expert_ids.shape)],
            out_specs=[whole(shape) for shape in shapes],
        ),
        out_shape=[jax.ShapeDtypeStruct(shape, jnp.int32) for shape in shapes],
        name="slot_rows",
        cost_estimate=cost(),
    )(flag(here), expert_ids)
    return rows, lanes[:2], ids


def projection_kernel(core_ref, *refs, parts, split):
    a_ref, dqkv_ref, dyb_ref, o_ref = refs[:4]
    routers, ones, twos = (refs[4 + n * parts : 4 + (n + 1) * parts] for n in range(3))
    out_ref = refs[-1]
    step = pl.program_id(0)
    last = pl.num_programs(0) - 1
    qkv = dot_tn(a_ref[0], dqkv_ref[0])
    out = dot_tn(dyb_ref[0], o_ref[0])

    @pl.when(step == 0)
    def _():
        out_ref[:, : 3 * HALF] = qkv
        out_ref[:, 3 * HALF : 4 * HALF] = out
        total = 0.5 * sum(r[...] for r in routers)
        sums = jnp.concatenate(
            [sum(r[0:2, :] for r in ones), 0.5 * sum(r[0:2, :] for r in twos), jnp.zeros((4, D), F32)],
            axis=0,
        )
        out_ref[:, 4 * HALF :] = jnp.transpose(
            jnp.concatenate([total[: LANES - 8], sums], axis=0)
        )

    @pl.when(step > 0)
    def _():
        out_ref[:, : 3 * HALF] += qkv
        out_ref[:, 3 * HALF : 4 * HALF] += out

    if split:

        @pl.when(step == last)
        def _():
            near_ref, away_ref = refs[-3:-1]
            dps, chips, rows, _ = near_ref.shape
            for d in range(dps):
                for chip in range(chips):
                    at = (2 * (d * chips + chip) + core_ref[0]) * rows
                    near_ref[d, chip] = out_ref[pl.ds(pl.multiple_of(at, 16), rows), :]
                    at = (2 * (d * chips + chip) + 1 - core_ref[0]) * rows
                    away = out_ref[pl.ds(pl.multiple_of(at, 16), rows), :]
                    away_ref[d, chip] = away.astype(BF)


def projection_grads(a_rows, dqkv, dyb, o_rows, *small):
    count = lax.axis_size("expert")
    core = lax.axis_index("expert") & 1
    rows = D // (2 * count)
    split = rows % 16 == 0
    shape = (D, 4 * HALF + LANES)
    shares = (2, count // 2, rows, shape[1])
    kinds = [(shares, F32), (shares, BF)] if split else [(shape, F32)]
    out = pl.pallas_call(
        functools.partial(projection_kernel, parts=len(small) // 3, split=split),
        grid_spec=pltpu.PrefetchScalarGridSpec(
            num_scalar_prefetch=1,
            grid=(a_rows.shape[0],),
            in_specs=[image(D), image(3 * HALF), image(D), image(HALF)]
            + [whole(v.shape) for v in small],
            out_specs=[whole(k) for k, _ in kinds],
            scratch_shapes=[pltpu.VMEM(shape, F32)] if split else [],
        ),
        out_shape=[jax.ShapeDtypeStruct(*kind) for kind in kinds],
        name="projection_grads",
        cost_estimate=cost(),
    )(flag(core), a_rows, dqkv, dyb, o_rows, *small)
    if split:
        return out
    blocks = out[0].reshape((2, count // 2, 2, rows, -1))
    return pick(blocks, core, 2), pick(blocks, 1 - core, 2).astype(BF)


def on_device(
    tokens,
    cotangent,
    ln1_gain,
    ln1_bias,
    ln2_gain,
    ln2_bias,
    w_query,
    w_key,
    w_value,
    w_out,
    w_router,
    w_in,
    w_back,
    expert_ids,
):
    count = lax.axis_size("expert")
    chips = count // 2
    tok = tokens.shape[0]
    capacity = (10 * tok + 32 * count - 1) // (32 * count) * 8
    pictures = tok // SEQ
    rows_all = pictures * ROWS
    cut = (pictures + 1) // 2
    groups = [(0, cut), (cut, pictures)] if pictures > 1 else [(0, pictures)]
    lanes_of = lambda value: [value[:, lo * ROWS : hi * ROWS] for lo, hi in groups]
    here = lax.axis_index("expert")
    here_dp = lax.axis_index("dp")
    here_t = lax.axis_index("tensor")
    which = here_t.astype(jnp.int32).reshape(1)
    same = here_t == here_dp

    order = Order()

    small = jnp.stack([ln1_gain, ln1_bias, ln2_gain, ln2_bias], axis=1)
    narrow = jnp.concatenate([w_router, small], axis=1)
    narrow = jnp.pad(narrow, ((0, 0), (0, LANES - narrow.shape[1])))
    first_pack = jnp.concatenate(
        [w_query, w_key, w_value, narrow, jnp.transpose(w_out)], axis=1
    ).astype(BF)
    pair = cross(first_pack)
    in_own = [follow(w_in, first_pack)[0, lo:hi].astype(BF) for lo, hi in IN_CUTS]
    back_own = [follow(w_back, first_pack)[0, :, lo:hi].astype(BF) for lo, hi in BACK_CUTS]
    rows, rows_lane, ids_pad = slot_rows(here, follow(expert_ids, first_pack), capacity)
    own_lanes = lanes_of(rows_lane)
    pair, in_own, back_own, rows, rows_lane, ids_pad, own_lanes = order.wait(
        (pair, in_own, back_own, rows, rows_lane, ids_pad, own_lanes)
    )

    same_chips = stacked(chip_copies(order.after(pair)))
    in_other = [hop(order.after(in_own[0]), "dp", 1)]
    x, cot, cot_here = order.run(lambda *v: image_rows(which, *v), tokens, cotangent)
    cot_here = cot_here.reshape(rows_all, D)
    same_chips, in_other[0] = order.wait((same_chips, in_other[0]))
    in_other.append(hop(order.after(in_own[1]), "dp", 1))
    flipped = order.wait(hop(order.after(same_chips), "expert", 1))
    qkv_w, narrow_all, out_here = order.run(
        lambda *v: assemble(*v, (3 * HALF, LANES, HALF)), same_chips, flipped
    )
    out_there = hop(order.after(out_here), "tensor", 1)
    vectors = order.run(lambda v: vectors_of(v, count), narrow_all)
    in_other[1] = order.wait(in_other[1])
    in_other.append(hop(order.after(in_own[2]), "dp", 1))
    rows_next = hop(order.after(rows_lane), "expert", 1)
    cot_next = hop(order.after(cot_here), "expert", 1)

    held, o_parts, got_parts = [], [], []
    for n, (lo, hi) in enumerate(groups):
        *held, o_part = order.run(
            lambda x, v, w, *h: attend(x, v, w, lo, hi, h), x, vectors, qkv_w, *held
        )
        o_parts.append(o_part)
        got_parts.append(hop(o_part, "tensor", 1))
        if n == 0:
            rows_next, cot_next = order.wait((rows_next, cot_next))
    a_rows, qkv, o_rows, lse = held
    out_there = order.wait(out_there)
    got_parts, in_other[2] = order.wait((got_parts, in_other[2]))
    back_other = [hop(order.after(back_own[0]), "dp", 1)]
    next_lanes = order.wait(lanes_of(rows_next))
    held, h_parts, h_next = [], [], []
    for n, (lo, hi) in enumerate(groups):
        *held, h_part = order.run(
            lambda x, o, g, v, w, t, r, i, *h: route(which, x, o, g, v, w, t, r, i, count, lo, hi, h),
            x, o_parts[n], got_parts[n], vectors, out_here, out_there, narrow_all, ids_pad, *held,
        )
        h_parts.append(h_part.reshape(-1, D))
        if n == len(groups) - 1:
            gates_lane = jnp.transpose(held[2].reshape(rows_all, LANES)[:, :2])
            back_other[0], gates_lane = order.wait((back_other[0], gates_lane))
            h_parts[-1] = order.after(h_parts[-1])
            back_other.append(hop(order.after(back_own[1]), "dp", 1))
        h_next.append(hop(h_parts[-1], "expert", 1))
    y, probs, gates = held
    gates_next = hop(order.after(gates_lane), "expert", 1)

    own = (own_lanes, h_parts)
    other = (next_lanes, h_next)
    far = list(range(1, chips))
    outgoing = order.run(lambda *v: send_rows(*v, capacity, far, False), own, other)
    arrived = [None] + [hop(o, "expert", 2 * c) for o, c in zip(outgoing, far)]
    (arrived[0],) = order.run(lambda *v: send_rows(*v, capacity, [0], False), own, other)
    gates_next = order.wait(gates_next)
    own = ([rows_lane], [cot_here], [gates_lane])
    other = ([rows_next], [cot_next], [gates_next])
    grad_outgoing = order.run(lambda *v: send_rows(*v, capacity, far, True), own, other)
    grad_arrived = [None] * chips
    back_other[1] = order.wait(back_other[1])
    (grad_arrived[0],) = order.run(lambda *v: send_rows(*v, capacity, [0], True), own, other)
    weights = (*in_own, *in_other, *back_own, *back_other)
    same = flag(same)

    hidden, slopes, grads = [], [], []
    came_back, grad_home = [None] * chips, [None] * chips

    def back_to(chip, waiting):
        value = order.run(add_halves, *waiting)
        return hop(value, "expert", 2 * chip) if chip else value

    leaving = []

    def settle_oldest():
        home, chip, waiting = leaving.pop(0)
        home[chip] = back_to(chip, waiting)

    for c in range(chips):
        if c == 1:
            arrived[1:] = order.wait(arrived[1:])
            if chips <= 4:
                grad_arrived[1:] = [
                    hop(order.after(o), "expert", 2 * k) for o, k in zip(grad_outgoing, far)
                ]
        if c and chips > 4:
            grad_arrived[c] = hop(order.after(grad_outgoing[c - 1]), "expert", 2 * c)
        if c == chips - 1 and chips <= 4:
            grad_arrived[1:] = order.wait(grad_arrived[1:])
        g, s, zt, zh = order.run(lambda *v: expert_forward(same, *v), arrived[c], *weights)
        hidden.append(g)
        slopes.append(s)
        if len(leaving) > 1:
            settle_oldest()
        leaving.append((came_back, c, (zh, hop(order.after(zt), "tensor", 1))))
    for c in range(chips):
        if c and chips > 4:
            grad_arrived[c] = order.wait(grad_arrived[c])
        u, mt, mh = order.run(
            lambda *v: expert_backward(same, *v), grad_arrived[c], slopes[c], *weights
        )
        grads.append(u)
        settle_oldest()
        leaving.append((grad_home, c, (mh, hop(order.after(mt), "tensor", 1))))
        if c >= chips // 2:
            step = 2 * (chips - 1) // chips
            for k in range(1 + (c - chips // 2) * step, 1 + (c - chips // 2 + 1) * step):
                came_back[k] = order.wait(came_back[k])
    z_here, z_there = order.run(lambda *v: sort_groups(v), *order.wait(tuple(came_back)))
    z_there = hop(z_there, "expert", 1)
    send_half = same
    settle_oldest()
    back_send = order.run(lambda h, g: outer(send_half, h, g, True), hidden, grad_arrived)
    settle_oldest()
    back_got = hop(order.after(back_send), "dp", 1)
    in_send = order.run(lambda g, a: outer(send_half, g, a, False), grads, arrived)
    grad_home = list(order.wait(tuple(grad_home)))
    m_here, m_there = order.run(lambda *v: sort_groups(v), *grad_home)
    m_there = hop(m_there, "expert", 1)

    out_half, dgate = order.run(
        lambda *v: bring_home(which, *v), rows, y, cot, gates, z_here, z_there
    )
    dgate_next = hop(dgate, "tensor", 1)
    m_there = order.wait(m_there)
    near_parts = []
    for n, (lo, hi) in enumerate(groups):
        near = order.run(lambda *v: sum_home(*v, lo, hi), rows, m_here, m_there)
        near_parts.append((near, hop(near, "tensor", 1)))
        if n == 0:
            back_got, dgate_next = order.wait((back_got, dgate_next))
    held, parts, sums, got = [], [], [], []
    for n, (lo, hi) in enumerate(groups):
        if n == len(groups) - 1:
            near_parts[n] = order.wait(near_parts[n])
            in_got = hop(order.after(in_send), "dp", 1)
        *held, part, sums2, sums1, grad_router = order.run(
            lambda *v: attend_back(which, *v[:15], lo, hi, v[15:]),
            x, y, *near_parts[n], dgate, dgate_next, probs, ids_pad, narrow_all, cot, vectors, out_here, qkv, lse, qkv_w, *held,
        )
        parts.append(part)
        got.append(hop(part, "tensor", 1))
        sums.append((grad_router, sums1, sums2))
    dy, dyb, dqkv = held

    routers, ones, twos = zip(*sums)
    total, total_away = order.run(
        projection_grads, a_rows, dqkv, dyb, o_rows, *routers, *ones, *twos
    )
    keep_half = 1 - send_half
    grad_back = order.run(
        lambda h, g, b: outer(keep_half, h, g, True, b), hidden, grad_arrived, back_got
    )[None]
    in_got, got[0] = order.wait((in_got, got[0]))
    total_got = hop(order.after(total_away), "expert", 1)
    grad_in = order.run(
        lambda g, a, b: outer(keep_half, g, a, False, b), grads, arrived, in_got
    )[None]
    total_got = order.wait(total_got)
    shards, leaving = chip_sum(order.wait(total + total_got.astype(F32)), BF)
    shards, leaving, got = order.wait((shards, leaving, got))
    entering = hop(leaving, "dp", 1)
    out_other = hop(order.after(out_half), "tensor", 1)
    grad_tokens = []
    for n, (lo, hi) in enumerate(groups):
        grad_tokens = [
            order.run(
                lambda *v: token_back(*v[:5], lo, hi, v[5:]),
                x, parts[n], got[n], dy, vectors, *grad_tokens,
            )
        ]
    shards = order.wait(shards + entering.astype(F32))
    tiny = shards[:, 4 * HALF :]
    tiny = tiny + hop(tiny, "tensor", 1)
    grad_tokens = grad_tokens[0][:, :SEQ].reshape(tok, D)
    block_out = jnp.where(
        here_t == 0,
        jnp.concatenate([out_half, out_other], axis=2),
        jnp.concatenate([out_other, out_half], axis=2),
    )
    block_out = block_out[:, :SEQ].reshape(tok, D)
    return (
        block_out,
        grad_tokens,
        tiny[:, LANES - 8],
        tiny[:, LANES - 7],
        tiny[:, LANES - 6],
        tiny[:, LANES - 5],
        shards[:, :HALF],
        shards[:, HALF : 2 * HALF],
        shards[:, 2 * HALF : 3 * HALF],
        jnp.transpose(shards[:, 3 * HALF : 4 * HALF]),
        tiny[:, :count],
        grad_in,
        grad_back,
    )


def solution(mesh):
    rows = ("dp", "expert")
    in_specs = (
        P(rows, None),
        P(rows, None),
        P(rows),
        P(rows),
        P(rows),
        P(rows),
        P(rows, "tensor"),
        P(rows, "tensor"),
        P(rows, "tensor"),
        P("tensor", rows),
        P(rows, None),
        P("expert", "dp", "tensor"),
        P("expert", "tensor", "dp"),
        P(rows, None),
    )
    out_specs = (
        P(rows, None),
        P(rows, None),
        P(rows),
        P(rows),
        P(rows),
        P(rows),
        P(rows, "tensor"),
        P(rows, "tensor"),
        P(rows, "tensor"),
        P("tensor", rows),
        P(rows, None),
        P("expert", "dp", "tensor"),
        P("expert", "tensor", "dp"),
    )
    return jax.shard_map(
        on_device, mesh=mesh, in_specs=in_specs, out_specs=out_specs, check_vma=False
    )
```

```python
import functools

import jax
import jax.numpy as jnp
from jax import lax
from jax.experimental import pallas as pl
from jax.experimental.pallas import tpu as pltpu
from jax.sharding import PartitionSpec as P

D = 768
HALF = 384
HEADS = 12
SEQ = 197
ROWS = 208
HEAD = D // HEADS
SCALE = HEAD ** (-0.5)
EPSILON = 1e-06
HIGH = lax.Precision.HIGHEST
BF = jnp.bfloat16
F32 = jnp.float32
LANES = 128
TILE = 512
IN_CUTS = ((0, 112), (112, 176), (176, 384))
BACK_CUTS = ((0, 128), (128, 256), (256, 384))
TAIL_RATE = 0.305
TAIL = (
    0.12163973686996697,
    0.12246675128071258,
    0.10342128505066615,
    0.12102026121907625,
    -0.03797407148483761,
    0.1857138128109823,
    -0.15298645906475614,
    0.03669873020693663,
)
DENSITY = 0.3989422804014327


def hop(value, axis, offset):
    count = lax.axis_size(axis)
    return lax.ppermute(value, axis, [(i, i ^ offset) for i in range(count)])


class Order:
    def __init__(self):
        self.token = lax.create_token()

    def after(self, value):
        return lax.optimization_barrier((self.token, value))[1]

    def wait(self, value):
        self.token, value = lax.optimization_barrier((self.token, value))
        return value

    def run(self, function, *operands):
        return self.wait(function(*self.after(operands)))


def follow(value, first):
    token = lax.optimization_barrier((lax.create_token(), first))[0]
    return lax.optimization_barrier((token, value))[1]


def dot_nn(a, b):
    return lax.dot_general(a, b, (((1,), (0,)), ((), ())), preferred_element_type=F32)


def dot_nt(a, b):
    return lax.dot_general(a, b, (((1,), (1,)), ((), ())), preferred_element_type=F32)


def dot_tn(a, b):
    return lax.dot_general(a, b, (((0,), (0,)), ((), ())), preferred_element_type=F32)


def cost(flops=1000):
    return pl.CostEstimate(flops=flops, bytes_accessed=1000, transcendentals=0)


def image(width, lo=0):
    return pl.BlockSpec((1, ROWS, width), lambda i, *_: (i + lo, 0, 0))


def images(count, width, kind):
    return jax.ShapeDtypeStruct((count, ROWS, width), kind)


ANY = pl.BlockSpec(memory_space=pl.ANY)


def whole(shape):
    zeros = (0,) * len(shape)
    return pl.BlockSpec(shape, lambda *_: zeros)


def flag(value):
    return value.astype(jnp.int32).reshape(1)


def cross_kernel(here_ref, own_ref, across_ref, out_ref):
    first = here_ref[0] == 0
    out_ref[0] = jnp.where(first, own_ref[...], across_ref[...])
    out_ref[1] = jnp.where(first, across_ref[...], own_ref[...])


def cross(shard):
    across = hop(shard, "dp", 1)
    return pl.pallas_call(
        cross_kernel,
        grid_spec=pltpu.PrefetchScalarGridSpec(
            num_scalar_prefetch=1,
            grid=(1,),
            in_specs=[whole(shard.shape)] * 2,
            out_specs=whole((2,) + shard.shape),
        ),
        out_shape=jax.ShapeDtypeStruct((2,) + shard.shape, shard.dtype),
        name="cross",
        cost_estimate=cost(),
    )(flag(lax.axis_index("dp")), shard, across)


def stack_kernel(*refs):
    for n, ref in enumerate(refs[:-1]):
        refs[-1][n] = ref[...]


def stacked(parts):
    shape = (len(parts),) + parts[0].shape
    return pl.pallas_call(
        stack_kernel,
        grid=(1,),
        in_specs=[whole(p.shape) for p in parts],
        out_specs=whole(shape),
        out_shape=jax.ShapeDtypeStruct(shape, parts[0].dtype),
        name="stacked",
        cost_estimate=cost(),
    )(*parts)


def sort_kernel(*refs):
    parts, (mine_ref, away_ref) = refs[:-2], refs[-2:]
    for n, ref in enumerate(parts):
        mine_ref[n] = ref[0]
        away_ref[n] = ref[1]


def sort_groups(parts):
    shape = (len(parts),) + parts[0].shape[1:]
    return pl.pallas_call(
        sort_kernel,
        grid=(1,),
        in_specs=[whole(p.shape) for p in parts],
        out_specs=[whole(shape)] * 2,
        out_shape=[jax.ShapeDtypeStruct(shape, parts[0].dtype)] * 2,
        name="sort_groups",
        cost_estimate=cost(),
    )(*parts)


def add_kernel(near_ref, away_ref, out_ref):
    out_ref[...] = (near_ref[...] + away_ref[...].astype(F32)).astype(BF)


def add_halves(near, away):
    part = pl.BlockSpec((1,) + near.shape[1:], lambda i: (i, 0, 0))
    return pl.pallas_call(
        add_kernel,
        grid=(near.shape[0],),
        in_specs=[part, part],
        out_specs=part,
        out_shape=jax.ShapeDtypeStruct(near.shape, BF),
        name="add_halves",
        cost_estimate=cost(),
    )(near, away)


def vector_kernel(narrow_ref, out_ref, *, start):
    row = lax.broadcasted_iota(jnp.int32, (8, LANES), 0)
    lane = lax.broadcasted_iota(jnp.int32, (8, LANES), 1)
    wanted = jnp.where((lane == row + start) & (row < 4), 1.0, 0.0).astype(BF)
    out_ref[...] = dot_nt(wanted, narrow_ref[...])


def vectors_of(narrow, start):
    return pl.pallas_call(
        functools.partial(vector_kernel, start=start),
        grid=(1,),
        in_specs=[whole(narrow.shape)],
        out_specs=whole((8, D)),
        out_shape=jax.ShapeDtypeStruct((8, D), F32),
        name="vectors",
        cost_estimate=cost(),
    )(narrow)


def assemble_kernel(here_ref, same_ref, flip_ref, *out_refs):
    chips, _, rows, _ = same_ref.shape
    for chip in range(chips):
        for b, ref in enumerate((same_ref, flip_ref)):
            place = here_ref[0] ^ (2 * chip + b)
            for d in range(2):
                at = pl.ds(pl.multiple_of((d * 2 * chips + place) * rows, 16), rows)
                lo = 0
                for out_ref in out_refs:
                    out_ref[at, :] = ref[chip, d, :, lo : lo + out_ref.shape[1]]
                    lo += out_ref.shape[1]


def assemble(same, flipped, widths):
    chips, _, rows, columns = same.shape
    here = lax.axis_index("expert").astype(jnp.int32)
    if rows % 16 == 0:
        return pl.pallas_call(
            assemble_kernel,
            grid_spec=pltpu.PrefetchScalarGridSpec(
                num_scalar_prefetch=1,
                grid=(1,),
                in_specs=[whole(same.shape), whole(same.shape)],
                out_specs=[whole((4 * chips * rows, w)) for w in widths],
            ),
            out_shape=[jax.ShapeDtypeStruct((4 * chips * rows, w), same.dtype) for w in widths],
            name="assemble",
            cost_estimate=cost(),
        )(here.reshape(1), same, flipped)
    buffer = jnp.zeros((2, 2 * chips, rows, columns), same.dtype)
    for j in range(chips):
        for b, both in enumerate((same, flipped)):
            buffer = lax.dynamic_update_slice(buffer, both[j][:, None], (0, here ^ (2 * j + b), 0, 0))
    buffer = buffer.reshape(-1, columns)
    cuts = [sum(widths[:n]) for n in range(len(widths) + 1)]
    return [buffer[:, cuts[n] : cuts[n + 1]] for n in range(len(widths))]


def chip_copies(pair):
    count = lax.axis_size("expert")
    return [pair] + [hop(pair, "expert", k) for k in range(2, count, 2)]


def pick(array, index, axis):
    return lax.dynamic_index_in_dim(array, index, axis, False)


def chip_sum(total, wide):
    here_dp = lax.axis_index("dp")
    chip = lax.axis_index("expert") >> 1
    summed = pick(total, chip, 1)
    for k in range(1, total.shape[1]):
        summed = summed + hop(pick(total, chip ^ k, 1).astype(wide), "expert", 2 * k).astype(F32)
    return pick(summed, here_dp, 0), pick(summed, 1 - here_dp, 0).astype(wide)


def normed(values):
    average = jnp.mean(values, axis=-1, keepdims=True)
    centred = values - average
    variance = jnp.mean(centred * centred, axis=-1, keepdims=True)
    scale = lax.rsqrt(variance + EPSILON)
    return centred * scale, scale


def attend_kernel(x_ref, vec_ref, w_ref, *refs):
    a_ref, qkv_ref, o_ref, lse_ref, part_ref = refs[-5:]
    hat, _ = normed(x_ref[0].astype(F32))
    a = (hat * vec_ref[0:1, :] + vec_ref[1:2, :]).astype(BF)
    a_ref[0] = a
    qkv_ref[0] = dot_nn(a, w_ref[...]).astype(BF)
    keys_in = lax.broadcasted_iota(jnp.int32, (ROWS, ROWS), 1) < SEQ
    lane = lax.broadcasted_iota(jnp.int32, (ROWS, LANES), 1)
    lse = jnp.zeros((ROWS, LANES), F32)
    for h in range(HALF // HEAD):
        at = h * HEAD
        q = qkv_ref[0, :, at : at + HEAD]
        k = qkv_ref[0, :, HALF + at : HALF + at + HEAD]
        v = qkv_ref[0, :, 2 * HALF + at : 2 * HALF + at + HEAD]
        s = jnp.where(keys_in, dot_nt(q, k) * SCALE, -1e30)
        top = jnp.max(s, axis=1, keepdims=True)
        total = top + jnp.log(jnp.sum(jnp.exp(s - top), axis=1, keepdims=True))
        weights = jnp.exp(s - total).astype(BF)
        part_ref[0, :, at : at + HEAD] = dot_nn(weights, v).astype(BF)
        lse = jnp.where(lane == h, total, lse)
    lse_ref[0] = lse
    o_ref[0] = part_ref[0]


def attend(x, vectors, weight, lo, hi, held):
    total = x.shape[0]
    return pl.pallas_call(
        attend_kernel,
        grid=(hi - lo,),
        in_specs=[image(D, lo), whole(vectors.shape), whole(weight.shape)] + [ANY] * len(held),
        out_specs=[image(D, lo), image(3 * HALF, lo), image(HALF, lo), image(LANES, lo), image(HALF)],
        out_shape=[
            images(total, D, BF),
            images(total, 3 * HALF, BF),
            images(total, HALF, BF),
            images(total, LANES, F32),
            images(hi - lo, HALF, BF),
        ],
        input_output_aliases={3 + n: n for n in range(len(held))},
        name="attend",
        cost_estimate=cost(),
    )(x, vectors, weight, *held)


def route_kernel(
    which_ref, x_ref, own_ref, got_ref, vec_ref, here_ref, there_ref, router_ref, ids_ref, *refs, count
):
    y_ref, r_ref, g_ref, h_ref = refs[-4:]
    y = x_ref[0].astype(F32) + (
        dot_nt(own_ref[0], here_ref[...]) + dot_nt(got_ref[0], there_ref[...])
    )
    y_ref[0] = y
    hat, _ = normed(y)
    h = (hat * vec_ref[2:3, :] + vec_ref[3:4, :]).astype(BF)
    first = which_ref[0] == 0
    h_ref[0, :, :HALF] = jnp.where(first, h[:, :HALF], h[:, HALF:])
    h_ref[0, :, HALF:] = jnp.where(first, h[:, HALF:], h[:, :HALF])
    lane = lax.broadcasted_iota(jnp.int32, (ROWS, LANES), 1)
    logits = jnp.where(lane < count, dot_nn(h, router_ref[...]), -1e30)
    logits = jnp.exp(logits - jnp.max(logits, axis=1, keepdims=True))
    probs = logits / jnp.sum(logits, axis=1, keepdims=True)
    r_ref[0] = probs
    gates = jnp.zeros((ROWS, LANES), F32)
    for c in range(2):
        gate = jnp.sum(jnp.where(lane == ids_ref[0, :, c : c + 1], probs, 0.0), axis=1, keepdims=True)
        gates = jnp.where(lane == c, gate, gates)
    g_ref[0] = gates


def route(which, x, own, got, vectors, out_here, out_there, router, ids, count, lo, hi, held):
    total = x.shape[0]
    return pl.pallas_call(
        functools.partial(route_kernel, count=count),
        grid_spec=pltpu.PrefetchScalarGridSpec(
            num_scalar_prefetch=1,
            grid=(hi - lo,),
            in_specs=[
                image(D, lo),
                image(HALF),
                image(HALF),
                whole(vectors.shape),
                whole(out_here.shape),
                whole(out_there.shape),
                whole(router.shape),
                image(2, lo),
            ]
            + [ANY] * len(held),
            out_specs=[image(D, lo), image(LANES, lo), image(LANES, lo), image(D)],
        ),
        out_shape=[
            images(total, D, F32),
            images(total, LANES, F32),
            images(total, LANES, F32),
            images(hi - lo, D, BF),
        ],
        input_output_aliases={9 + n: n for n in range(len(held))},
        name="route",
        cost_estimate=cost(),
    )(which, x, own, got, vectors, out_here, out_there, router, ids, *held)


def send_kernel(*refs, parts, chips, gated):
    per = 3 if gated else 2
    groups = [refs[n * per * parts : (n + 1) * per * parts] for n in range(2)]
    out_refs = refs[2 * per * parts :]
    capacity = out_refs[0].shape[1]
    for out_ref, chip in zip(out_refs, chips):
        for r in range(2):
            rows, values, gates = (groups[r][n * parts : (n + 1) * parts] for n in range(3))
            places = lax.broadcasted_iota(jnp.int32, (capacity, 1), 0) + (2 * chip + r) * capacity
            picked = jnp.zeros((capacity, D), F32)
            weight = jnp.zeros((capacity, 1), F32)
            for n in range(parts):
                first = places == rows[n][0:1, :]
                second = places == rows[n][1:2, :]
                chosen = jnp.where(first | second, 1.0, 0.0).astype(BF)
                picked = picked + dot_nn(chosen, values[n][...])
                if gated:
                    each = jnp.where(
                        first, gates[n][0:1, :], jnp.where(second, gates[n][1:2, :], 0.0)
                    )
                    weight = weight + jnp.sum(each, axis=1, keepdims=True)
            if gated:
                picked = picked * weight
            out_ref[r] = picked.astype(BF)


def send_rows(own, other, capacity, chips, gated):
    operands = [part for group in (own, other) for kind in group for part in kind]
    return pl.pallas_call(
        functools.partial(send_kernel, parts=len(own[0]), chips=chips, gated=gated),
        grid=(1,),
        in_specs=[whole(o.shape) for o in operands],
        out_specs=[whole((2, capacity, D))] * len(chips),
        out_shape=[jax.ShapeDtypeStruct((2, capacity, D), BF)] * len(chips),
        name="send_gated" if gated else "send_rows",
        cost_estimate=cost(),
    )(*operands)


def first_lanes():
    row = lax.broadcasted_iota(jnp.int32, (8, LANES), 0)
    return jnp.where(row == lax.broadcasted_iota(jnp.int32, (8, LANES), 1), 1.0, 0.0)


def turn(columns):
    return lax.dot_general(
        first_lanes(), columns, (((1,), (1,)), ((), ())), precision=HIGH, preferred_element_type=F32
    )


def turn_back(rows):
    return lax.dot_general(
        rows, first_lanes(), (((0,), (0,)), ((), ())), precision=HIGH, preferred_element_type=F32
    )


def home_kernel(which_ref, rows_ref, middle_ref, grad_ref, gates_ref, own_ref, other_ref, out_ref, dgate_ref):
    value = middle_ref[0]
    grad = grad_ref[0].astype(F32)
    lane = lax.broadcasted_iota(jnp.int32, (ROWS, LANES), 1)
    found = jnp.zeros((ROWS, LANES), F32)
    chips, capacity = own_ref.shape[:2]
    places = lax.broadcasted_iota(jnp.int32, (1, capacity), 1)
    for c in range(2):
        picked = jnp.zeros((ROWS, HALF), F32)
        for chip in range(chips):
            for r, back_ref in enumerate((own_ref, other_ref)):
                at = rows_ref[0, :, c : c + 1] - (2 * chip + r) * capacity
                chosen = jnp.where(at == places, 1.0, 0.0)
                picked = picked + dot_nn(chosen.astype(BF), back_ref[chip])
        value = value + gates_ref[0, :, c : c + 1] * picked
        dgate = jnp.sum(picked * grad, axis=1, keepdims=True)
        found = jnp.where(lane == c, dgate, found)
    out_ref[0] = value.astype(BF)
    dgate_ref[0] = turn(found)


def bring_home(which, rows, middle, grad, gates, own, other):
    total = middle.shape[0]
    part = pl.BlockSpec((1, ROWS, HALF), lambda i, s: (i, 0, s[0]))
    return pl.pallas_call(
        home_kernel,
        grid_spec=pltpu.PrefetchScalarGridSpec(
            num_scalar_prefetch=1,
            grid=(total,),
            in_specs=[image(2), part, part, image(LANES), whole(own.shape), whole(other.shape)],
            out_specs=[image(HALF), pl.BlockSpec((1, 8, ROWS), lambda i, s: (i, 0, 0))],
        ),
        out_shape=[images(total, HALF, BF), jax.ShapeDtypeStruct((total, 8, ROWS), F32)],
        name="bring_home",
        cost_estimate=cost(),
    )(which, rows, middle, grad, gates, own, other)


def sum_kernel(rows_ref, own_ref, other_ref, out_ref):
    chips, capacity = own_ref.shape[:2]
    places = lax.broadcasted_iota(jnp.int32, (1, capacity), 1)
    total = jnp.zeros((ROWS, HALF), F32)
    for chip in range(chips):
        for r, back_ref in enumerate((own_ref, other_ref)):
            base = (2 * chip + r) * capacity
            chosen = (rows_ref[0, :, 0:1] - base == places) | (rows_ref[0, :, 1:2] - base == places)
            total = total + dot_nn(jnp.where(chosen, 1.0, 0.0).astype(BF), back_ref[chip])
    out_ref[0] = total.astype(BF)


def sum_home(rows, own, other, lo, hi):
    return pl.pallas_call(
        sum_kernel,
        grid=(hi - lo,),
        in_specs=[image(2, lo), whole(own.shape), whole(other.shape)],
        out_specs=image(HALF),
        out_shape=images(hi - lo, HALF, BF),
        name="sum_home",
        cost_estimate=cost(),
    )(rows, own, other)


def gelu_parts(u):
    size = jnp.abs(u)
    t = 1.0 / (1.0 + TAIL_RATE * size)
    poly = jnp.full_like(t, TAIL[-1])
    for c in TAIL[-2::-1]:
        poly = poly * t + c
    bell = jnp.exp(-0.5 * (u * u))
    tail = bell * (t * poly)
    normal = jnp.where(u >= 0.0, 1.0 - tail, tail)
    return u * normal, normal + u * (DENSITY * bell)


def in_order(same_ref, refs):
    same = same_ref[0] == 1
    n, m = len(IN_CUTS), len(BACK_CUTS)
    join = lambda refs, axis: jnp.concatenate([ref[...] for ref in refs], axis=axis)
    pairs = [
        (join(refs[:n], 0), join(refs[n : 2 * n], 0)),
        (join(refs[2 * n : 2 * n + m], 1), join(refs[2 * n + m :], 1)),
    ]
    return [v for a, b in pairs for v in (jnp.where(same, a, b), jnp.where(same, b, a))]


def weight_specs():
    across = [pl.BlockSpec((hi - lo, TILE), lambda i, s: (0, i)) for lo, hi in IN_CUTS]
    down = [pl.BlockSpec((TILE, hi - lo), lambda i, s: (i, 0)) for lo, hi in BACK_CUTS]
    return across * 2 + down * 2


def forward_kernel(same_ref, m_ref, *refs):
    *weights, g_ref, s_ref, zt_ref, zh_ref, acc = refs
    w1h, w1t, w2h, w2t = in_order(same_ref, weights)
    step = pl.program_id(0)
    last = pl.num_programs(0) - 1
    for b in range(m_ref.shape[0]):
        u = dot_nn(m_ref[b, :, :HALF], w1h) + dot_nn(m_ref[b, :, HALF:], w1t)
        g, slope = gelu_parts(u)
        g = g.astype(BF)
        g_ref[b] = g
        s_ref[b] = slope.astype(BF)
        away = dot_nn(g, w2t)
        near = dot_nn(g, w2h)

        @pl.when(step == 0)
        def _():
            acc[b] = away
            zh_ref[b] = near

        @pl.when(step > 0)
        def _():
            acc[b] += away
            zh_ref[b] += near

        @pl.when(step == last)
        def _():
            zt_ref[b] = acc[b].astype(BF)


def expert_forward(same, rows, *weights):
    blocks, capacity, _ = rows.shape
    hidden = weights[0].shape[1]
    wide = pl.BlockSpec((blocks, capacity, TILE), lambda i, s: (0, 0, i))
    make = lambda w, t: jax.ShapeDtypeStruct((blocks, capacity, w), t)
    return pl.pallas_call(
        forward_kernel,
        grid_spec=pltpu.PrefetchScalarGridSpec(
            num_scalar_prefetch=1,
            grid=(hidden // TILE,),
            in_specs=[whole(rows.shape)] + weight_specs(),
            out_specs=[wide, wide] + [whole((blocks, capacity, HALF))] * 2,
            scratch_shapes=[pltpu.VMEM((blocks, capacity, HALF), F32)],
        ),
        out_shape=[make(hidden, BF), make(hidden, BF), make(HALF, BF), make(HALF, F32)],
        name="expert_forward",
        cost_estimate=cost(),
    )(same, rows, *weights)


def backward_kernel(same_ref, z_ref, s_ref, *refs):
    *weights, u_ref, mt_ref, mh_ref, acc = refs
    w1h, w1t, w2h, w2t = in_order(same_ref, weights)
    step = pl.program_id(0)
    last = pl.num_programs(0) - 1
    for b in range(z_ref.shape[0]):
        grad = dot_nt(z_ref[b, :, :HALF], w2h) + dot_nt(z_ref[b, :, HALF:], w2t)
        grad = (grad * s_ref[b].astype(F32)).astype(BF)
        u_ref[b] = grad
        away = dot_nt(grad, w1t)
        near = dot_nt(grad, w1h)

        @pl.when(step == 0)
        def _():
            acc[b] = away
            mh_ref[b] = near

        @pl.when(step > 0)
        def _():
            acc[b] += away
            mh_ref[b] += near

        @pl.when(step == last)
        def _():
            mt_ref[b] = acc[b].astype(BF)


def expert_backward(same, rows, slope, *weights):
    blocks, capacity, _ = rows.shape
    hidden = weights[0].shape[1]
    wide = pl.BlockSpec((blocks, capacity, TILE), lambda i, s: (0, 0, i))
    make = lambda w, t: jax.ShapeDtypeStruct((blocks, capacity, w), t)
    return pl.pallas_call(
        backward_kernel,
        grid_spec=pltpu.PrefetchScalarGridSpec(
            num_scalar_prefetch=1,
            grid=(hidden // TILE,),
            in_specs=[whole(rows.shape), wide] + weight_specs(),
            out_specs=[wide] + [whole((blocks, capacity, HALF))] * 2,
            scratch_shapes=[pltpu.VMEM((blocks, capacity, HALF), F32)],
        ),
        out_shape=[make(hidden, BF), make(HALF, BF), make(HALF, F32)],
        name="expert_backward",
        cost_estimate=cost(),
    )(same, rows, slope, *weights)


def outer_kernel(which_ref, *refs, chunks, hidden_first, added):
    step = pl.program_id(0)
    wides = refs[:chunks]
    narrows = refs[chunks : 2 * chunks]
    out_ref = refs[-1]
    total = None
    for wide_ref, slim_ref in zip(wides, narrows):
        for b in range(wide_ref.shape[0]):
            slim = slim_ref[b]
            term = dot_tn(wide_ref[b], slim) if hidden_first else dot_tn(slim, wide_ref[b])
            total = term if total is None else total + term
    if added == 1:
        total = total + refs[-2][...].astype(F32)
    elif added == 2:
        total = total + jnp.where(step == 0, refs[-3][...], refs[-2][...]).astype(F32)
    out_ref[...] = total.astype(out_ref.dtype)


def outer(which, wides, narrows, hidden_first, extra=None):
    per, capacity, hidden = wides[0].shape
    slim = pl.BlockSpec((per, capacity, HALF), lambda i, s: (0, 0, s[0]))
    if hidden_first:
        shape, out = (hidden, HALF), pl.BlockSpec((TILE, HALF), lambda i, s: (i, 0))
    else:
        shape, out = (HALF, hidden), pl.BlockSpec((HALF, TILE), lambda i, s: (0, i))
    specs = [pl.BlockSpec((per, capacity, TILE), lambda i, s: (0, 0, i))] * len(wides)
    specs += [slim] * len(narrows)
    operands = list(wides) + list(narrows)
    extra = [] if extra is None else list(extra)
    if len(extra) == 1:
        specs.append(out)
    elif len(extra) == 2:
        specs.append(pl.BlockSpec((TILE, HALF), lambda i, s: (0, 0)))
        specs.append(pl.BlockSpec((TILE, HALF), lambda i, s: (jnp.maximum(i - 1, 0), 0)))
    operands += extra
    return pl.pallas_call(
        functools.partial(
            outer_kernel,
            chunks=len(wides),
            hidden_first=hidden_first,
            added=len(extra),
        ),
        grid_spec=pltpu.PrefetchScalarGridSpec(
            num_scalar_prefetch=1, grid=(hidden // TILE,), in_specs=specs, out_specs=out
        ),
        out_shape=jax.ShapeDtypeStruct(shape, F32 if extra else BF),
        name="outer_keep" if extra else "outer_send",
        cost_estimate=cost(),
    )(which, *operands)


def norm_back(grad, hat, scale, gain):
    inner = grad * gain
    return scale * (
        inner
        - jnp.mean(inner, axis=-1, keepdims=True)
        - hat * jnp.mean(inner * hat, axis=-1, keepdims=True)
    )


def add_sums(ref, grad, hat, first):
    sums = [jnp.sum(grad * hat, axis=0, keepdims=True), jnp.sum(grad, axis=0, keepdims=True)]

    @pl.when(first)
    def _():
        ref[...] = jnp.zeros_like(ref)

    ref[0:1, :] += sums[0]
    ref[1:2, :] += sums[1]


def attend_back_kernel(
    which_ref,
    x_ref,
    y_ref,
    near_ref,
    away_ref,
    dgate_ref,
    dgate2_ref,
    probs_ref,
    ids_ref,
    narrow_ref,
    cot_ref,
    vec_ref,
    out_w_ref,
    qkv_ref,
    lse_ref,
    w_ref,
    *refs,
):
    dy_ref, dyb_ref, dqkv_ref, part_ref, sums2_ref, sums1_ref, router_ref, att_ref = refs[-8:]
    first = which_ref[0] == 0
    start = pl.program_id(0) == 0
    near = near_ref[0].astype(F32)
    away = away_ref[0].astype(F32)
    dgate = turn_back(dgate_ref[0] + dgate2_ref[0])
    lane = lax.broadcasted_iota(jnp.int32, (ROWS, LANES), 1)
    probs = probs_ref[0]
    grad_probs = sum(
        jnp.where(lane == ids_ref[0, :, c : c + 1], dgate[:, c : c + 1], 0.0) for c in range(2)
    )
    grad_logits = probs * (grad_probs - jnp.sum(probs * grad_probs, axis=1, keepdims=True))
    high = grad_logits.astype(BF)
    low = (grad_logits - high.astype(F32)).astype(BF)
    narrow = narrow_ref[...]
    grad = (dot_nt(high, narrow) + dot_nt(low, narrow)) + jnp.concatenate(
        [jnp.where(first, near, away), jnp.where(first, away, near)], axis=1
    )
    hat, scale = normed(y_ref[0])
    h = (hat * vec_ref[2:3, :] + vec_ref[3:4, :]).astype(BF)
    grad_router = dot_tn(high, h) + dot_tn(low, h)

    @pl.when(start)
    def _():
        router_ref[...] = grad_router

    @pl.when(jnp.logical_not(start))
    def _():
        router_ref[...] += grad_router

    add_sums(sums2_ref, grad, hat, start)
    dy = cot_ref[0].astype(F32) + norm_back(grad, hat, scale, vec_ref[2:3, :])
    dy_ref[0] = dy
    dyb = dy.astype(BF)
    dyb_ref[0] = dyb
    att_ref[...] = dot_nn(dyb, out_w_ref[...]).astype(BF)
    keys_in = lax.broadcasted_iota(jnp.int32, (ROWS, ROWS), 1) < SEQ
    for h in range(HALF // HEAD):
        at = h * HEAD
        q = qkv_ref[0, :, at : at + HEAD]
        k = qkv_ref[0, :, HALF + at : HALF + at + HEAD]
        v = qkv_ref[0, :, 2 * HALF + at : 2 * HALF + at + HEAD]
        do = att_ref[:, at : at + HEAD]
        s = jnp.where(keys_in, dot_nt(q, k) * SCALE, -1e30)
        weights = jnp.exp(s - lse_ref[0, :, h : h + 1])
        dv = dot_tn(weights.astype(BF), do)
        dp = dot_nt(do, v)
        ds = (weights * (dp - jnp.sum(weights * dp, axis=1, keepdims=True))).astype(BF)
        dqkv_ref[0, :, at : at + HEAD] = (dot_nn(ds, k) * SCALE).astype(BF)
        dqkv_ref[0, :, HALF + at : HALF + at + HEAD] = (dot_tn(ds, q) * SCALE).astype(BF)
        dqkv_ref[0, :, 2 * HALF + at : 2 * HALF + at + HEAD] = dv.astype(BF)
    part = dot_nt(dqkv_ref[0], w_ref[...])
    part_ref[0] = part.astype(BF)
    hat, _ = normed(x_ref[0].astype(F32))
    add_sums(sums1_ref, part, hat, start)


def attend_back(which, x, y, near, away, dgate, dgate2, probs, ids, narrow, cot, vectors, out_w, qkv, lse, weight, lo, hi, held):
    total = y.shape[0]
    turned = pl.BlockSpec((1, 8, ROWS), lambda i, s: (i + lo, 0, 0))
    return pl.pallas_call(
        attend_back_kernel,
        grid_spec=pltpu.PrefetchScalarGridSpec(
            num_scalar_prefetch=1,
            grid=(hi - lo,),
            in_specs=[
                image(D, lo),
                image(D, lo),
                image(HALF, lo),
                image(HALF, lo),
                turned,
                turned,
                image(LANES, lo),
                image(2, lo),
                whole(narrow.shape),
                image(D, lo),
                whole(vectors.shape),
                whole(out_w.shape),
                image(3 * HALF, lo),
                image(LANES, lo),
                whole(weight.shape),
            ]
            + [ANY] * len(held),
            out_specs=[
                image(D, lo),
                image(D, lo),
                image(3 * HALF, lo),
                image(D),
                whole((8, D)),
                whole((8, D)),
                whole((LANES, D)),
            ],
            scratch_shapes=[pltpu.VMEM((ROWS, HALF), BF)],
        ),
        out_shape=[
            images(total, D, F32),
            images(total, D, BF),
            images(total, 3 * HALF, BF),
            images(hi - lo, D, BF),
            jax.ShapeDtypeStruct((8, D), F32),
            jax.ShapeDtypeStruct((8, D), F32),
            jax.ShapeDtypeStruct((LANES, D), F32),
        ],
        input_output_aliases={16 + n: n for n in range(len(held))},
        name="attend_back",
        cost_estimate=cost(),
    )(which, x, y, near, away, dgate, dgate2, probs, ids, narrow, cot, vectors, out_w, qkv, lse, weight, *held)


def token_kernel(x_ref, own_ref, got_ref, dy_ref, vec_ref, *refs):
    out_ref = refs[-1]
    grad = own_ref[0].astype(F32) + got_ref[0].astype(F32)
    hat, scale = normed(x_ref[0].astype(F32))
    out_ref[0] = dy_ref[0] + norm_back(grad, hat, scale, vec_ref[0:1, :])


def token_back(x, own, got, dy, vectors, lo, hi, held):
    total = x.shape[0]
    return pl.pallas_call(
        token_kernel,
        grid=(hi - lo,),
        in_specs=[image(D, lo), image(D), image(D), image(D, lo), whole(vectors.shape)]
        + [ANY] * len(held),
        out_specs=image(D, lo),
        out_shape=images(total, D, F32),
        input_output_aliases={5 + n: n for n in range(len(held))},
        name="token_back",
        cost_estimate=cost(),
    )(x, own, got, dy, vectors, *held)


def exact(a, b, contract):
    return lax.dot_general(
        a, b, ((contract[:1], contract[1:]), ((), ())), precision=HIGH, preferred_element_type=F32
    )


def of_image(i, tok):
    row = lax.broadcasted_iota(jnp.int32, (ROWS, tok), 0)
    token = lax.broadcasted_iota(jnp.int32, (ROWS, tok), 1)
    return jnp.where((token == row + i * SEQ) & (row < SEQ), 1.0, 0.0)


def image_kernel(which_ref, tok_ref, cot_ref, x_ref, cot_out_ref, here_ref):
    mine = of_image(pl.program_id(0), tok_ref.shape[0]).astype(BF)
    x_ref[0] = dot_nn(mine, tok_ref[...]).astype(BF)
    cot = dot_nn(mine, cot_ref[...]).astype(BF)
    cot_out_ref[0] = cot
    first = which_ref[0] == 0
    here_ref[0, :, :HALF] = jnp.where(first, cot[:, :HALF], cot[:, HALF:])
    here_ref[0, :, HALF:] = jnp.where(first, cot[:, HALF:], cot[:, :HALF])


def image_rows(which, tokens, cotangent):
    pictures = tokens.shape[0] // SEQ
    return pl.pallas_call(
        image_kernel,
        grid_spec=pltpu.PrefetchScalarGridSpec(
            num_scalar_prefetch=1,
            grid=(pictures,),
            in_specs=[whole(tokens.shape)] * 2,
            out_specs=[image(D)] * 3,
        ),
        out_shape=[images(pictures, D, BF)] * 3,
        name="image_rows",
        cost_estimate=cost(),
    )(which, tokens, cotangent)


def slot_kernel(here_ref, ids_ref, rows_ref, lanes_ref, ids_out_ref, *, capacity):
    tok = ids_ref.shape[0]
    lane = lax.broadcasted_iota(jnp.int32, (tok, LANES), 1)
    earlier = jnp.where(
        lax.broadcasted_iota(jnp.int32, (tok, tok), 1) < lax.broadcasted_iota(jnp.int32, (tok, tok), 0),
        1.0, 0.0,
    ).astype(BF)
    ids = [ids_ref[:, c : c + 1] for c in range(2)]
    taken = jnp.zeros((1, LANES), F32)
    table = jnp.zeros((tok, LANES), F32)
    for c in range(2):
        onehot = jnp.where(lane == ids[c], 1.0, 0.0)
        before = dot_nn(earlier, onehot.astype(BF)) + taken
        slot = jnp.sum(before * onehot, axis=1, keepdims=True)
        taken = taken + jnp.sum(onehot, axis=0, keepdims=True)
        place = ((ids[c] ^ here_ref[0]) * capacity).astype(F32) + slot + 1.0
        table = jnp.where(lane == c, place, table)
        table = jnp.where(lane == 2 + c, ids[c].astype(F32) + 1.0, table)
    for i in range(rows_ref.shape[0]):
        part = exact(of_image(i, tok), table, (1, 0)) - 1.0
        whole_part = part.astype(jnp.int32)
        rows_ref[i] = whole_part[:, 0:2]
        ids_out_ref[i] = whole_part[:, 2:4]
        lanes_ref[:, i * ROWS : (i + 1) * ROWS] = exact(first_lanes(), part, (1, 1)).astype(jnp.int32)


def slot_rows(here, expert_ids, capacity):
    tok = expert_ids.shape[0]
    pictures = tok // SEQ
    shapes = [(pictures, ROWS, 2), (8, pictures * ROWS), (pictures, ROWS, 2)]
    rows, lanes, ids = pl.pallas_call(
        functools.partial(slot_kernel, capacity=capacity),
        grid_spec=pltpu.PrefetchScalarGridSpec(
            num_scalar_prefetch=1,
            grid=(1,),
            in_specs=[whole(expert_ids.shape)],
            out_specs=[whole(shape) for shape in shapes],
        ),
        out_shape=[jax.ShapeDtypeStruct(shape, jnp.int32) for shape in shapes],
        name="slot_rows",
        cost_estimate=cost(),
    )(flag(here), expert_ids)
    return rows, lanes, ids


def projection_kernel(core_ref, *refs, parts, split):
    a_ref, dqkv_ref, dyb_ref, o_ref = refs[:4]
    routers, ones, twos = (refs[4 + n * parts : 4 + (n + 1) * parts] for n in range(3))
    out_ref = refs[-1]
    step = pl.program_id(0)
    last = pl.num_programs(0) - 1
    qkv = dot_tn(a_ref[0], dqkv_ref[0])
    out = dot_tn(dyb_ref[0], o_ref[0])

    @pl.when(step == 0)
    def _():
        out_ref[:, : 3 * HALF] = qkv
        out_ref[:, 3 * HALF : 4 * HALF] = out
        total = 0.5 * sum(r[...] for r in routers)
        sums = jnp.concatenate(
            [sum(r[0:2, :] for r in ones), 0.5 * sum(r[0:2, :] for r in twos), jnp.zeros((4, D), F32)],
            axis=0,
        )
        out_ref[:, 4 * HALF :] = jnp.transpose(
            jnp.concatenate([total[: LANES - 8], sums], axis=0)
        )

    @pl.when(step > 0)
    def _():
        out_ref[:, : 3 * HALF] += qkv
        out_ref[:, 3 * HALF : 4 * HALF] += out

    if split:

        @pl.when(step == last)
        def _():
            near_ref, away_ref = refs[-3:-1]
            dps, chips, rows, _ = near_ref.shape
            for d in range(dps):
                for chip in range(chips):
                    at = (2 * (d * chips + chip) + core_ref[0]) * rows
                    near_ref[d, chip] = out_ref[pl.ds(pl.multiple_of(at, 16), rows), :]
                    at = (2 * (d * chips + chip) + 1 - core_ref[0]) * rows
                    away = out_ref[pl.ds(pl.multiple_of(at, 16), rows), :]
                    away_ref[d, chip] = away.astype(BF)


def projection_grads(a_rows, dqkv, dyb, o_rows, *small):
    count = lax.axis_size("expert")
    core = lax.axis_index("expert") & 1
    rows = D // (2 * count)
    split = rows % 16 == 0
    shape = (D, 4 * HALF + LANES)
    shares = (2, count // 2, rows, shape[1])
    kinds = [(shares, F32), (shares, BF)] if split else [(shape, F32)]
    out = pl.pallas_call(
        functools.partial(projection_kernel, parts=len(small) // 3, split=split),
        grid_spec=pltpu.PrefetchScalarGridSpec(
            num_scalar_prefetch=1,
            grid=(a_rows.shape[0],),
            in_specs=[image(D), image(3 * HALF), image(D), image(HALF)]
            + [whole(v.shape) for v in small],
            out_specs=[whole(k) for k, _ in kinds],
            scratch_shapes=[pltpu.VMEM(shape, F32)] if split else [],
        ),
        out_shape=[jax.ShapeDtypeStruct(*kind) for kind in kinds],
        name="projection_grads",
        cost_estimate=cost(),
    )(flag(core), a_rows, dqkv, dyb, o_rows, *small)
    if split:
        return out
    blocks = out[0].reshape((2, count // 2, 2, rows, -1))
    return pick(blocks, core, 2), pick(blocks, 1 - core, 2).astype(BF)


def on_device(
    tokens,
    cotangent,
    ln1_gain,
    ln1_bias,
    ln2_gain,
    ln2_bias,
    w_query,
    w_key,
    w_value,
    w_out,
    w_router,
    w_in,
    w_back,
    expert_ids,
):
    count = lax.axis_size("expert")
    chips = count // 2
    tok = tokens.shape[0]
    capacity = (10 * tok + 32 * count - 1) // (32 * count) * 8
    pictures = tok // SEQ
    rows_all = pictures * ROWS
    cut = (pictures + 1) // 2
    groups = [(0, cut), (cut, pictures)] if pictures > 1 else [(0, pictures)]
    lanes_of = lambda value: [value[:, lo * ROWS : hi * ROWS] for lo, hi in groups]
    here = lax.axis_index("expert")
    here_dp = lax.axis_index("dp")
    here_t = lax.axis_index("tensor")
    which = here_t.astype(jnp.int32).reshape(1)
    same = here_t == here_dp

    order = Order()

    small = jnp.stack([ln1_gain, ln1_bias, ln2_gain, ln2_bias], axis=1)
    narrow = jnp.concatenate([w_router, small], axis=1)
    narrow = jnp.pad(narrow, ((0, 0), (0, LANES - narrow.shape[1])))
    first_pack = jnp.concatenate(
        [w_query, w_key, w_value, narrow, jnp.transpose(w_out)], axis=1
    ).astype(BF)
    pair = cross(first_pack)
    in_own = [follow(w_in, first_pack)[0, lo:hi].astype(BF) for lo, hi in IN_CUTS]
    back_own = [follow(w_back, first_pack)[0, :, lo:hi].astype(BF) for lo, hi in BACK_CUTS]
    pair, in_own, back_own = order.wait((pair, in_own, back_own))

    same_chips = stacked(chip_copies(order.after(pair)))
    in_other = [hop(order.after(in_own[0]), "dp", 1)]
    x, cot, cot_here = order.run(lambda *v: image_rows(which, *v), tokens, cotangent)
    cot_here = cot_here.reshape(rows_all, D)
    rows, rows_lanes, ids_pad = order.run(lambda v: slot_rows(here, v, capacity), expert_ids)
    same_chips, in_other[0] = order.wait((same_chips, in_other[0]))
    rows_lane = order.wait(rows_lanes[:2])
    in_other.append(hop(order.after(in_own[1]), "dp", 1))
    rows_next = hop(order.after(rows_lane), "expert", 1)
    cot_next = hop(order.after(cot_here), "expert", 1)
    flipped = order.wait(hop(order.after(same_chips), "expert", 1))
    qkv_w, narrow_all, out_here = order.run(
        lambda *v: assemble(*v, (3 * HALF, LANES, HALF)), same_chips, flipped
    )
    out_there = hop(order.after(out_here), "tensor", 1)
    vectors = order.run(lambda v: vectors_of(v, count), narrow_all)
    in_other[1] = order.wait(in_other[1])
    in_other.append(hop(order.after(in_own[2]), "dp", 1))
    back_other = [hop(order.after(back_own[0]), "dp", 1)]
    rows_next, cot_next = order.wait((rows_next, cot_next))
    own_lanes, next_lanes = order.wait((lanes_of(rows_lane), lanes_of(rows_next)))

    held, o_parts, got_parts = [], [], []
    for n, (lo, hi) in enumerate(groups):
        *held, o_part = order.run(
            lambda x, v, w, *h: attend(x, v, w, lo, hi, h), x, vectors, qkv_w, *held
        )
        o_parts.append(o_part)
        got_parts.append(hop(o_part, "tensor", 1))
    a_rows, qkv, o_rows, lse = held
    out_there = order.wait(out_there)
    got_parts, in_other[2], back_other[0] = order.wait((got_parts, in_other[2], back_other[0]))
    back_other.append(hop(order.after(back_own[1]), "dp", 1))
    held, h_parts, h_next = [], [], []
    for n, (lo, hi) in enumerate(groups):
        *held, h_part = order.run(
            lambda x, o, g, v, w, t, r, i, *h: route(which, x, o, g, v, w, t, r, i, count, lo, hi, h),
            x, o_parts[n], got_parts[n], vectors, out_here, out_there, narrow_all, ids_pad, *held,
        )
        h_parts.append(h_part.reshape(-1, D))
        if n == len(groups) - 1:
            gates_lane = jnp.transpose(held[2].reshape(rows_all, LANES)[:, :2])
            back_other[1], gates_lane = order.wait((back_other[1], gates_lane))
            h_parts[-1] = order.after(h_parts[-1])
            back_other.append(hop(order.after(back_own[2]), "dp", 1))
        h_next.append(hop(h_parts[-1], "expert", 1))
    y, probs, gates = held
    gates_next = hop(order.after(gates_lane), "expert", 1)

    own = (own_lanes, h_parts)
    other = (next_lanes, h_next)
    far = list(range(1, chips))
    outgoing = order.run(lambda *v: send_rows(*v, capacity, far, False), own, other)
    back_other[2] = order.wait(back_other[2])
    arrived = [None] + [hop(order.after(o), "expert", 2 * c) for o, c in zip(outgoing, far)]
    (arrived[0],) = order.run(lambda *v: send_rows(*v, capacity, [0], False), own, other)
    gates_next = order.wait(gates_next)
    own = ([rows_lane], [cot_here], [gates_lane])
    other = ([rows_next], [cot_next], [gates_next])
    grad_outgoing = order.run(lambda *v: send_rows(*v, capacity, far, True), own, other)
    grad_arrived = [None] * chips
    (grad_arrived[0],) = order.run(lambda *v: send_rows(*v, capacity, [0], True), own, other)
    weights = (*in_own, *in_other, *back_own, *back_other)
    same = flag(same)

    hidden, slopes, grads = [], [], []
    came_back, grad_home = [None] * chips, [None] * chips

    def back_to(chip, waiting):
        value = order.run(add_halves, *waiting)
        return hop(value, "expert", 2 * chip) if chip else value

    leaving = []

    def settle_oldest():
        home, chip, waiting = leaving.pop(0)
        home[chip] = back_to(chip, waiting)

    for c in range(chips):
        if c == 1:
            arrived[1:] = order.wait(arrived[1:])
            if chips <= 4:
                grad_arrived[1:] = [
                    hop(order.after(o), "expert", 2 * k) for o, k in zip(grad_outgoing, far)
                ]
        if c and chips > 4:
            grad_arrived[c] = hop(order.after(grad_outgoing[c - 1]), "expert", 2 * c)
        if c == chips - 1 and chips <= 4:
            grad_arrived[1:] = order.wait(grad_arrived[1:])
        g, s, zt, zh = order.run(lambda *v: expert_forward(same, *v), arrived[c], *weights)
        hidden.append(g)
        slopes.append(s)
        if len(leaving) > 1:
            settle_oldest()
        leaving.append((came_back, c, (zh, hop(order.after(zt), "tensor", 1))))
    for c in range(chips):
        if c and chips > 4:
            grad_arrived[c] = order.wait(grad_arrived[c])
        u, mt, mh = order.run(
            lambda *v: expert_backward(same, *v), grad_arrived[c], slopes[c], *weights
        )
        grads.append(u)
        settle_oldest()
        leaving.append((grad_home, c, (mh, hop(order.after(mt), "tensor", 1))))
        if c >= chips // 2:
            step = 2 * (chips - 1) // chips
            for k in range(1 + (c - chips // 2) * step, 1 + (c - chips // 2 + 1) * step):
                came_back[k] = order.wait(came_back[k])
    z_here, z_there = order.run(lambda *v: sort_groups(v), *order.wait(tuple(came_back)))
    z_there = hop(z_there, "expert", 1)
    send_half = same
    settle_oldest()
    back_send = order.run(lambda h, g: outer(send_half, h, g, True), hidden, grad_arrived)
    back_send = order.wait([back_send[:TILE], back_send[TILE:]])
    settle_oldest()
    back_got = [hop(order.after(back_send[0]), "dp", 1)]
    in_send = order.run(lambda g, a: outer(send_half, g, a, False), grads, arrived)
    grad_home = list(order.wait(tuple(grad_home)))
    m_here, m_there = order.run(lambda *v: sort_groups(v), *grad_home)
    back_got[0] = order.wait(back_got[0])
    back_got.append(hop(order.after(back_send[1]), "dp", 1))
    m_there = hop(order.after(m_there), "expert", 1)

    out_half, dgate = order.run(
        lambda *v: bring_home(which, *v), rows, y, cot, gates, z_here, z_there
    )
    dgate_next = hop(dgate, "tensor", 1)
    m_there = order.wait(m_there)
    near = order.run(lambda *v: sum_home(*v, 0, pictures), rows, m_here, m_there)
    away = hop(near, "tensor", 1)
    back_got, dgate_next = order.wait((back_got, dgate_next))
    in_got = hop(order.after(in_send), "dp", 1)
    away = order.wait(away)
    held, parts, sums, got = [], [], [], []
    for n, (lo, hi) in enumerate(groups):
        *held, part, sums2, sums1, grad_router = order.run(
            lambda *v: attend_back(which, *v[:15], lo, hi, v[15:]),
            x, y, near, away, dgate, dgate_next, probs, ids_pad, narrow_all, cot, vectors, out_here, qkv, lse, qkv_w, *held,
        )
        parts.append(part)
        got.append(hop(part, "tensor", 1))
        sums.append((grad_router, sums1, sums2))
    dy, dyb, dqkv = held

    routers, ones, twos = zip(*sums)
    total, total_away = order.run(
        projection_grads, a_rows, dqkv, dyb, o_rows, *routers, *ones, *twos
    )
    keep_half = 1 - send_half
    grad_back = order.run(
        lambda h, g, b: outer(keep_half, h, g, True, b), hidden, grad_arrived, back_got
    )[None]
    in_got, got[0] = order.wait((in_got, got[0]))
    total_got = hop(order.after(total_away), "expert", 1)
    grad_in = order.run(
        lambda g, a, b: outer(keep_half, g, a, False, [b]), grads, arrived, in_got
    )[None]
    total_got = order.wait(total_got)
    shards, leaving = chip_sum(order.wait(total + total_got.astype(F32)), BF)
    shards, leaving, got = order.wait((shards, leaving, got))
    entering = hop(leaving, "dp", 1)
    out_other = hop(order.after(out_half), "tensor", 1)
    grad_tokens = []
    for n, (lo, hi) in enumerate(groups):
        grad_tokens = [
            order.run(
                lambda *v: token_back(*v[:5], lo, hi, v[5:]),
                x, parts[n], got[n], dy, vectors, *grad_tokens,
            )
        ]
    shards, out_other = order.wait((shards + entering.astype(F32), out_other))
    tiny = shards[:, 4 * HALF :]
    tiny = tiny + hop(tiny, "tensor", 1)
    grad_tokens = grad_tokens[0][:, :SEQ].reshape(tok, D)
    block_out = jnp.where(
        here_t == 0,
        jnp.concatenate([out_half, out_other], axis=2),
        jnp.concatenate([out_other, out_half], axis=2),
    )
    block_out = block_out[:, :SEQ].reshape(tok, D)
    return (
        block_out,
        grad_tokens,
        tiny[:, LANES - 8],
        tiny[:, LANES - 7],
        tiny[:, LANES - 6],
        tiny[:, LANES - 5],
        shards[:, :HALF],
        shards[:, HALF : 2 * HALF],
        shards[:, 2 * HALF : 3 * HALF],
        jnp.transpose(shards[:, 3 * HALF : 4 * HALF]),
        tiny[:, :count],
        grad_in,
        grad_back,
    )


def solution(mesh):
    rows = ("dp", "expert")
    in_specs = (
        P(rows, None),
        P(rows, None),
        P(rows),
        P(rows),
        P(rows),
        P(rows),
        P(rows, "tensor"),
        P(rows, "tensor"),
        P(rows, "tensor"),
        P("tensor", rows),
        P(rows, None),
        P("expert", "dp", "tensor"),
        P("expert", "tensor", "dp"),
        P(rows, None),
    )
    out_specs = (
        P(rows, None),
        P(rows, None),
        P(rows),
        P(rows),
        P(rows),
        P(rows),
        P(rows, "tensor"),
        P(rows, "tensor"),
        P(rows, "tensor"),
        P("tensor", rows),
        P(rows, None),
        P("expert", "dp", "tensor"),
        P("expert", "tensor", "dp"),
    )
    return jax.shard_map(
        on_device, mesh=mesh, in_specs=in_specs, out_specs=out_specs, check_vma=False
    )
```

```python
import functools

import jax
import jax.numpy as jnp
from jax import lax
from jax.experimental import pallas as pl
from jax.experimental.pallas import tpu as pltpu
from jax.sharding import PartitionSpec as P

D = 768
HALF = 384
HEADS = 12
SEQ = 197
ROWS = 208
HEAD = D // HEADS
SCALE = HEAD ** (-0.5)
EPSILON = 1e-06
HIGH = lax.Precision.HIGHEST
BF = jnp.bfloat16
F32 = jnp.float32
LANES = 128
TILE = 512
IN_CUTS = ((0, 176), (176, 240), (240, 384))
BACK_CUTS = ((0, 128), (128, 256), (256, 384))
TAIL_RATE = 0.305
TAIL = (
    0.12163973686996697,
    0.12246675128071258,
    0.10342128505066615,
    0.12102026121907625,
    -0.03797407148483761,
    0.1857138128109823,
    -0.15298645906475614,
    0.03669873020693663,
)
DENSITY = 0.3989422804014327


def hop(value, axis, offset):
    count = lax.axis_size(axis)
    return lax.ppermute(value, axis, [(i, i ^ offset) for i in range(count)])


class Order:
    def __init__(self):
        self.token = lax.create_token()

    def after(self, value):
        return lax.optimization_barrier((self.token, value))[1]

    def wait(self, value):
        self.token, value = lax.optimization_barrier((self.token, value))
        return value

    def run(self, function, *operands):
        return self.wait(function(*self.after(operands)))


def follow(value, first):
    token = lax.optimization_barrier((lax.create_token(), first))[0]
    return lax.optimization_barrier((token, value))[1]


def dot_nn(a, b):
    return lax.dot_general(a, b, (((1,), (0,)), ((), ())), preferred_element_type=F32)


def dot_nt(a, b):
    return lax.dot_general(a, b, (((1,), (1,)), ((), ())), preferred_element_type=F32)


def dot_tn(a, b):
    return lax.dot_general(a, b, (((0,), (0,)), ((), ())), preferred_element_type=F32)


def cost(flops=1000):
    return pl.CostEstimate(flops=flops, bytes_accessed=1000, transcendentals=0)


def image(width, lo=0):
    return pl.BlockSpec((1, ROWS, width), lambda i, *_: (i + lo, 0, 0))


def images(count, width, kind):
    return jax.ShapeDtypeStruct((count, ROWS, width), kind)


ANY = pl.BlockSpec(memory_space=pl.ANY)


def whole(shape):
    zeros = (0,) * len(shape)
    return pl.BlockSpec(shape, lambda *_: zeros)


def flag(value):
    return value.astype(jnp.int32).reshape(1)


def cross_kernel(here_ref, own_ref, across_ref, out_ref):
    first = here_ref[0] == 0
    out_ref[0] = jnp.where(first, own_ref[...], across_ref[...])
    out_ref[1] = jnp.where(first, across_ref[...], own_ref[...])


def cross(shard):
    across = hop(shard, "dp", 1)
    return pl.pallas_call(
        cross_kernel,
        grid_spec=pltpu.PrefetchScalarGridSpec(
            num_scalar_prefetch=1,
            grid=(1,),
            in_specs=[whole(shard.shape)] * 2,
            out_specs=whole((2,) + shard.shape),
        ),
        out_shape=jax.ShapeDtypeStruct((2,) + shard.shape, shard.dtype),
        name="cross",
        cost_estimate=cost(),
    )(flag(lax.axis_index("dp")), shard, across)


def stack_kernel(*refs):
    for n, ref in enumerate(refs[:-1]):
        refs[-1][n] = ref[...]


def stacked(parts):
    shape = (len(parts),) + parts[0].shape
    return pl.pallas_call(
        stack_kernel,
        grid=(1,),
        in_specs=[whole(p.shape) for p in parts],
        out_specs=whole(shape),
        out_shape=jax.ShapeDtypeStruct(shape, parts[0].dtype),
        name="stacked",
        cost_estimate=cost(),
    )(*parts)


def sort_kernel(*refs):
    parts, (mine_ref, away_ref) = refs[:-2], refs[-2:]
    for n, ref in enumerate(parts):
        mine_ref[n] = ref[0]
        away_ref[n] = ref[1]


def sort_groups(parts):
    shape = (len(parts),) + parts[0].shape[1:]
    return pl.pallas_call(
        sort_kernel,
        grid=(1,),
        in_specs=[whole(p.shape) for p in parts],
        out_specs=[whole(shape)] * 2,
        out_shape=[jax.ShapeDtypeStruct(shape, parts[0].dtype)] * 2,
        name="sort_groups",
        cost_estimate=cost(),
    )(*parts)


def add_kernel(near_ref, away_ref, out_ref):
    out_ref[...] = (near_ref[...] + away_ref[...].astype(F32)).astype(BF)


def add_halves(near, away):
    part = pl.BlockSpec((1,) + near.shape[1:], lambda i: (i, 0, 0))
    return pl.pallas_call(
        add_kernel,
        grid=(near.shape[0],),
        in_specs=[part, part],
        out_specs=part,
        out_shape=jax.ShapeDtypeStruct(near.shape, BF),
        name="add_halves",
        cost_estimate=cost(),
    )(near, away)


def vector_kernel(narrow_ref, out_ref, *, start):
    row = lax.broadcasted_iota(jnp.int32, (8, LANES), 0)
    lane = lax.broadcasted_iota(jnp.int32, (8, LANES), 1)
    wanted = jnp.where((lane == row + start) & (row < 4), 1.0, 0.0).astype(BF)
    out_ref[...] = dot_nt(wanted, narrow_ref[...])


def vectors_of(narrow, start):
    return pl.pallas_call(
        functools.partial(vector_kernel, start=start),
        grid=(1,),
        in_specs=[whole(narrow.shape)],
        out_specs=whole((8, D)),
        out_shape=jax.ShapeDtypeStruct((8, D), F32),
        name="vectors",
        cost_estimate=cost(),
    )(narrow)


def assemble_kernel(here_ref, same_ref, flip_ref, *out_refs):
    chips, _, rows, _ = same_ref.shape
    for chip in range(chips):
        for b, ref in enumerate((same_ref, flip_ref)):
            place = here_ref[0] ^ (2 * chip + b)
            for d in range(2):
                at = pl.ds(pl.multiple_of((d * 2 * chips + place) * rows, 16), rows)
                lo = 0
                for out_ref in out_refs:
                    out_ref[at, :] = ref[chip, d, :, lo : lo + out_ref.shape[1]]
                    lo += out_ref.shape[1]


def assemble(same, flipped, widths):
    chips, _, rows, columns = same.shape
    here = lax.axis_index("expert").astype(jnp.int32)
    if rows % 16 == 0:
        return pl.pallas_call(
            assemble_kernel,
            grid_spec=pltpu.PrefetchScalarGridSpec(
                num_scalar_prefetch=1,
                grid=(1,),
                in_specs=[whole(same.shape), whole(same.shape)],
                out_specs=[whole((4 * chips * rows, w)) for w in widths],
            ),
            out_shape=[jax.ShapeDtypeStruct((4 * chips * rows, w), same.dtype) for w in widths],
            name="assemble",
            cost_estimate=cost(),
        )(here.reshape(1), same, flipped)
    buffer = jnp.zeros((2, 2 * chips, rows, columns), same.dtype)
    for j in range(chips):
        for b, both in enumerate((same, flipped)):
            buffer = lax.dynamic_update_slice(buffer, both[j][:, None], (0, here ^ (2 * j + b), 0, 0))
    buffer = buffer.reshape(-1, columns)
    cuts = [sum(widths[:n]) for n in range(len(widths) + 1)]
    return [buffer[:, cuts[n] : cuts[n + 1]] for n in range(len(widths))]


def chip_copies(pair):
    count = lax.axis_size("expert")
    return [pair] + [hop(pair, "expert", k) for k in range(2, count, 2)]


def pick(array, index, axis):
    return lax.dynamic_index_in_dim(array, index, axis, False)


def chip_sum(total, wide):
    here_dp = lax.axis_index("dp")
    chip = lax.axis_index("expert") >> 1
    summed = pick(total, chip, 1)
    for k in range(1, total.shape[1]):
        summed = summed + hop(pick(total, chip ^ k, 1).astype(wide), "expert", 2 * k).astype(F32)
    return pick(summed, here_dp, 0), pick(summed, 1 - here_dp, 0).astype(wide)


def normed(values):
    average = jnp.mean(values, axis=-1, keepdims=True)
    centred = values - average
    variance = jnp.mean(centred * centred, axis=-1, keepdims=True)
    scale = lax.rsqrt(variance + EPSILON)
    return centred * scale, scale


def attend_kernel(x_ref, vec_ref, w_ref, *refs):
    a_ref, qkv_ref, o_ref, lse_ref, part_ref = refs[-5:]
    hat, _ = normed(x_ref[0].astype(F32))
    a = (hat * vec_ref[0:1, :] + vec_ref[1:2, :]).astype(BF)
    a_ref[0] = a
    qkv_ref[0] = dot_nn(a, w_ref[...]).astype(BF)
    keys_in = lax.broadcasted_iota(jnp.int32, (ROWS, ROWS), 1) < SEQ
    lane = lax.broadcasted_iota(jnp.int32, (ROWS, LANES), 1)
    lse = jnp.zeros((ROWS, LANES), F32)
    for h in range(HALF // HEAD):
        at = h * HEAD
        q = qkv_ref[0, :, at : at + HEAD]
        k = qkv_ref[0, :, HALF + at : HALF + at + HEAD]
        v = qkv_ref[0, :, 2 * HALF + at : 2 * HALF + at + HEAD]
        s = jnp.where(keys_in, dot_nt(q, k) * SCALE, -1e30)
        top = jnp.max(s, axis=1, keepdims=True)
        total = top + jnp.log(jnp.sum(jnp.exp(s - top), axis=1, keepdims=True))
        weights = jnp.exp(s - total).astype(BF)
        part_ref[0, :, at : at + HEAD] = dot_nn(weights, v).astype(BF)
        lse = jnp.where(lane == h, total, lse)
    lse_ref[0] = lse
    o_ref[0] = part_ref[0]


def attend(x, vectors, weight, lo, hi, held):
    total = x.shape[0]
    return pl.pallas_call(
        attend_kernel,
        grid=(hi - lo,),
        in_specs=[image(D, lo), whole(vectors.shape), whole(weight.shape)] + [ANY] * len(held),
        out_specs=[image(D, lo), image(3 * HALF, lo), image(HALF, lo), image(LANES, lo), image(HALF)],
        out_shape=[
            images(total, D, BF),
            images(total, 3 * HALF, BF),
            images(total, HALF, BF),
            images(total, LANES, F32),
            images(hi - lo, HALF, BF),
        ],
        input_output_aliases={3 + n: n for n in range(len(held))},
        name="attend",
        cost_estimate=cost(),
    )(x, vectors, weight, *held)


def route_kernel(
    which_ref, x_ref, own_ref, got_ref, vec_ref, here_ref, there_ref, router_ref, ids_ref, *refs, count
):
    y_ref, r_ref, g_ref, h_ref = refs[-4:]
    y = x_ref[0].astype(F32) + (
        dot_nt(own_ref[0], here_ref[...]) + dot_nt(got_ref[0], there_ref[...])
    )
    y_ref[0] = y
    hat, _ = normed(y)
    h = (hat * vec_ref[2:3, :] + vec_ref[3:4, :]).astype(BF)
    first = which_ref[0] == 0
    h_ref[0, :, :HALF] = jnp.where(first, h[:, :HALF], h[:, HALF:])
    h_ref[0, :, HALF:] = jnp.where(first, h[:, HALF:], h[:, :HALF])
    lane = lax.broadcasted_iota(jnp.int32, (ROWS, LANES), 1)
    logits = jnp.where(lane < count, dot_nn(h, router_ref[...]), -1e30)
    logits = jnp.exp(logits - jnp.max(logits, axis=1, keepdims=True))
    probs = logits / jnp.sum(logits, axis=1, keepdims=True)
    r_ref[0] = probs
    gates = jnp.zeros((ROWS, LANES), F32)
    for c in range(2):
        gate = jnp.sum(jnp.where(lane == ids_ref[0, :, c : c + 1], probs, 0.0), axis=1, keepdims=True)
        gates = jnp.where(lane == c, gate, gates)
    g_ref[0] = gates


def route(which, x, own, got, vectors, out_here, out_there, router, ids, count, lo, hi, held):
    total = x.shape[0]
    return pl.pallas_call(
        functools.partial(route_kernel, count=count),
        grid_spec=pltpu.PrefetchScalarGridSpec(
            num_scalar_prefetch=1,
            grid=(hi - lo,),
            in_specs=[
                image(D, lo),
                image(HALF),
                image(HALF),
                whole(vectors.shape),
                whole(out_here.shape),
                whole(out_there.shape),
                whole(router.shape),
                image(2, lo),
            ]
            + [ANY] * len(held),
            out_specs=[image(D, lo), image(LANES, lo), image(LANES, lo), image(D)],
        ),
        out_shape=[
            images(total, D, F32),
            images(total, LANES, F32),
            images(total, LANES, F32),
            images(hi - lo, D, BF),
        ],
        input_output_aliases={9 + n: n for n in range(len(held))},
        name="route",
        cost_estimate=cost(),
    )(which, x, own, got, vectors, out_here, out_there, router, ids, *held)


def send_kernel(*refs, parts, chips, gated):
    per = 3 if gated else 2
    groups = [refs[n * per * parts : (n + 1) * per * parts] for n in range(2)]
    out_refs = refs[2 * per * parts :]
    capacity = out_refs[0].shape[1]
    for out_ref, chip in zip(out_refs, chips):
        for r in range(2):
            rows, values, gates = (groups[r][n * parts : (n + 1) * parts] for n in range(3))
            places = lax.broadcasted_iota(jnp.int32, (capacity, 1), 0) + (2 * chip + r) * capacity
            picked = jnp.zeros((capacity, D), F32)
            weight = jnp.zeros((capacity, 1), F32)
            for n in range(parts):
                first = places == rows[n][0:1, :]
                second = places == rows[n][1:2, :]
                chosen = jnp.where(first | second, 1.0, 0.0).astype(BF)
                picked = picked + dot_nn(chosen, values[n][...])
                if gated:
                    each = jnp.where(
                        first, gates[n][0:1, :], jnp.where(second, gates[n][1:2, :], 0.0)
                    )
                    weight = weight + jnp.sum(each, axis=1, keepdims=True)
            if gated:
                picked = picked * weight
            out_ref[r] = picked.astype(BF)


def send_rows(own, other, capacity, chips, gated):
    operands = [part for group in (own, other) for kind in group for part in kind]
    return pl.pallas_call(
        functools.partial(send_kernel, parts=len(own[0]), chips=chips, gated=gated),
        grid=(1,),
        in_specs=[whole(o.shape) for o in operands],
        out_specs=[whole((2, capacity, D))] * len(chips),
        out_shape=[jax.ShapeDtypeStruct((2, capacity, D), BF)] * len(chips),
        name="send_gated" if gated else "send_rows",
        cost_estimate=cost(),
    )(*operands)


def first_lanes():
    row = lax.broadcasted_iota(jnp.int32, (8, LANES), 0)
    return jnp.where(row == lax.broadcasted_iota(jnp.int32, (8, LANES), 1), 1.0, 0.0)


def turn(columns):
    return lax.dot_general(
        first_lanes(), columns, (((1,), (1,)), ((), ())), precision=HIGH, preferred_element_type=F32
    )


def turn_back(rows):
    return lax.dot_general(
        rows, first_lanes(), (((0,), (0,)), ((), ())), precision=HIGH, preferred_element_type=F32
    )


def home_kernel(which_ref, rows_ref, middle_ref, grad_ref, gates_ref, own_ref, other_ref, out_ref, dgate_ref):
    value = middle_ref[0]
    grad = grad_ref[0].astype(F32)
    lane = lax.broadcasted_iota(jnp.int32, (ROWS, LANES), 1)
    found = jnp.zeros((ROWS, LANES), F32)
    chips, capacity = own_ref.shape[:2]
    places = lax.broadcasted_iota(jnp.int32, (1, capacity), 1)
    for c in range(2):
        picked = jnp.zeros((ROWS, HALF), F32)
        for chip in range(chips):
            for r, back_ref in enumerate((own_ref, other_ref)):
                at = rows_ref[0, :, c : c + 1] - (2 * chip + r) * capacity
                chosen = jnp.where(at == places, 1.0, 0.0)
                picked = picked + dot_nn(chosen.astype(BF), back_ref[chip])
        value = value + gates_ref[0, :, c : c + 1] * picked
        dgate = jnp.sum(picked * grad, axis=1, keepdims=True)
        found = jnp.where(lane == c, dgate, found)
    out_ref[0] = value.astype(BF)
    dgate_ref[0] = turn(found)


def bring_home(which, rows, middle, grad, gates, own, other):
    total = middle.shape[0]
    part = pl.BlockSpec((1, ROWS, HALF), lambda i, s: (i, 0, s[0]))
    return pl.pallas_call(
        home_kernel,
        grid_spec=pltpu.PrefetchScalarGridSpec(
            num_scalar_prefetch=1,
            grid=(total,),
            in_specs=[image(2), part, part, image(LANES), whole(own.shape), whole(other.shape)],
            out_specs=[image(HALF), pl.BlockSpec((1, 8, ROWS), lambda i, s: (i, 0, 0))],
        ),
        out_shape=[images(total, HALF, BF), jax.ShapeDtypeStruct((total, 8, ROWS), F32)],
        name="bring_home",
        cost_estimate=cost(),
    )(which, rows, middle, grad, gates, own, other)


def sum_kernel(rows_ref, own_ref, other_ref, out_ref):
    chips, capacity = own_ref.shape[:2]
    places = lax.broadcasted_iota(jnp.int32, (1, capacity), 1)
    total = jnp.zeros((ROWS, HALF), F32)
    for chip in range(chips):
        for r, back_ref in enumerate((own_ref, other_ref)):
            base = (2 * chip + r) * capacity
            chosen = (rows_ref[0, :, 0:1] - base == places) | (rows_ref[0, :, 1:2] - base == places)
            total = total + dot_nn(jnp.where(chosen, 1.0, 0.0).astype(BF), back_ref[chip])
    out_ref[0] = total.astype(BF)


def sum_home(rows, own, other, lo, hi):
    return pl.pallas_call(
        sum_kernel,
        grid=(hi - lo,),
        in_specs=[image(2, lo), whole(own.shape), whole(other.shape)],
        out_specs=image(HALF),
        out_shape=images(hi - lo, HALF, BF),
        name="sum_home",
        cost_estimate=cost(),
    )(rows, own, other)


def gelu_parts(u):
    size = jnp.abs(u)
    t = 1.0 / (1.0 + TAIL_RATE * size)
    poly = jnp.full_like(t, TAIL[-1])
    for c in TAIL[-2::-1]:
        poly = poly * t + c
    bell = jnp.exp(-0.5 * (u * u))
    tail = bell * (t * poly)
    normal = jnp.where(u >= 0.0, 1.0 - tail, tail)
    return u * normal, normal + u * (DENSITY * bell)


def in_order(same_ref, refs):
    same = same_ref[0] == 1
    n, m = len(IN_CUTS), len(BACK_CUTS)
    join = lambda refs, axis: jnp.concatenate([ref[...] for ref in refs], axis=axis)
    pairs = [
        (join(refs[:n], 0), join(refs[n : 2 * n], 0)),
        (join(refs[2 * n : 2 * n + m], 1), join(refs[2 * n + m :], 1)),
    ]
    return [v for a, b in pairs for v in (jnp.where(same, a, b), jnp.where(same, b, a))]


def weight_specs():
    across = [pl.BlockSpec((hi - lo, TILE), lambda i, s: (0, i)) for lo, hi in IN_CUTS]
    down = [pl.BlockSpec((TILE, hi - lo), lambda i, s: (i, 0)) for lo, hi in BACK_CUTS]
    return across * 2 + down * 2


def forward_kernel(same_ref, m_ref, *refs):
    *weights, g_ref, s_ref, zt_ref, zh_ref, acc = refs
    w1h, w1t, w2h, w2t = in_order(same_ref, weights)
    step = pl.program_id(0)
    last = pl.num_programs(0) - 1
    for b in range(m_ref.shape[0]):
        u = dot_nn(m_ref[b, :, :HALF], w1h) + dot_nn(m_ref[b, :, HALF:], w1t)
        g, slope = gelu_parts(u)
        g = g.astype(BF)
        g_ref[b] = g
        s_ref[b] = slope.astype(BF)
        away = dot_nn(g, w2t)
        near = dot_nn(g, w2h)

        @pl.when(step == 0)
        def _():
            acc[b] = away
            zh_ref[b] = near

        @pl.when(step > 0)
        def _():
            acc[b] += away
            zh_ref[b] += near

        @pl.when(step == last)
        def _():
            zt_ref[b] = acc[b].astype(BF)


def expert_forward(same, rows, *weights):
    blocks, capacity, _ = rows.shape
    hidden = weights[0].shape[1]
    wide = pl.BlockSpec((blocks, capacity, TILE), lambda i, s: (0, 0, i))
    make = lambda w, t: jax.ShapeDtypeStruct((blocks, capacity, w), t)
    return pl.pallas_call(
        forward_kernel,
        grid_spec=pltpu.PrefetchScalarGridSpec(
            num_scalar_prefetch=1,
            grid=(hidden // TILE,),
            in_specs=[whole(rows.shape)] + weight_specs(),
            out_specs=[wide, wide] + [whole((blocks, capacity, HALF))] * 2,
            scratch_shapes=[pltpu.VMEM((blocks, capacity, HALF), F32)],
        ),
        out_shape=[make(hidden, BF), make(hidden, BF), make(HALF, BF), make(HALF, F32)],
        name="expert_forward",
        cost_estimate=cost(),
    )(same, rows, *weights)


def backward_kernel(same_ref, z_ref, s_ref, *refs):
    *weights, u_ref, mt_ref, mh_ref, acc = refs
    w1h, w1t, w2h, w2t = in_order(same_ref, weights)
    step = pl.program_id(0)
    last = pl.num_programs(0) - 1
    for b in range(z_ref.shape[0]):
        grad = dot_nt(z_ref[b, :, :HALF], w2h) + dot_nt(z_ref[b, :, HALF:], w2t)
        grad = (grad * s_ref[b].astype(F32)).astype(BF)
        u_ref[b] = grad
        away = dot_nt(grad, w1t)
        near = dot_nt(grad, w1h)

        @pl.when(step == 0)
        def _():
            acc[b] = away
            mh_ref[b] = near

        @pl.when(step > 0)
        def _():
            acc[b] += away
            mh_ref[b] += near

        @pl.when(step == last)
        def _():
            mt_ref[b] = acc[b].astype(BF)


def expert_backward(same, rows, slope, *weights):
    blocks, capacity, _ = rows.shape
    hidden = weights[0].shape[1]
    wide = pl.BlockSpec((blocks, capacity, TILE), lambda i, s: (0, 0, i))
    make = lambda w, t: jax.ShapeDtypeStruct((blocks, capacity, w), t)
    return pl.pallas_call(
        backward_kernel,
        grid_spec=pltpu.PrefetchScalarGridSpec(
            num_scalar_prefetch=1,
            grid=(hidden // TILE,),
            in_specs=[whole(rows.shape), wide] + weight_specs(),
            out_specs=[wide] + [whole((blocks, capacity, HALF))] * 2,
            scratch_shapes=[pltpu.VMEM((blocks, capacity, HALF), F32)],
        ),
        out_shape=[make(hidden, BF), make(HALF, BF), make(HALF, F32)],
        name="expert_backward",
        cost_estimate=cost(),
    )(same, rows, slope, *weights)


def outer_kernel(which_ref, *refs, chunks, hidden_first, added):
    step = pl.program_id(0)
    wides = refs[:chunks]
    narrows = refs[chunks : 2 * chunks]
    out_ref = refs[-1]
    total = None
    for wide_ref, slim_ref in zip(wides, narrows):
        for b in range(wide_ref.shape[0]):
            slim = slim_ref[b]
            term = dot_tn(wide_ref[b], slim) if hidden_first else dot_tn(slim, wide_ref[b])
            total = term if total is None else total + term
    if added == 1:
        total = total + refs[-2][...].astype(F32)
    elif added == 2 and not hidden_first:
        total = total + jnp.concatenate([refs[-3][...], refs[-2][...]], axis=0).astype(F32)
    elif added == 2:
        total = total + jnp.where(step == 0, refs[-3][...], refs[-2][...]).astype(F32)
    out_ref[...] = total.astype(out_ref.dtype)


def outer(which, wides, narrows, hidden_first, extra=None):
    per, capacity, hidden = wides[0].shape
    slim = pl.BlockSpec((per, capacity, HALF), lambda i, s: (0, 0, s[0]))
    if hidden_first:
        shape, out = (hidden, HALF), pl.BlockSpec((TILE, HALF), lambda i, s: (i, 0))
    else:
        shape, out = (HALF, hidden), pl.BlockSpec((HALF, TILE), lambda i, s: (0, i))
    specs = [pl.BlockSpec((per, capacity, TILE), lambda i, s: (0, 0, i))] * len(wides)
    specs += [slim] * len(narrows)
    operands = list(wides) + list(narrows)
    extra = [] if extra is None else list(extra)
    if len(extra) == 1:
        specs.append(out)
    elif len(extra) == 2 and not hidden_first:
        specs += [pl.BlockSpec((HALF // 2, TILE), lambda i, s: (0, i))] * 2
    elif len(extra) == 2:
        specs.append(pl.BlockSpec((TILE, HALF), lambda i, s: (0, 0)))
        specs.append(pl.BlockSpec((TILE, HALF), lambda i, s: (jnp.maximum(i - 1, 0), 0)))
    operands += extra
    return pl.pallas_call(
        functools.partial(
            outer_kernel,
            chunks=len(wides),
            hidden_first=hidden_first,
            added=len(extra),
        ),
        grid_spec=pltpu.PrefetchScalarGridSpec(
            num_scalar_prefetch=1, grid=(hidden // TILE,), in_specs=specs, out_specs=out
        ),
        out_shape=jax.ShapeDtypeStruct(shape, F32 if extra else BF),
        name="outer_keep" if extra else "outer_send",
        cost_estimate=cost(),
    )(which, *operands)


def norm_back(grad, hat, scale, gain):
    inner = grad * gain
    return scale * (
        inner
        - jnp.mean(inner, axis=-1, keepdims=True)
        - hat * jnp.mean(inner * hat, axis=-1, keepdims=True)
    )


def add_sums(ref, grad, hat, first):
    sums = [jnp.sum(grad * hat, axis=0, keepdims=True), jnp.sum(grad, axis=0, keepdims=True)]

    @pl.when(first)
    def _():
        ref[...] = jnp.zeros_like(ref)

    ref[0:1, :] += sums[0]
    ref[1:2, :] += sums[1]


def attend_back_kernel(
    which_ref,
    x_ref,
    y_ref,
    near_ref,
    away_ref,
    dgate_ref,
    dgate2_ref,
    probs_ref,
    ids_ref,
    narrow_ref,
    cot_ref,
    vec_ref,
    out_w_ref,
    qkv_ref,
    lse_ref,
    w_ref,
    *refs,
):
    dy_ref, dyb_ref, dqkv_ref, part_ref, sums2_ref, sums1_ref, router_ref, att_ref = refs[-8:]
    first = which_ref[0] == 0
    start = pl.program_id(0) == 0
    near = near_ref[0].astype(F32)
    away = away_ref[0].astype(F32)
    dgate = turn_back(dgate_ref[0] + dgate2_ref[0])
    lane = lax.broadcasted_iota(jnp.int32, (ROWS, LANES), 1)
    probs = probs_ref[0]
    grad_probs = sum(
        jnp.where(lane == ids_ref[0, :, c : c + 1], dgate[:, c : c + 1], 0.0) for c in range(2)
    )
    grad_logits = probs * (grad_probs - jnp.sum(probs * grad_probs, axis=1, keepdims=True))
    high = grad_logits.astype(BF)
    low = (grad_logits - high.astype(F32)).astype(BF)
    narrow = narrow_ref[...]
    grad = (dot_nt(high, narrow) + dot_nt(low, narrow)) + jnp.concatenate(
        [jnp.where(first, near, away), jnp.where(first, away, near)], axis=1
    )
    hat, scale = normed(y_ref[0])
    h = (hat * vec_ref[2:3, :] + vec_ref[3:4, :]).astype(BF)
    grad_router = dot_tn(high, h) + dot_tn(low, h)

    @pl.when(start)
    def _():
        router_ref[...] = grad_router

    @pl.when(jnp.logical_not(start))
    def _():
        router_ref[...] += grad_router

    add_sums(sums2_ref, grad, hat, start)
    dy = cot_ref[0].astype(F32) + norm_back(grad, hat, scale, vec_ref[2:3, :])
    dy_ref[0] = dy
    dyb = dy.astype(BF)
    dyb_ref[0] = dyb
    att_ref[...] = dot_nn(dyb, out_w_ref[...]).astype(BF)
    keys_in = lax.broadcasted_iota(jnp.int32, (ROWS, ROWS), 1) < SEQ
    for h in range(HALF // HEAD):
        at = h * HEAD
        q = qkv_ref[0, :, at : at + HEAD]
        k = qkv_ref[0, :, HALF + at : HALF + at + HEAD]
        v = qkv_ref[0, :, 2 * HALF + at : 2 * HALF + at + HEAD]
        do = att_ref[:, at : at + HEAD]
        s = jnp.where(keys_in, dot_nt(q, k) * SCALE, -1e30)
        weights = jnp.exp(s - lse_ref[0, :, h : h + 1])
        dv = dot_tn(weights.astype(BF), do)
        dp = dot_nt(do, v)
        ds = (weights * (dp - jnp.sum(weights * dp, axis=1, keepdims=True))).astype(BF)
        dqkv_ref[0, :, at : at + HEAD] = (dot_nn(ds, k) * SCALE).astype(BF)
        dqkv_ref[0, :, HALF + at : HALF + at + HEAD] = (dot_tn(ds, q) * SCALE).astype(BF)
        dqkv_ref[0, :, 2 * HALF + at : 2 * HALF + at + HEAD] = dv.astype(BF)
    part = dot_nt(dqkv_ref[0], w_ref[...])
    part_ref[0] = part.astype(BF)
    hat, _ = normed(x_ref[0].astype(F32))
    add_sums(sums1_ref, part, hat, start)


def attend_back(which, x, y, near, away, dgate, dgate2, probs, ids, narrow, cot, vectors, out_w, qkv, lse, weight, lo, hi, held):
    total = y.shape[0]
    turned = pl.BlockSpec((1, 8, ROWS), lambda i, s: (i + lo, 0, 0))
    return pl.pallas_call(
        attend_back_kernel,
        grid_spec=pltpu.PrefetchScalarGridSpec(
            num_scalar_prefetch=1,
            grid=(hi - lo,),
            in_specs=[
                image(D, lo),
                image(D, lo),
                image(HALF, lo),
                image(HALF, lo),
                turned,
                turned,
                image(LANES, lo),
                image(2, lo),
                whole(narrow.shape),
                image(D, lo),
                whole(vectors.shape),
                whole(out_w.shape),
                image(3 * HALF, lo),
                image(LANES, lo),
                whole(weight.shape),
            ]
            + [ANY] * len(held),
            out_specs=[
                image(D, lo),
                image(D, lo),
                image(3 * HALF, lo),
                image(D),
                whole((8, D)),
                whole((8, D)),
                whole((LANES, D)),
            ],
            scratch_shapes=[pltpu.VMEM((ROWS, HALF), BF)],
        ),
        out_shape=[
            images(total, D, F32),
            images(total, D, BF),
            images(total, 3 * HALF, BF),
            images(hi - lo, D, BF),
            jax.ShapeDtypeStruct((8, D), F32),
            jax.ShapeDtypeStruct((8, D), F32),
            jax.ShapeDtypeStruct((LANES, D), F32),
        ],
        input_output_aliases={16 + n: n for n in range(len(held))},
        name="attend_back",
        cost_estimate=cost(),
    )(which, x, y, near, away, dgate, dgate2, probs, ids, narrow, cot, vectors, out_w, qkv, lse, weight, *held)


def token_kernel(x_ref, own_ref, got_ref, dy_ref, vec_ref, *refs):
    out_ref = refs[-1]
    grad = own_ref[0].astype(F32) + got_ref[0].astype(F32)
    hat, scale = normed(x_ref[0].astype(F32))
    out_ref[0] = dy_ref[0] + norm_back(grad, hat, scale, vec_ref[0:1, :])


def token_back(x, own, got, dy, vectors, lo, hi, held):
    total = x.shape[0]
    return pl.pallas_call(
        token_kernel,
        grid=(hi - lo,),
        in_specs=[image(D, lo), image(D), image(D), image(D, lo), whole(vectors.shape)]
        + [ANY] * len(held),
        out_specs=image(D, lo),
        out_shape=images(total, D, F32),
        input_output_aliases={5 + n: n for n in range(len(held))},
        name="token_back",
        cost_estimate=cost(),
    )(x, own, got, dy, vectors, *held)


def exact(a, b, contract):
    return lax.dot_general(
        a, b, ((contract[:1], contract[1:]), ((), ())), precision=HIGH, preferred_element_type=F32
    )


def of_image(i, tok):
    row = lax.broadcasted_iota(jnp.int32, (ROWS, tok), 0)
    token = lax.broadcasted_iota(jnp.int32, (ROWS, tok), 1)
    return jnp.where((token == row + i * SEQ) & (row < SEQ), 1.0, 0.0)


def image_kernel(which_ref, tok_ref, cot_ref, x_ref, cot_out_ref, here_ref):
    mine = of_image(pl.program_id(0), tok_ref.shape[0]).astype(BF)
    x_ref[0] = dot_nn(mine, tok_ref[...]).astype(BF)
    cot = dot_nn(mine, cot_ref[...]).astype(BF)
    cot_out_ref[0] = cot
    first = which_ref[0] == 0
    here_ref[0, :, :HALF] = jnp.where(first, cot[:, :HALF], cot[:, HALF:])
    here_ref[0, :, HALF:] = jnp.where(first, cot[:, HALF:], cot[:, :HALF])


def image_rows(which, tokens, cotangent):
    pictures = tokens.shape[0] // SEQ
    return pl.pallas_call(
        image_kernel,
        grid_spec=pltpu.PrefetchScalarGridSpec(
            num_scalar_prefetch=1,
            grid=(pictures,),
            in_specs=[whole(tokens.shape)] * 2,
            out_specs=[image(D)] * 3,
        ),
        out_shape=[images(pictures, D, BF)] * 3,
        name="image_rows",
        cost_estimate=cost(),
    )(which, tokens, cotangent)


def slot_kernel(here_ref, ids_ref, rows_ref, lanes_ref, ids_out_ref, *, capacity):
    tok = ids_ref.shape[0]
    lane = lax.broadcasted_iota(jnp.int32, (tok, LANES), 1)
    earlier = jnp.where(
        lax.broadcasted_iota(jnp.int32, (tok, tok), 1) < lax.broadcasted_iota(jnp.int32, (tok, tok), 0),
        1.0, 0.0,
    ).astype(BF)
    ids = [ids_ref[:, c : c + 1] for c in range(2)]
    taken = jnp.zeros((1, LANES), F32)
    table = jnp.zeros((tok, LANES), F32)
    for c in range(2):
        onehot = jnp.where(lane == ids[c], 1.0, 0.0)
        before = dot_nn(earlier, onehot.astype(BF)) + taken
        slot = jnp.sum(before * onehot, axis=1, keepdims=True)
        taken = taken + jnp.sum(onehot, axis=0, keepdims=True)
        place = ((ids[c] ^ here_ref[0]) * capacity).astype(F32) + slot + 1.0
        table = jnp.where(lane == c, place, table)
        table = jnp.where(lane == 2 + c, ids[c].astype(F32) + 1.0, table)
    for i in range(rows_ref.shape[0]):
        part = exact(of_image(i, tok), table, (1, 0)) - 1.0
        whole_part = part.astype(jnp.int32)
        rows_ref[i] = whole_part[:, 0:2]
        ids_out_ref[i] = whole_part[:, 2:4]
        lanes_ref[:, i * ROWS : (i + 1) * ROWS] = exact(first_lanes(), part, (1, 1)).astype(jnp.int32)


def slot_rows(here, expert_ids, capacity):
    tok = expert_ids.shape[0]
    pictures = tok // SEQ
    shapes = [(pictures, ROWS, 2), (8, pictures * ROWS), (pictures, ROWS, 2)]
    rows, lanes, ids = pl.pallas_call(
        functools.partial(slot_kernel, capacity=capacity),
        grid_spec=pltpu.PrefetchScalarGridSpec(
            num_scalar_prefetch=1,
            grid=(1,),
            in_specs=[whole(expert_ids.shape)],
            out_specs=[whole(shape) for shape in shapes],
        ),
        out_shape=[jax.ShapeDtypeStruct(shape, jnp.int32) for shape in shapes],
        name="slot_rows",
        cost_estimate=cost(),
    )(flag(here), expert_ids)
    return rows, lanes, ids


def projection_kernel(core_ref, *refs, parts, split):
    a_ref, dqkv_ref, dyb_ref, o_ref = refs[:4]
    routers, ones, twos = (refs[4 + n * parts : 4 + (n + 1) * parts] for n in range(3))
    out_ref = refs[-1]
    step = pl.program_id(0)
    last = pl.num_programs(0) - 1
    qkv = dot_tn(a_ref[0], dqkv_ref[0])
    out = dot_tn(dyb_ref[0], o_ref[0])

    @pl.when(step == 0)
    def _():
        out_ref[:, : 3 * HALF] = qkv
        out_ref[:, 3 * HALF : 4 * HALF] = out
        total = 0.5 * sum(r[...] for r in routers)
        sums = jnp.concatenate(
            [sum(r[0:2, :] for r in ones), 0.5 * sum(r[0:2, :] for r in twos), jnp.zeros((4, D), F32)],
            axis=0,
        )
        out_ref[:, 4 * HALF :] = jnp.transpose(
            jnp.concatenate([total[: LANES - 8], sums], axis=0)
        )

    @pl.when(step > 0)
    def _():
        out_ref[:, : 3 * HALF] += qkv
        out_ref[:, 3 * HALF : 4 * HALF] += out

    if split:

        @pl.when(step == last)
        def _():
            near_ref, away_ref = refs[-3:-1]
            dps, chips, rows, _ = near_ref.shape
            for d in range(dps):
                for chip in range(chips):
                    at = (2 * (d * chips + chip) + core_ref[0]) * rows
                    near_ref[d, chip] = out_ref[pl.ds(pl.multiple_of(at, 16), rows), :]
                    at = (2 * (d * chips + chip) + 1 - core_ref[0]) * rows
                    away = out_ref[pl.ds(pl.multiple_of(at, 16), rows), :]
                    away_ref[d, chip] = away.astype(BF)


def projection_grads(a_rows, dqkv, dyb, o_rows, *small):
    count = lax.axis_size("expert")
    core = lax.axis_index("expert") & 1
    rows = D // (2 * count)
    split = rows % 16 == 0
    shape = (D, 4 * HALF + LANES)
    shares = (2, count // 2, rows, shape[1])
    kinds = [(shares, F32), (shares, BF)] if split else [(shape, F32)]
    out = pl.pallas_call(
        functools.partial(projection_kernel, parts=len(small) // 3, split=split),
        grid_spec=pltpu.PrefetchScalarGridSpec(
            num_scalar_prefetch=1,
            grid=(a_rows.shape[0],),
            in_specs=[image(D), image(3 * HALF), image(D), image(HALF)]
            + [whole(v.shape) for v in small],
            out_specs=[whole(k) for k, _ in kinds],
            scratch_shapes=[pltpu.VMEM(shape, F32)] if split else [],
        ),
        out_shape=[jax.ShapeDtypeStruct(*kind) for kind in kinds],
        name="projection_grads",
        cost_estimate=cost(),
    )(flag(core), a_rows, dqkv, dyb, o_rows, *small)
    if split:
        return out
    blocks = out[0].reshape((2, count // 2, 2, rows, -1))
    return pick(blocks, core, 2), pick(blocks, 1 - core, 2).astype(BF)


def on_device(
    tokens,
    cotangent,
    ln1_gain,
    ln1_bias,
    ln2_gain,
    ln2_bias,
    w_query,
    w_key,
    w_value,
    w_out,
    w_router,
    w_in,
    w_back,
    expert_ids,
):
    count = lax.axis_size("expert")
    chips = count // 2
    tok = tokens.shape[0]
    capacity = (10 * tok + 32 * count - 1) // (32 * count) * 8
    pictures = tok // SEQ
    rows_all = pictures * ROWS
    cut = (pictures + 1) // 2
    groups = [(0, cut), (cut, pictures)] if pictures > 1 else [(0, pictures)]
    lanes_of = lambda value: [value[:, lo * ROWS : hi * ROWS] for lo, hi in groups]
    here = lax.axis_index("expert")
    here_dp = lax.axis_index("dp")
    here_t = lax.axis_index("tensor")
    which = here_t.astype(jnp.int32).reshape(1)
    same = here_t == here_dp

    order = Order()

    small = jnp.stack([ln1_gain, ln1_bias, ln2_gain, ln2_bias], axis=1)
    narrow = jnp.concatenate([w_router, small], axis=1)
    narrow = jnp.pad(narrow, ((0, 0), (0, LANES - narrow.shape[1])))
    first_pack = jnp.concatenate(
        [w_query, w_key, w_value, narrow, jnp.transpose(w_out)], axis=1
    ).astype(BF)
    pair = cross(first_pack)
    in_own = [follow(w_in, first_pack)[0, lo:hi].astype(BF) for lo, hi in IN_CUTS]
    back_own = [follow(w_back, first_pack)[0, :, lo:hi].astype(BF) for lo, hi in BACK_CUTS]
    pair, in_own, back_own = order.wait((pair, in_own, back_own))

    same_chips = stacked(chip_copies(order.after(pair)))
    in_other = [hop(order.after(in_own[0]), "dp", 1)]
    x, cot, cot_here = order.run(lambda *v: image_rows(which, *v), tokens, cotangent)
    cot_here = cot_here.reshape(rows_all, D)
    rows, rows_lanes, ids_pad = order.run(lambda v: slot_rows(here, v, capacity), expert_ids)
    same_chips, in_other[0] = order.wait((same_chips, in_other[0]))
    rows_lane = order.wait(rows_lanes[:2])
    in_other.append(hop(order.after(in_own[1]), "dp", 1))
    rows_next = hop(order.after(rows_lane), "expert", 1)
    cot_next = hop(order.after(cot_here), "expert", 1)
    flipped = order.wait(hop(order.after(same_chips), "expert", 1))
    qkv_w, narrow_all, out_here = order.run(
        lambda *v: assemble(*v, (3 * HALF, LANES, HALF)), same_chips, flipped
    )
    out_there = hop(order.after(out_here), "tensor", 1)
    vectors = order.run(lambda v: vectors_of(v, count), narrow_all)
    in_other[1] = order.wait(in_other[1])
    in_other.append(hop(order.after(in_own[2]), "dp", 1))
    back_other = [hop(order.after(back_own[0]), "dp", 1)]
    rows_next, cot_next = order.wait((rows_next, cot_next))
    own_lanes, next_lanes = order.wait((lanes_of(rows_lane), lanes_of(rows_next)))

    held, o_parts, got_parts = [], [], []
    for n, (lo, hi) in enumerate(groups):
        *held, o_part = order.run(
            lambda x, v, w, *h: attend(x, v, w, lo, hi, h), x, vectors, qkv_w, *held
        )
        o_parts.append(o_part)
        got_parts.append(hop(o_part, "tensor", 1))
    a_rows, qkv, o_rows, lse = held
    out_there = order.wait(out_there)
    got_parts, in_other[2], back_other[0] = order.wait((got_parts, in_other[2], back_other[0]))
    back_other.append(hop(order.after(back_own[1]), "dp", 1))
    held, h_parts, h_next = [], [], []
    for n, (lo, hi) in enumerate(groups):
        *held, h_part = order.run(
            lambda x, o, g, v, w, t, r, i, *h: route(which, x, o, g, v, w, t, r, i, count, lo, hi, h),
            x, o_parts[n], got_parts[n], vectors, out_here, out_there, narrow_all, ids_pad, *held,
        )
        h_parts.append(h_part.reshape(-1, D))
        if n == len(groups) - 1:
            gates_lane = jnp.transpose(held[2].reshape(rows_all, LANES)[:, :2])
            back_other[1], gates_lane = order.wait((back_other[1], gates_lane))
            h_parts[-1] = order.after(h_parts[-1])
            back_other.append(hop(order.after(back_own[2]), "dp", 1))
        h_next.append(hop(h_parts[-1], "expert", 1))
    y, probs, gates = held
    gates_next = hop(order.after(gates_lane), "expert", 1)

    own = (own_lanes, h_parts)
    other = (next_lanes, h_next)
    far = list(range(1, chips))
    outgoing = order.run(lambda *v: send_rows(*v, capacity, far, False), own, other)
    back_other[2] = order.wait(back_other[2])
    arrived = [None] + [hop(order.after(o), "expert", 2 * c) for o, c in zip(outgoing, far)]
    (arrived[0],) = order.run(lambda *v: send_rows(*v, capacity, [0], False), own, other)
    gates_next = order.wait(gates_next)
    own = ([rows_lane], [cot_here], [gates_lane])
    other = ([rows_next], [cot_next], [gates_next])
    grad_outgoing = order.run(lambda *v: send_rows(*v, capacity, far, True), own, other)
    grad_arrived = [None] * chips
    (grad_arrived[0],) = order.run(lambda *v: send_rows(*v, capacity, [0], True), own, other)
    weights = (*in_own, *in_other, *back_own, *back_other)
    same = flag(same)

    hidden, slopes, grads = [], [], []
    came_back, grad_home = [None] * chips, [None] * chips

    def back_to(chip, waiting):
        value = order.run(add_halves, *waiting)
        return hop(value, "expert", 2 * chip) if chip else value

    leaving = []

    def settle_oldest():
        home, chip, waiting = leaving.pop(0)
        home[chip] = back_to(chip, waiting)

    for c in range(chips):
        if c == 1:
            arrived[1:] = order.wait(arrived[1:])
            if chips <= 4:
                grad_arrived[1:] = [
                    hop(order.after(o), "expert", 2 * k) for o, k in zip(grad_outgoing, far)
                ]
        if c and chips > 4:
            grad_arrived[c] = hop(order.after(grad_outgoing[c - 1]), "expert", 2 * c)
        if c == chips - 1 and chips <= 4:
            grad_arrived[1:] = order.wait(grad_arrived[1:])
        g, s, zt, zh = order.run(lambda *v: expert_forward(same, *v), arrived[c], *weights)
        hidden.append(g)
        slopes.append(s)
        if len(leaving) > 1:
            settle_oldest()
        leaving.append((came_back, c, (zh, hop(order.after(zt), "tensor", 1))))
    for c in range(chips):
        if c and chips > 4:
            grad_arrived[c] = order.wait(grad_arrived[c])
        u, mt, mh = order.run(
            lambda *v: expert_backward(same, *v), grad_arrived[c], slopes[c], *weights
        )
        grads.append(u)
        settle_oldest()
        leaving.append((grad_home, c, (mh, hop(order.after(mt), "tensor", 1))))
        if c >= chips // 2:
            step = 2 * (chips - 1) // chips
            for k in range(1 + (c - chips // 2) * step, 1 + (c - chips // 2 + 1) * step):
                came_back[k] = order.wait(came_back[k])
    z_here, z_there = order.run(lambda *v: sort_groups(v), *order.wait(tuple(came_back)))
    z_there = hop(z_there, "expert", 1)
    send_half = same
    settle_oldest()
    back_send = order.run(lambda h, g: outer(send_half, h, g, True), hidden, grad_arrived)
    back_send = order.wait([back_send[:TILE], back_send[TILE:]])
    settle_oldest()
    back_got = [hop(order.after(back_send[0]), "dp", 1)]
    in_send = order.run(lambda g, a: outer(send_half, g, a, False), grads, arrived)
    grad_home = list(order.wait(tuple(grad_home)))
    m_here, m_there = order.run(lambda *v: sort_groups(v), *grad_home)
    back_got[0], in_send = order.wait((back_got[0], in_send))
    in_send = order.wait([in_send[: HALF // 2], in_send[HALF // 2 :]])
    back_got.append(hop(order.after(back_send[1]), "dp", 1))
    m_there = hop(order.after(m_there), "expert", 1)

    out_half, dgate = order.run(
        lambda *v: bring_home(which, *v), rows, y, cot, gates, z_here, z_there
    )
    dgate_next = hop(dgate, "tensor", 1)
    m_there = order.wait(m_there)
    near = order.run(lambda *v: sum_home(*v, 0, pictures), rows, m_here, m_there)
    away = hop(near, "tensor", 1)
    back_got, dgate_next = order.wait((back_got, dgate_next))
    in_got = [hop(order.after(in_send[0]), "dp", 1)]
    away = order.wait(away)
    held, parts, sums, got = [], [], [], []
    for n, (lo, hi) in enumerate(groups):
        *held, part, sums2, sums1, grad_router = order.run(
            lambda *v: attend_back(which, *v[:15], lo, hi, v[15:]),
            x, y, near, away, dgate, dgate_next, probs, ids_pad, narrow_all, cot, vectors, out_here, qkv, lse, qkv_w, *held,
        )
        parts.append(part)
        if n == 0:
            in_got[0] = order.wait(in_got[0])
            in_got.append(hop(order.after(in_send[1]), "dp", 1))
            part = order.after(part)
        got.append(hop(part, "tensor", 1))
        sums.append((grad_router, sums1, sums2))
    dy, dyb, dqkv = held

    routers, ones, twos = zip(*sums)
    total, total_away = order.run(
        projection_grads, a_rows, dqkv, dyb, o_rows, *routers, *ones, *twos
    )
    keep_half = 1 - send_half
    got[0], in_got[1] = order.wait((got[0], in_got[1]))
    total_got = hop(order.after(total_away), "expert", 1)
    grad_back = order.run(
        lambda h, g, b: outer(keep_half, h, g, True, b), hidden, grad_arrived, back_got
    )[None]
    total_got = order.wait(total_got)
    shards, leaving = chip_sum(order.wait(total + total_got.astype(F32)), BF)
    grad_in = order.run(
        lambda g, a, b: outer(keep_half, g, a, False, b), grads, arrived, in_got
    )[None]
    shards, leaving, got = order.wait((shards, leaving, got))
    entering = hop(leaving, "dp", 1)
    out_other = hop(order.after(out_half), "tensor", 1)
    grad_tokens = []
    for n, (lo, hi) in enumerate(groups):
        grad_tokens = [
            order.run(
                lambda *v: token_back(*v[:5], lo, hi, v[5:]),
                x, parts[n], got[n], dy, vectors, *grad_tokens,
            )
        ]
    shards, out_other = order.wait((shards + entering.astype(F32), out_other))
    tiny = shards[:, 4 * HALF :]
    tiny = tiny + hop(tiny, "tensor", 1)
    grad_tokens = grad_tokens[0][:, :SEQ].reshape(tok, D)
    block_out = jnp.where(
        here_t == 0,
        jnp.concatenate([out_half, out_other], axis=2),
        jnp.concatenate([out_other, out_half], axis=2),
    )
    block_out = block_out[:, :SEQ].reshape(tok, D)
    return (
        block_out,
        grad_tokens,
        tiny[:, LANES - 8],
        tiny[:, LANES - 7],
        tiny[:, LANES - 6],
        tiny[:, LANES - 5],
        shards[:, :HALF],
        shards[:, HALF : 2 * HALF],
        shards[:, 2 * HALF : 3 * HALF],
        jnp.transpose(shards[:, 3 * HALF : 4 * HALF]),
        tiny[:, :count],
        grad_in,
        grad_back,
    )


def solution(mesh):
    rows = ("dp", "expert")
    in_specs = (
        P(rows, None),
        P(rows, None),
        P(rows),
        P(rows),
        P(rows),
        P(rows),
        P(rows, "tensor"),
        P(rows, "tensor"),
        P(rows, "tensor"),
        P("tensor", rows),
        P(rows, None),
        P("expert", "dp", "tensor"),
        P("expert", "tensor", "dp"),
        P(rows, None),
    )
    out_specs = (
        P(rows, None),
        P(rows, None),
        P(rows),
        P(rows),
        P(rows),
        P(rows),
        P(rows, "tensor"),
        P(rows, "tensor"),
        P(rows, "tensor"),
        P("tensor", rows),
        P(rows, None),
        P("expert", "dp", "tensor"),
        P("expert", "tensor", "dp"),
    )
    return jax.shard_map(
        on_device, mesh=mesh, in_specs=in_specs, out_specs=out_specs, check_vma=False
    )
```

```python
import functools

import jax
import jax.numpy as jnp
from jax import lax
from jax.experimental import pallas as pl
from jax.experimental.pallas import tpu as pltpu
from jax.sharding import PartitionSpec as P

D = 768
HALF = 384
HEADS = 12
SEQ = 197
ROWS = 208
HEAD = D // HEADS
SCALE = HEAD ** (-0.5)
EPSILON = 1e-06
HIGH = lax.Precision.HIGHEST
BF = jnp.bfloat16
F32 = jnp.float32
LANES = 128
TILE = 512
IN_CUTS = ((0, 176), (176, 240), (240, 384))
BACK_CUTS = ((0, 128), (128, 384))
TAIL_RATE = 0.305
TAIL = (
    0.12163973686996697,
    0.12246675128071258,
    0.10342128505066615,
    0.12102026121907625,
    -0.03797407148483761,
    0.1857138128109823,
    -0.15298645906475614,
    0.03669873020693663,
)
DENSITY = 0.3989422804014327


def hop(value, axis, offset):
    count = lax.axis_size(axis)
    return lax.ppermute(value, axis, [(i, i ^ offset) for i in range(count)])


class Order:
    def __init__(self):
        self.token = lax.create_token()

    def after(self, value):
        return lax.optimization_barrier((self.token, value))[1]

    def wait(self, value):
        self.token, value = lax.optimization_barrier((self.token, value))
        return value

    def run(self, function, *operands):
        return self.wait(function(*self.after(operands)))


def follow(value, first):
    token = lax.optimization_barrier((lax.create_token(), first))[0]
    return lax.optimization_barrier((token, value))[1]


def dot_nn(a, b):
    return lax.dot_general(a, b, (((1,), (0,)), ((), ())), preferred_element_type=F32)


def dot_nt(a, b):
    return lax.dot_general(a, b, (((1,), (1,)), ((), ())), preferred_element_type=F32)


def dot_tn(a, b):
    return lax.dot_general(a, b, (((0,), (0,)), ((), ())), preferred_element_type=F32)


def cost(flops=1000):
    return pl.CostEstimate(flops=flops, bytes_accessed=1000, transcendentals=0)


def image(width, lo=0):
    return pl.BlockSpec((1, ROWS, width), lambda i, *_: (i + lo, 0, 0))


def images(count, width, kind):
    return jax.ShapeDtypeStruct((count, ROWS, width), kind)


ANY = pl.BlockSpec(memory_space=pl.ANY)


def whole(shape):
    zeros = (0,) * len(shape)
    return pl.BlockSpec(shape, lambda *_: zeros)


def flag(value):
    return value.astype(jnp.int32).reshape(1)


def cross_kernel(here_ref, own_ref, across_ref, out_ref):
    first = here_ref[0] == 0
    out_ref[0] = jnp.where(first, own_ref[...], across_ref[...])
    out_ref[1] = jnp.where(first, across_ref[...], own_ref[...])


def cross(shard):
    across = hop(shard, "dp", 1)
    return pl.pallas_call(
        cross_kernel,
        grid_spec=pltpu.PrefetchScalarGridSpec(
            num_scalar_prefetch=1,
            grid=(1,),
            in_specs=[whole(shard.shape)] * 2,
            out_specs=whole((2,) + shard.shape),
        ),
        out_shape=jax.ShapeDtypeStruct((2,) + shard.shape, shard.dtype),
        name="cross",
        cost_estimate=cost(),
    )(flag(lax.axis_index("dp")), shard, across)


def stack_kernel(*refs):
    for n, ref in enumerate(refs[:-1]):
        refs[-1][n] = ref[...]


def stacked(parts):
    shape = (len(parts),) + parts[0].shape
    return pl.pallas_call(
        stack_kernel,
        grid=(1,),
        in_specs=[whole(p.shape) for p in parts],
        out_specs=whole(shape),
        out_shape=jax.ShapeDtypeStruct(shape, parts[0].dtype),
        name="stacked",
        cost_estimate=cost(),
    )(*parts)


def sort_kernel(*refs):
    parts, (mine_ref, away_ref) = refs[:-2], refs[-2:]
    for n, ref in enumerate(parts):
        mine_ref[n] = ref[0]
        away_ref[n] = ref[1]


def sort_groups(parts):
    shape = (len(parts),) + parts[0].shape[1:]
    return pl.pallas_call(
        sort_kernel,
        grid=(1,),
        in_specs=[whole(p.shape) for p in parts],
        out_specs=[whole(shape)] * 2,
        out_shape=[jax.ShapeDtypeStruct(shape, parts[0].dtype)] * 2,
        name="sort_groups",
        cost_estimate=cost(),
    )(*parts)


def add_kernel(near_ref, away_ref, out_ref):
    out_ref[...] = (near_ref[...] + away_ref[...].astype(F32)).astype(BF)


def add_halves(near, away):
    part = pl.BlockSpec((1,) + near.shape[1:], lambda i: (i, 0, 0))
    return pl.pallas_call(
        add_kernel,
        grid=(near.shape[0],),
        in_specs=[part, part],
        out_specs=part,
        out_shape=jax.ShapeDtypeStruct(near.shape, BF),
        name="add_halves",
        cost_estimate=cost(),
    )(near, away)


def vector_kernel(narrow_ref, out_ref, *, start):
    row = lax.broadcasted_iota(jnp.int32, (8, LANES), 0)
    lane = lax.broadcasted_iota(jnp.int32, (8, LANES), 1)
    wanted = jnp.where((lane == row + start) & (row < 4), 1.0, 0.0).astype(BF)
    out_ref[...] = dot_nt(wanted, narrow_ref[...])


def vectors_of(narrow, start):
    return pl.pallas_call(
        functools.partial(vector_kernel, start=start),
        grid=(1,),
        in_specs=[whole(narrow.shape)],
        out_specs=whole((8, D)),
        out_shape=jax.ShapeDtypeStruct((8, D), F32),
        name="vectors",
        cost_estimate=cost(),
    )(narrow)


def assemble_kernel(here_ref, same_ref, flip_ref, *out_refs):
    chips, _, rows, _ = same_ref.shape
    for chip in range(chips):
        for b, ref in enumerate((same_ref, flip_ref)):
            place = here_ref[0] ^ (2 * chip + b)
            for d in range(2):
                at = pl.ds(pl.multiple_of((d * 2 * chips + place) * rows, 16), rows)
                lo = 0
                for out_ref in out_refs:
                    out_ref[at, :] = ref[chip, d, :, lo : lo + out_ref.shape[1]]
                    lo += out_ref.shape[1]


def assemble(same, flipped, widths):
    chips, _, rows, columns = same.shape
    here = lax.axis_index("expert").astype(jnp.int32)
    if rows % 16 == 0:
        return pl.pallas_call(
            assemble_kernel,
            grid_spec=pltpu.PrefetchScalarGridSpec(
                num_scalar_prefetch=1,
                grid=(1,),
                in_specs=[whole(same.shape), whole(same.shape)],
                out_specs=[whole((4 * chips * rows, w)) for w in widths],
            ),
            out_shape=[jax.ShapeDtypeStruct((4 * chips * rows, w), same.dtype) for w in widths],
            name="assemble",
            cost_estimate=cost(),
        )(here.reshape(1), same, flipped)
    buffer = jnp.zeros((2, 2 * chips, rows, columns), same.dtype)
    for j in range(chips):
        for b, both in enumerate((same, flipped)):
            buffer = lax.dynamic_update_slice(buffer, both[j][:, None], (0, here ^ (2 * j + b), 0, 0))
    buffer = buffer.reshape(-1, columns)
    cuts = [sum(widths[:n]) for n in range(len(widths) + 1)]
    return [buffer[:, cuts[n] : cuts[n + 1]] for n in range(len(widths))]


def chip_copies(pair):
    count = lax.axis_size("expert")
    return [pair] + [hop(pair, "expert", k) for k in range(2, count, 2)]


def pick(array, index, axis):
    return lax.dynamic_index_in_dim(array, index, axis, False)


def chip_sum(total, wide):
    here_dp = lax.axis_index("dp")
    chip = lax.axis_index("expert") >> 1
    summed = pick(total, chip, 1)
    for k in range(1, total.shape[1]):
        summed = summed + hop(pick(total, chip ^ k, 1).astype(wide), "expert", 2 * k).astype(F32)
    return pick(summed, here_dp, 0), pick(summed, 1 - here_dp, 0).astype(wide)


def normed(values):
    average = jnp.mean(values, axis=-1, keepdims=True)
    centred = values - average
    variance = jnp.mean(centred * centred, axis=-1, keepdims=True)
    scale = lax.rsqrt(variance + EPSILON)
    return centred * scale, scale


def attend_kernel(x_ref, vec_ref, w_ref, *refs):
    a_ref, qkv_ref, o_ref, lse_ref, part_ref = refs[-5:]
    hat, _ = normed(x_ref[0].astype(F32))
    a = (hat * vec_ref[0:1, :] + vec_ref[1:2, :]).astype(BF)
    a_ref[0] = a
    qkv_ref[0] = dot_nn(a, w_ref[...]).astype(BF)
    keys_in = lax.broadcasted_iota(jnp.int32, (ROWS, ROWS), 1) < SEQ
    lane = lax.broadcasted_iota(jnp.int32, (ROWS, LANES), 1)
    lse = jnp.zeros((ROWS, LANES), F32)
    for h in range(HALF // HEAD):
        at = h * HEAD
        q = qkv_ref[0, :, at : at + HEAD]
        k = qkv_ref[0, :, HALF + at : HALF + at + HEAD]
        v = qkv_ref[0, :, 2 * HALF + at : 2 * HALF + at + HEAD]
        s = jnp.where(keys_in, dot_nt(q, k) * SCALE, -1e30)
        top = jnp.max(s, axis=1, keepdims=True)
        total = top + jnp.log(jnp.sum(jnp.exp(s - top), axis=1, keepdims=True))
        weights = jnp.exp(s - total).astype(BF)
        part_ref[0, :, at : at + HEAD] = dot_nn(weights, v).astype(BF)
        lse = jnp.where(lane == h, total, lse)
    lse_ref[0] = lse
    o_ref[0] = part_ref[0]


def attend(x, vectors, weight, lo, hi, held):
    total = x.shape[0]
    return pl.pallas_call(
        attend_kernel,
        grid=(hi - lo,),
        in_specs=[image(D, lo), whole(vectors.shape), whole(weight.shape)] + [ANY] * len(held),
        out_specs=[image(D, lo), image(3 * HALF, lo), image(HALF, lo), image(LANES, lo), image(HALF)],
        out_shape=[
            images(total, D, BF),
            images(total, 3 * HALF, BF),
            images(total, HALF, BF),
            images(total, LANES, F32),
            images(hi - lo, HALF, BF),
        ],
        input_output_aliases={3 + n: n for n in range(len(held))},
        name="attend",
        cost_estimate=cost(),
    )(x, vectors, weight, *held)


def route_kernel(
    which_ref, x_ref, own_ref, got_ref, vec_ref, here_ref, there_ref, router_ref, ids_ref, *refs, count
):
    y_ref, r_ref, g_ref, h_ref = refs[-4:]
    y = x_ref[0].astype(F32) + (
        dot_nt(own_ref[0], here_ref[...]) + dot_nt(got_ref[0], there_ref[...])
    )
    y_ref[0] = y
    hat, _ = normed(y)
    h = (hat * vec_ref[2:3, :] + vec_ref[3:4, :]).astype(BF)
    first = which_ref[0] == 0
    h_ref[0, :, :HALF] = jnp.where(first, h[:, :HALF], h[:, HALF:])
    h_ref[0, :, HALF:] = jnp.where(first, h[:, HALF:], h[:, :HALF])
    lane = lax.broadcasted_iota(jnp.int32, (ROWS, LANES), 1)
    logits = jnp.where(lane < count, dot_nn(h, router_ref[...]), -1e30)
    logits = jnp.exp(logits - jnp.max(logits, axis=1, keepdims=True))
    probs = logits / jnp.sum(logits, axis=1, keepdims=True)
    r_ref[0] = probs
    gates = jnp.zeros((ROWS, LANES), F32)
    for c in range(2):
        gate = jnp.sum(jnp.where(lane == ids_ref[0, :, c : c + 1], probs, 0.0), axis=1, keepdims=True)
        gates = jnp.where(lane == c, gate, gates)
    g_ref[0] = gates


def route(which, x, own, got, vectors, out_here, out_there, router, ids, count, lo, hi, held):
    total = x.shape[0]
    return pl.pallas_call(
        functools.partial(route_kernel, count=count),
        grid_spec=pltpu.PrefetchScalarGridSpec(
            num_scalar_prefetch=1,
            grid=(hi - lo,),
            in_specs=[
                image(D, lo),
                image(HALF),
                image(HALF),
                whole(vectors.shape),
                whole(out_here.shape),
                whole(out_there.shape),
                whole(router.shape),
                image(2, lo),
            ]
            + [ANY] * len(held),
            out_specs=[image(D, lo), image(LANES, lo), image(LANES, lo), image(D)],
        ),
        out_shape=[
            images(total, D, F32),
            images(total, LANES, F32),
            images(total, LANES, F32),
            images(hi - lo, D, BF),
        ],
        input_output_aliases={9 + n: n for n in range(len(held))},
        name="route",
        cost_estimate=cost(),
    )(which, x, own, got, vectors, out_here, out_there, router, ids, *held)


def send_kernel(*refs, parts, chips, gated):
    per = 3 if gated else 2
    groups = [refs[n * per * parts : (n + 1) * per * parts] for n in range(2)]
    out_refs = refs[2 * per * parts :]
    capacity = out_refs[0].shape[1]
    for out_ref, chip in zip(out_refs, chips):
        for r in range(2):
            rows, values, gates = (groups[r][n * parts : (n + 1) * parts] for n in range(3))
            places = lax.broadcasted_iota(jnp.int32, (capacity, 1), 0) + (2 * chip + r) * capacity
            picked = jnp.zeros((capacity, D), F32)
            weight = jnp.zeros((capacity, 1), F32)
            for n in range(parts):
                first = places == rows[n][0:1, :]
                second = places == rows[n][1:2, :]
                chosen = jnp.where(first | second, 1.0, 0.0).astype(BF)
                picked = picked + dot_nn(chosen, values[n][...])
                if gated:
                    each = jnp.where(
                        first, gates[n][0:1, :], jnp.where(second, gates[n][1:2, :], 0.0)
                    )
                    weight = weight + jnp.sum(each, axis=1, keepdims=True)
            if gated:
                picked = picked * weight
            out_ref[r] = picked.astype(BF)


def send_rows(own, other, capacity, chips, gated):
    operands = [part for group in (own, other) for kind in group for part in kind]
    return pl.pallas_call(
        functools.partial(send_kernel, parts=len(own[0]), chips=chips, gated=gated),
        grid=(1,),
        in_specs=[whole(o.shape) for o in operands],
        out_specs=[whole((2, capacity, D))] * len(chips),
        out_shape=[jax.ShapeDtypeStruct((2, capacity, D), BF)] * len(chips),
        name="send_gated" if gated else "send_rows",
        cost_estimate=cost(),
    )(*operands)


def first_lanes():
    row = lax.broadcasted_iota(jnp.int32, (8, LANES), 0)
    return jnp.where(row == lax.broadcasted_iota(jnp.int32, (8, LANES), 1), 1.0, 0.0)


def turn(columns):
    return lax.dot_general(
        first_lanes(), columns, (((1,), (1,)), ((), ())), precision=HIGH, preferred_element_type=F32
    )


def turn_back(rows):
    return lax.dot_general(
        rows, first_lanes(), (((0,), (0,)), ((), ())), precision=HIGH, preferred_element_type=F32
    )


def home_kernel(which_ref, rows_ref, middle_ref, grad_ref, gates_ref, own_ref, other_ref, out_ref, dgate_ref):
    value = middle_ref[0]
    grad = grad_ref[0].astype(F32)
    lane = lax.broadcasted_iota(jnp.int32, (ROWS, LANES), 1)
    found = jnp.zeros((ROWS, LANES), F32)
    chips, capacity = own_ref.shape[:2]
    places = lax.broadcasted_iota(jnp.int32, (1, capacity), 1)
    for c in range(2):
        picked = jnp.zeros((ROWS, HALF), F32)
        for chip in range(chips):
            for r, back_ref in enumerate((own_ref, other_ref)):
                at = rows_ref[0, :, c : c + 1] - (2 * chip + r) * capacity
                chosen = jnp.where(at == places, 1.0, 0.0)
                picked = picked + dot_nn(chosen.astype(BF), back_ref[chip])
        value = value + gates_ref[0, :, c : c + 1] * picked
        dgate = jnp.sum(picked * grad, axis=1, keepdims=True)
        found = jnp.where(lane == c, dgate, found)
    out_ref[0] = value.astype(BF)
    dgate_ref[0] = turn(found)


def bring_home(which, rows, middle, grad, gates, own, other):
    total = middle.shape[0]
    part = pl.BlockSpec((1, ROWS, HALF), lambda i, s: (i, 0, s[0]))
    return pl.pallas_call(
        home_kernel,
        grid_spec=pltpu.PrefetchScalarGridSpec(
            num_scalar_prefetch=1,
            grid=(total,),
            in_specs=[image(2), part, part, image(LANES), whole(own.shape), whole(other.shape)],
            out_specs=[image(HALF), pl.BlockSpec((1, 8, ROWS), lambda i, s: (i, 0, 0))],
        ),
        out_shape=[images(total, HALF, BF), jax.ShapeDtypeStruct((total, 8, ROWS), F32)],
        name="bring_home",
        cost_estimate=cost(),
    )(which, rows, middle, grad, gates, own, other)


def sum_kernel(rows_ref, own_ref, other_ref, out_ref):
    chips, capacity = own_ref.shape[:2]
    places = lax.broadcasted_iota(jnp.int32, (1, capacity), 1)
    total = jnp.zeros((ROWS, HALF), F32)
    for chip in range(chips):
        for r, back_ref in enumerate((own_ref, other_ref)):
            base = (2 * chip + r) * capacity
            chosen = (rows_ref[0, :, 0:1] - base == places) | (rows_ref[0, :, 1:2] - base == places)
            total = total + dot_nn(jnp.where(chosen, 1.0, 0.0).astype(BF), back_ref[chip])
    out_ref[0] = total.astype(BF)


def sum_home(rows, own, other, lo, hi):
    return pl.pallas_call(
        sum_kernel,
        grid=(hi - lo,),
        in_specs=[image(2, lo), whole(own.shape), whole(other.shape)],
        out_specs=image(HALF),
        out_shape=images(hi - lo, HALF, BF),
        name="sum_home",
        cost_estimate=cost(),
    )(rows, own, other)


def gelu_parts(u):
    size = jnp.abs(u)
    t = 1.0 / (1.0 + TAIL_RATE * size)
    poly = jnp.full_like(t, TAIL[-1])
    for c in TAIL[-2::-1]:
        poly = poly * t + c
    bell = jnp.exp(-0.5 * (u * u))
    tail = bell * (t * poly)
    normal = jnp.where(u >= 0.0, 1.0 - tail, tail)
    return u * normal, normal + u * (DENSITY * bell)


def in_order(same_ref, refs):
    same = same_ref[0] == 1
    n, m = len(IN_CUTS), len(BACK_CUTS)
    join = lambda refs, axis: jnp.concatenate([ref[...] for ref in refs], axis=axis)
    pairs = [
        (join(refs[:n], 0), join(refs[n : 2 * n], 0)),
        (join(refs[2 * n : 2 * n + m], 1), join(refs[2 * n + m :], 1)),
    ]
    return [v for a, b in pairs for v in (jnp.where(same, a, b), jnp.where(same, b, a))]


def weight_specs():
    across = [pl.BlockSpec((hi - lo, TILE), lambda i, s: (0, i)) for lo, hi in IN_CUTS]
    down = [pl.BlockSpec((TILE, hi - lo), lambda i, s: (i, 0)) for lo, hi in BACK_CUTS]
    return across * 2 + down * 2


def forward_kernel(same_ref, m_ref, *refs):
    *weights, g_ref, s_ref, zt_ref, zh_ref, acc = refs
    w1h, w1t, w2h, w2t = in_order(same_ref, weights)
    step = pl.program_id(0)
    last = pl.num_programs(0) - 1
    for b in range(m_ref.shape[0]):
        u = dot_nn(m_ref[b, :, :HALF], w1h) + dot_nn(m_ref[b, :, HALF:], w1t)
        g, slope = gelu_parts(u)
        g = g.astype(BF)
        g_ref[b] = g
        s_ref[b] = slope.astype(BF)
        away = dot_nn(g, w2t)
        near = dot_nn(g, w2h)

        @pl.when(step == 0)
        def _():
            acc[b] = away
            zh_ref[b] = near

        @pl.when(step > 0)
        def _():
            acc[b] += away
            zh_ref[b] += near

        @pl.when(step == last)
        def _():
            zt_ref[b] = acc[b].astype(BF)


def expert_forward(same, rows, *weights):
    blocks, capacity, _ = rows.shape
    hidden = weights[0].shape[1]
    wide = pl.BlockSpec((blocks, capacity, TILE), lambda i, s: (0, 0, i))
    make = lambda w, t: jax.ShapeDtypeStruct((blocks, capacity, w), t)
    return pl.pallas_call(
        forward_kernel,
        grid_spec=pltpu.PrefetchScalarGridSpec(
            num_scalar_prefetch=1,
            grid=(hidden // TILE,),
            in_specs=[whole(rows.shape)] + weight_specs(),
            out_specs=[wide, wide] + [whole((blocks, capacity, HALF))] * 2,
            scratch_shapes=[pltpu.VMEM((blocks, capacity, HALF), F32)],
        ),
        out_shape=[make(hidden, BF), make(hidden, BF), make(HALF, BF), make(HALF, F32)],
        name="expert_forward",
        cost_estimate=cost(),
    )(same, rows, *weights)


def backward_kernel(same_ref, z_ref, s_ref, *refs):
    *weights, u_ref, mt_ref, mh_ref, acc = refs
    w1h, w1t, w2h, w2t = in_order(same_ref, weights)
    step = pl.program_id(0)
    last = pl.num_programs(0) - 1
    for b in range(z_ref.shape[0]):
        grad = dot_nt(z_ref[b, :, :HALF], w2h) + dot_nt(z_ref[b, :, HALF:], w2t)
        grad = (grad * s_ref[b].astype(F32)).astype(BF)
        u_ref[b] = grad
        away = dot_nt(grad, w1t)
        near = dot_nt(grad, w1h)

        @pl.when(step == 0)
        def _():
            acc[b] = away
            mh_ref[b] = near

        @pl.when(step > 0)
        def _():
            acc[b] += away
            mh_ref[b] += near

        @pl.when(step == last)
        def _():
            mt_ref[b] = acc[b].astype(BF)


def expert_backward(same, rows, slope, *weights):
    blocks, capacity, _ = rows.shape
    hidden = weights[0].shape[1]
    wide = pl.BlockSpec((blocks, capacity, TILE), lambda i, s: (0, 0, i))
    make = lambda w, t: jax.ShapeDtypeStruct((blocks, capacity, w), t)
    return pl.pallas_call(
        backward_kernel,
        grid_spec=pltpu.PrefetchScalarGridSpec(
            num_scalar_prefetch=1,
            grid=(hidden // TILE,),
            in_specs=[whole(rows.shape), wide] + weight_specs(),
            out_specs=[wide] + [whole((blocks, capacity, HALF))] * 2,
            scratch_shapes=[pltpu.VMEM((blocks, capacity, HALF), F32)],
        ),
        out_shape=[make(hidden, BF), make(HALF, BF), make(HALF, F32)],
        name="expert_backward",
        cost_estimate=cost(),
    )(same, rows, slope, *weights)


def outer_kernel(which_ref, *refs, chunks, hidden_first, added):
    step = pl.program_id(0)
    wides = refs[:chunks]
    narrows = refs[chunks : 2 * chunks]
    out_ref = refs[-1]
    total = None
    for wide_ref, slim_ref in zip(wides, narrows):
        for b in range(wide_ref.shape[0]):
            slim = slim_ref[b]
            term = dot_tn(wide_ref[b], slim) if hidden_first else dot_tn(slim, wide_ref[b])
            total = term if total is None else total + term
    if added == 1:
        total = total + refs[-2][...].astype(F32)
    elif added == 2 and not hidden_first:
        total = total + jnp.concatenate([refs[-3][...], refs[-2][...]], axis=0).astype(F32)
    elif added == 2:
        total = total + jnp.where(step == 0, refs[-3][...], refs[-2][...]).astype(F32)
    out_ref[...] = total.astype(out_ref.dtype)


def outer(which, wides, narrows, hidden_first, extra=None):
    per, capacity, hidden = wides[0].shape
    slim = pl.BlockSpec((per, capacity, HALF), lambda i, s: (0, 0, s[0]))
    if hidden_first:
        shape, out = (hidden, HALF), pl.BlockSpec((TILE, HALF), lambda i, s: (i, 0))
    else:
        shape, out = (HALF, hidden), pl.BlockSpec((HALF, TILE), lambda i, s: (0, i))
    specs = [pl.BlockSpec((per, capacity, TILE), lambda i, s: (0, 0, i))] * len(wides)
    specs += [slim] * len(narrows)
    operands = list(wides) + list(narrows)
    extra = [] if extra is None else list(extra)
    if len(extra) == 1:
        specs.append(out)
    elif len(extra) == 2 and not hidden_first:
        specs += [pl.BlockSpec((HALF // 2, TILE), lambda i, s: (0, i))] * 2
    elif len(extra) == 2:
        specs.append(pl.BlockSpec((TILE, HALF), lambda i, s: (0, 0)))
        specs.append(pl.BlockSpec((TILE, HALF), lambda i, s: (jnp.maximum(i - 1, 0), 0)))
    operands += extra
    return pl.pallas_call(
        functools.partial(
            outer_kernel,
            chunks=len(wides),
            hidden_first=hidden_first,
            added=len(extra),
        ),
        grid_spec=pltpu.PrefetchScalarGridSpec(
            num_scalar_prefetch=1, grid=(hidden // TILE,), in_specs=specs, out_specs=out
        ),
        out_shape=jax.ShapeDtypeStruct(shape, F32 if extra else BF),
        name="outer_keep" if extra else "outer_send",
        cost_estimate=cost(),
    )(which, *operands)


def norm_back(grad, hat, scale, gain):
    inner = grad * gain
    return scale * (
        inner
        - jnp.mean(inner, axis=-1, keepdims=True)
        - hat * jnp.mean(inner * hat, axis=-1, keepdims=True)
    )


def add_sums(ref, grad, hat, first):
    sums = [jnp.sum(grad * hat, axis=0, keepdims=True), jnp.sum(grad, axis=0, keepdims=True)]

    @pl.when(first)
    def _():
        ref[...] = jnp.zeros_like(ref)

    ref[0:1, :] += sums[0]
    ref[1:2, :] += sums[1]


def attend_back_kernel(
    which_ref,
    x_ref,
    y_ref,
    near_ref,
    away_ref,
    dgate_ref,
    dgate2_ref,
    probs_ref,
    ids_ref,
    narrow_ref,
    cot_ref,
    vec_ref,
    out_w_ref,
    qkv_ref,
    lse_ref,
    w_ref,
    *refs,
):
    dy_ref, dyb_ref, dqkv_ref, part_ref, sums2_ref, sums1_ref, router_ref, att_ref = refs[-8:]
    first = which_ref[0] == 0
    start = pl.program_id(0) == 0
    near = near_ref[0].astype(F32)
    away = away_ref[0].astype(F32)
    dgate = turn_back(dgate_ref[0] + dgate2_ref[0])
    lane = lax.broadcasted_iota(jnp.int32, (ROWS, LANES), 1)
    probs = probs_ref[0]
    grad_probs = sum(
        jnp.where(lane == ids_ref[0, :, c : c + 1], dgate[:, c : c + 1], 0.0) for c in range(2)
    )
    grad_logits = probs * (grad_probs - jnp.sum(probs * grad_probs, axis=1, keepdims=True))
    high = grad_logits.astype(BF)
    low = (grad_logits - high.astype(F32)).astype(BF)
    narrow = narrow_ref[...]
    grad = (dot_nt(high, narrow) + dot_nt(low, narrow)) + jnp.concatenate(
        [jnp.where(first, near, away), jnp.where(first, away, near)], axis=1
    )
    hat, scale = normed(y_ref[0])
    h = (hat * vec_ref[2:3, :] + vec_ref[3:4, :]).astype(BF)
    grad_router = dot_tn(high, h) + dot_tn(low, h)

    @pl.when(start)
    def _():
        router_ref[...] = grad_router

    @pl.when(jnp.logical_not(start))
    def _():
        router_ref[...] += grad_router

    add_sums(sums2_ref, grad, hat, start)
    dy = cot_ref[0].astype(F32) + norm_back(grad, hat, scale, vec_ref[2:3, :])
    dy_ref[0] = dy
    dyb = dy.astype(BF)
    dyb_ref[0] = dyb
    att_ref[...] = dot_nn(dyb, out_w_ref[...]).astype(BF)
    keys_in = lax.broadcasted_iota(jnp.int32, (ROWS, ROWS), 1) < SEQ
    for h in range(HALF // HEAD):
        at = h * HEAD
        q = qkv_ref[0, :, at : at + HEAD]
        k = qkv_ref[0, :, HALF + at : HALF + at + HEAD]
        v = qkv_ref[0, :, 2 * HALF + at : 2 * HALF + at + HEAD]
        do = att_ref[:, at : at + HEAD]
        s = jnp.where(keys_in, dot_nt(q, k) * SCALE, -1e30)
        weights = jnp.exp(s - lse_ref[0, :, h : h + 1])
        dv = dot_tn(weights.astype(BF), do)
        dp = dot_nt(do, v)
        ds = (weights * (dp - jnp.sum(weights * dp, axis=1, keepdims=True))).astype(BF)
        dqkv_ref[0, :, at : at + HEAD] = (dot_nn(ds, k) * SCALE).astype(BF)
        dqkv_ref[0, :, HALF + at : HALF + at + HEAD] = (dot_tn(ds, q) * SCALE).astype(BF)
        dqkv_ref[0, :, 2 * HALF + at : 2 * HALF + at + HEAD] = dv.astype(BF)
    part = dot_nt(dqkv_ref[0], w_ref[...])
    part_ref[0] = part.astype(BF)
    hat, _ = normed(x_ref[0].astype(F32))
    add_sums(sums1_ref, part, hat, start)


def attend_back(which, x, y, near, away, dgate, dgate2, probs, ids, narrow, cot, vectors, out_w, qkv, lse, weight, lo, hi, held):
    total = y.shape[0]
    turned = pl.BlockSpec((1, 8, ROWS), lambda i, s: (i + lo, 0, 0))
    return pl.pallas_call(
        attend_back_kernel,
        grid_spec=pltpu.PrefetchScalarGridSpec(
            num_scalar_prefetch=1,
            grid=(hi - lo,),
            in_specs=[
                image(D, lo),
                image(D, lo),
                image(HALF, lo),
                image(HALF, lo),
                turned,
                turned,
                image(LANES, lo),
                image(2, lo),
                whole(narrow.shape),
                image(D, lo),
                whole(vectors.shape),
                whole(out_w.shape),
                image(3 * HALF, lo),
                image(LANES, lo),
                whole(weight.shape),
            ]
            + [ANY] * len(held),
            out_specs=[
                image(D, lo),
                image(D, lo),
                image(3 * HALF, lo),
                image(D),
                whole((8, D)),
                whole((8, D)),
                whole((LANES, D)),
            ],
            scratch_shapes=[pltpu.VMEM((ROWS, HALF), BF)],
        ),
        out_shape=[
            images(total, D, F32),
            images(total, D, BF),
            images(total, 3 * HALF, BF),
            images(hi - lo, D, BF),
            jax.ShapeDtypeStruct((8, D), F32),
            jax.ShapeDtypeStruct((8, D), F32),
            jax.ShapeDtypeStruct((LANES, D), F32),
        ],
        input_output_aliases={16 + n: n for n in range(len(held))},
        name="attend_back",
        cost_estimate=cost(),
    )(which, x, y, near, away, dgate, dgate2, probs, ids, narrow, cot, vectors, out_w, qkv, lse, weight, *held)


def token_kernel(x_ref, own_ref, got_ref, dy_ref, vec_ref, *refs):
    out_ref = refs[-1]
    grad = own_ref[0].astype(F32) + got_ref[0].astype(F32)
    hat, scale = normed(x_ref[0].astype(F32))
    out_ref[0] = dy_ref[0] + norm_back(grad, hat, scale, vec_ref[0:1, :])


def token_back(x, own, got, dy, vectors, lo, hi, held):
    total = x.shape[0]
    return pl.pallas_call(
        token_kernel,
        grid=(hi - lo,),
        in_specs=[image(D, lo), image(D), image(D), image(D, lo), whole(vectors.shape)]
        + [ANY] * len(held),
        out_specs=image(D, lo),
        out_shape=images(total, D, F32),
        input_output_aliases={5 + n: n for n in range(len(held))},
        name="token_back",
        cost_estimate=cost(),
    )(x, own, got, dy, vectors, *held)


def exact(a, b, contract):
    return lax.dot_general(
        a, b, ((contract[:1], contract[1:]), ((), ())), precision=HIGH, preferred_element_type=F32
    )


def of_image(i, tok):
    row = lax.broadcasted_iota(jnp.int32, (ROWS, tok), 0)
    token = lax.broadcasted_iota(jnp.int32, (ROWS, tok), 1)
    return jnp.where((token == row + i * SEQ) & (row < SEQ), 1.0, 0.0)


def image_kernel(which_ref, tok_ref, cot_ref, x_ref, cot_out_ref, here_ref):
    mine = of_image(pl.program_id(0), tok_ref.shape[0]).astype(BF)
    x_ref[0] = dot_nn(mine, tok_ref[...]).astype(BF)
    cot = dot_nn(mine, cot_ref[...]).astype(BF)
    cot_out_ref[0] = cot
    first = which_ref[0] == 0
    here_ref[0, :, :HALF] = jnp.where(first, cot[:, :HALF], cot[:, HALF:])
    here_ref[0, :, HALF:] = jnp.where(first, cot[:, HALF:], cot[:, :HALF])


def image_rows(which, tokens, cotangent):
    pictures = tokens.shape[0] // SEQ
    return pl.pallas_call(
        image_kernel,
        grid_spec=pltpu.PrefetchScalarGridSpec(
            num_scalar_prefetch=1,
            grid=(pictures,),
            in_specs=[whole(tokens.shape)] * 2,
            out_specs=[image(D)] * 3,
        ),
        out_shape=[images(pictures, D, BF)] * 3,
        name="image_rows",
        cost_estimate=cost(),
    )(which, tokens, cotangent)


def slot_kernel(here_ref, ids_ref, rows_ref, lanes_ref, ids_out_ref, *, capacity):
    tok = ids_ref.shape[0]
    lane = lax.broadcasted_iota(jnp.int32, (tok, LANES), 1)
    earlier = jnp.where(
        lax.broadcasted_iota(jnp.int32, (tok, tok), 1) < lax.broadcasted_iota(jnp.int32, (tok, tok), 0),
        1.0, 0.0,
    ).astype(BF)
    ids = [ids_ref[:, c : c + 1] for c in range(2)]
    taken = jnp.zeros((1, LANES), F32)
    table = jnp.zeros((tok, LANES), F32)
    for c in range(2):
        onehot = jnp.where(lane == ids[c], 1.0, 0.0)
        before = dot_nn(earlier, onehot.astype(BF)) + taken
        slot = jnp.sum(before * onehot, axis=1, keepdims=True)
        taken = taken + jnp.sum(onehot, axis=0, keepdims=True)
        place = ((ids[c] ^ here_ref[0]) * capacity).astype(F32) + slot + 1.0
        table = jnp.where(lane == c, place, table)
        table = jnp.where(lane == 2 + c, ids[c].astype(F32) + 1.0, table)
    for i in range(rows_ref.shape[0]):
        part = exact(of_image(i, tok), table, (1, 0)) - 1.0
        whole_part = part.astype(jnp.int32)
        rows_ref[i] = whole_part[:, 0:2]
        ids_out_ref[i] = whole_part[:, 2:4]
        lanes_ref[:, i * ROWS : (i + 1) * ROWS] = exact(first_lanes(), part, (1, 1)).astype(jnp.int32)


def slot_rows(here, expert_ids, capacity):
    tok = expert_ids.shape[0]
    pictures = tok // SEQ
    shapes = [(pictures, ROWS, 2), (8, pictures * ROWS), (pictures, ROWS, 2)]
    rows, lanes, ids = pl.pallas_call(
        functools.partial(slot_kernel, capacity=capacity),
        grid_spec=pltpu.PrefetchScalarGridSpec(
            num_scalar_prefetch=1,
            grid=(1,),
            in_specs=[whole(expert_ids.shape)],
            out_specs=[whole(shape) for shape in shapes],
        ),
        out_shape=[jax.ShapeDtypeStruct(shape, jnp.int32) for shape in shapes],
        name="slot_rows",
        cost_estimate=cost(),
    )(flag(here), expert_ids)
    return rows, lanes, ids


def projection_kernel(core_ref, *refs, parts, split):
    a_ref, dqkv_ref, dyb_ref, o_ref = refs[:4]
    routers, ones, twos = (refs[4 + n * parts : 4 + (n + 1) * parts] for n in range(3))
    out_ref = refs[-1]
    step = pl.program_id(0)
    last = pl.num_programs(0) - 1
    qkv = dot_tn(a_ref[0], dqkv_ref[0])
    out = dot_tn(dyb_ref[0], o_ref[0])

    @pl.when(step == 0)
    def _():
        out_ref[:, : 3 * HALF] = qkv
        out_ref[:, 3 * HALF : 4 * HALF] = out
        total = 0.5 * sum(r[...] for r in routers)
        sums = jnp.concatenate(
            [sum(r[0:2, :] for r in ones), 0.5 * sum(r[0:2, :] for r in twos), jnp.zeros((4, D), F32)],
            axis=0,
        )
        out_ref[:, 4 * HALF :] = jnp.transpose(
            jnp.concatenate([total[: LANES - 8], sums], axis=0)
        )

    @pl.when(step > 0)
    def _():
        out_ref[:, : 3 * HALF] += qkv
        out_ref[:, 3 * HALF : 4 * HALF] += out

    if split:

        @pl.when(step == last)
        def _():
            near_ref, away_ref = refs[-3:-1]
            dps, chips, rows, _ = near_ref.shape
            for d in range(dps):
                for chip in range(chips):
                    at = (2 * (d * chips + chip) + core_ref[0]) * rows
                    near_ref[d, chip] = out_ref[pl.ds(pl.multiple_of(at, 16), rows), :]
                    at = (2 * (d * chips + chip) + 1 - core_ref[0]) * rows
                    away = out_ref[pl.ds(pl.multiple_of(at, 16), rows), :]
                    away_ref[d, chip] = away.astype(BF)


def projection_grads(a_rows, dqkv, dyb, o_rows, *small):
    count = lax.axis_size("expert")
    core = lax.axis_index("expert") & 1
    rows = D // (2 * count)
    split = rows % 16 == 0
    shape = (D, 4 * HALF + LANES)
    shares = (2, count // 2, rows, shape[1])
    kinds = [(shares, F32), (shares, BF)] if split else [(shape, F32)]
    out = pl.pallas_call(
        functools.partial(projection_kernel, parts=len(small) // 3, split=split),
        grid_spec=pltpu.PrefetchScalarGridSpec(
            num_scalar_prefetch=1,
            grid=(a_rows.shape[0],),
            in_specs=[image(D), image(3 * HALF), image(D), image(HALF)]
            + [whole(v.shape) for v in small],
            out_specs=[whole(k) for k, _ in kinds],
            scratch_shapes=[pltpu.VMEM(shape, F32)] if split else [],
        ),
        out_shape=[jax.ShapeDtypeStruct(*kind) for kind in kinds],
        name="projection_grads",
        cost_estimate=cost(),
    )(flag(core), a_rows, dqkv, dyb, o_rows, *small)
    if split:
        return out
    blocks = out[0].reshape((2, count // 2, 2, rows, -1))
    return pick(blocks, core, 2), pick(blocks, 1 - core, 2).astype(BF)


def on_device(
    tokens,
    cotangent,
    ln1_gain,
    ln1_bias,
    ln2_gain,
    ln2_bias,
    w_query,
    w_key,
    w_value,
    w_out,
    w_router,
    w_in,
    w_back,
    expert_ids,
):
    count = lax.axis_size("expert")
    chips = count // 2
    tok = tokens.shape[0]
    capacity = (10 * tok + 32 * count - 1) // (32 * count) * 8
    pictures = tok // SEQ
    rows_all = pictures * ROWS
    cut = (pictures + 1) // 2
    groups = [(0, cut), (cut, pictures)] if pictures > 1 else [(0, pictures)]
    lanes_of = lambda value: [value[:, lo * ROWS : hi * ROWS] for lo, hi in groups]
    here = lax.axis_index("expert")
    here_dp = lax.axis_index("dp")
    here_t = lax.axis_index("tensor")
    which = here_t.astype(jnp.int32).reshape(1)
    same = here_t == here_dp

    order = Order()

    small = jnp.stack([ln1_gain, ln1_bias, ln2_gain, ln2_bias], axis=1)
    narrow = jnp.concatenate([w_router, small], axis=1)
    narrow = jnp.pad(narrow, ((0, 0), (0, LANES - narrow.shape[1])))
    first_pack = jnp.concatenate(
        [w_query, w_key, w_value, narrow, jnp.transpose(w_out)], axis=1
    ).astype(BF)
    pair = cross(first_pack)
    in_own = [follow(w_in, first_pack)[0, lo:hi].astype(BF) for lo, hi in IN_CUTS]
    back_own = [follow(w_back, first_pack)[0, :, lo:hi].astype(BF) for lo, hi in BACK_CUTS]
    pair, in_own, back_own = order.wait((pair, in_own, back_own))

    same_chips = stacked(chip_copies(order.after(pair)))
    in_other = [hop(order.after(in_own[0]), "dp", 1)]
    x, cot, cot_here = order.run(lambda *v: image_rows(which, *v), tokens, cotangent)
    cot_here = cot_here.reshape(rows_all, D)
    rows, rows_lanes, ids_pad = order.run(lambda v: slot_rows(here, v, capacity), expert_ids)
    same_chips, in_other[0] = order.wait((same_chips, in_other[0]))
    rows_lane = order.wait(rows_lanes[:2])
    in_other.append(hop(order.after(in_own[1]), "dp", 1))
    rows_next = hop(order.after(rows_lane), "expert", 1)
    cot_next = hop(order.after(cot_here), "expert", 1)
    flipped = order.wait(hop(order.after(same_chips), "expert", 1))
    qkv_w, narrow_all, out_here = order.run(
        lambda *v: assemble(*v, (3 * HALF, LANES, HALF)), same_chips, flipped
    )
    out_there = hop(order.after(out_here), "tensor", 1)
    vectors = order.run(lambda v: vectors_of(v, count), narrow_all)
    in_other[1] = order.wait(in_other[1])
    in_other.append(hop(order.after(in_own[2]), "dp", 1))
    rows_next, cot_next = order.wait((rows_next, cot_next))
    own_lanes, next_lanes = order.wait((lanes_of(rows_lane), lanes_of(rows_next)))

    held, o_parts, got_parts = [], [], []
    for n, (lo, hi) in enumerate(groups):
        *held, o_part = order.run(
            lambda x, v, w, *h: attend(x, v, w, lo, hi, h), x, vectors, qkv_w, *held
        )
        o_parts.append(o_part)
        got_parts.append(hop(o_part, "tensor", 1))
    a_rows, qkv, o_rows, lse = held
    out_there = order.wait(out_there)
    got_parts, in_other[2] = order.wait((got_parts, in_other[2]))
    back_other = [hop(order.after(back_own[0]), "dp", 1)]
    held, h_parts, h_next = [], [], []
    for n, (lo, hi) in enumerate(groups):
        *held, h_part = order.run(
            lambda x, o, g, v, w, t, r, i, *h: route(which, x, o, g, v, w, t, r, i, count, lo, hi, h),
            x, o_parts[n], got_parts[n], vectors, out_here, out_there, narrow_all, ids_pad, *held,
        )
        h_parts.append(h_part.reshape(-1, D))
        if n == len(groups) - 1:
            gates_lane = jnp.transpose(held[2].reshape(rows_all, LANES)[:, :2])
            back_other[0], gates_lane = order.wait((back_other[0], gates_lane))
            h_parts[-1] = order.after(h_parts[-1])
            back_other.append(hop(order.after(back_own[1]), "dp", 1))
        h_next.append(hop(h_parts[-1], "expert", 1))
    y, probs, gates = held
    gates_next = hop(order.after(gates_lane), "expert", 1)

    own = (own_lanes, h_parts)
    other = (next_lanes, h_next)
    far = list(range(1, chips))
    outgoing = order.run(lambda *v: send_rows(*v, capacity, far, False), own, other)
    arrived = [None] + [hop(o, "expert", 2 * c) for o, c in zip(outgoing, far)]
    (arrived[0],) = order.run(lambda *v: send_rows(*v, capacity, [0], False), own, other)
    gates_next = order.wait(gates_next)
    own = ([rows_lane], [cot_here], [gates_lane])
    other = ([rows_next], [cot_next], [gates_next])
    grad_outgoing = order.run(lambda *v: send_rows(*v, capacity, far, True), own, other)
    grad_arrived = [None] * chips
    (grad_arrived[0],) = order.run(lambda *v: send_rows(*v, capacity, [0], True), own, other)
    back_other[1] = order.wait(back_other[1])
    weights = (*in_own, *in_other, *back_own, *back_other)
    same = flag(same)

    hidden, slopes, grads = [], [], []
    came_back, grad_home = [None] * chips, [None] * chips

    def back_to(chip, waiting):
        value = order.run(add_halves, *waiting)
        return hop(value, "expert", 2 * chip) if chip else value

    leaving = []

    def settle_oldest():
        home, chip, waiting = leaving.pop(0)
        home[chip] = back_to(chip, waiting)

    for c in range(chips):
        if c == 1:
            arrived[1:] = order.wait(arrived[1:])
            if chips <= 4:
                grad_arrived[1:] = [
                    hop(order.after(o), "expert", 2 * k) for o, k in zip(grad_outgoing, far)
                ]
        if c and chips > 4:
            grad_arrived[c] = hop(order.after(grad_outgoing[c - 1]), "expert", 2 * c)
        if c == chips - 1 and chips <= 4:
            grad_arrived[1:] = order.wait(grad_arrived[1:])
        g, s, zt, zh = order.run(lambda *v: expert_forward(same, *v), arrived[c], *weights)
        hidden.append(g)
        slopes.append(s)
        if len(leaving) > 1:
            settle_oldest()
        leaving.append((came_back, c, (zh, hop(order.after(zt), "tensor", 1))))
    for c in range(chips):
        if c and chips > 4:
            grad_arrived[c] = order.wait(grad_arrived[c])
        u, mt, mh = order.run(
            lambda *v: expert_backward(same, *v), grad_arrived[c], slopes[c], *weights
        )
        grads.append(u)
        settle_oldest()
        leaving.append((grad_home, c, (mh, hop(order.after(mt), "tensor", 1))))
        if c >= chips // 2:
            step = 2 * (chips - 1) // chips
            for k in range(1 + (c - chips // 2) * step, 1 + (c - chips // 2 + 1) * step):
                came_back[k] = order.wait(came_back[k])
    z_here, z_there = order.run(lambda *v: sort_groups(v), *order.wait(tuple(came_back)))
    z_there = hop(z_there, "expert", 1)
    send_half = same
    settle_oldest()
    back_send = order.run(lambda h, g: outer(send_half, h, g, True), hidden, grad_arrived)
    back_send = order.wait([back_send[:TILE], back_send[TILE:]])
    settle_oldest()
    back_got = [hop(order.after(back_send[0]), "dp", 1)]
    in_send = order.run(lambda g, a: outer(send_half, g, a, False), grads, arrived)
    grad_home = list(order.wait(tuple(grad_home)))
    m_here, m_there = order.run(lambda *v: sort_groups(v), *grad_home)
    back_got[0], in_send = order.wait((back_got[0], in_send))
    in_send = order.wait([in_send[: HALF // 2], in_send[HALF // 2 :]])
    back_got.append(hop(order.after(back_send[1]), "dp", 1))
    m_there = hop(order.after(m_there), "expert", 1)

    out_half, dgate = order.run(
        lambda *v: bring_home(which, *v), rows, y, cot, gates, z_here, z_there
    )
    dgate_next = hop(dgate, "tensor", 1)
    m_there = order.wait(m_there)
    near = order.run(lambda *v: sum_home(*v, 0, pictures), rows, m_here, m_there)
    away = hop(near, "tensor", 1)
    back_got, dgate_next = order.wait((back_got, dgate_next))
    in_got = [hop(order.after(in_send[0]), "dp", 1)]
    away = order.wait(away)
    held, parts, sums, got = [], [], [], []
    for n, (lo, hi) in enumerate(groups):
        *held, part, sums2, sums1, grad_router = order.run(
            lambda *v: attend_back(which, *v[:15], lo, hi, v[15:]),
            x, y, near, away, dgate, dgate_next, probs, ids_pad, narrow_all, cot, vectors, out_here, qkv, lse, qkv_w, *held,
        )
        parts.append(part)
        if n == 0:
            in_got[0] = order.wait(in_got[0])
            in_got.append(hop(order.after(in_send[1]), "dp", 1))
            part = order.after(part)
        got.append(hop(part, "tensor", 1))
        sums.append((grad_router, sums1, sums2))
    dy, dyb, dqkv = held

    routers, ones, twos = zip(*sums)
    total, total_away = order.run(
        projection_grads, a_rows, dqkv, dyb, o_rows, *routers, *ones, *twos
    )
    keep_half = 1 - send_half
    got[0], in_got[1] = order.wait((got[0], in_got[1]))
    total_got = hop(order.after(total_away), "expert", 1)
    grad_back = order.run(
        lambda h, g, b: outer(keep_half, h, g, True, b), hidden, grad_arrived, back_got
    )[None]
    total_got = order.wait(total_got)
    shards, leaving = chip_sum(order.wait(total + total_got.astype(F32)), BF)
    grad_in = order.run(
        lambda g, a, b: outer(keep_half, g, a, False, b), grads, arrived, in_got
    )[None]
    shards, leaving, got = order.wait((shards, leaving, got))
    entering = hop(leaving, "dp", 1)
    out_other = hop(order.after(out_half), "tensor", 1)
    grad_tokens = []
    for n, (lo, hi) in enumerate(groups):
        grad_tokens = [
            order.run(
                lambda *v: token_back(*v[:5], lo, hi, v[5:]),
                x, parts[n], got[n], dy, vectors, *grad_tokens,
            )
        ]
    shards, out_other = order.wait((shards + entering.astype(F32), out_other))
    tiny = shards[:, 4 * HALF :]
    tiny = tiny + hop(tiny, "tensor", 1)
    grad_tokens = grad_tokens[0][:, :SEQ].reshape(tok, D)
    block_out = jnp.where(
        here_t == 0,
        jnp.concatenate([out_half, out_other], axis=2),
        jnp.concatenate([out_other, out_half], axis=2),
    )
    block_out = block_out[:, :SEQ].reshape(tok, D)
    return (
        block_out,
        grad_tokens,
        tiny[:, LANES - 8],
        tiny[:, LANES - 7],
        tiny[:, LANES - 6],
        tiny[:, LANES - 5],
        shards[:, :HALF],
        shards[:, HALF : 2 * HALF],
        shards[:, 2 * HALF : 3 * HALF],
        jnp.transpose(shards[:, 3 * HALF : 4 * HALF]),
        tiny[:, :count],
        grad_in,
        grad_back,
    )


def solution(mesh):
    rows = ("dp", "expert")
    in_specs = (
        P(rows, None),
        P(rows, None),
        P(rows),
        P(rows),
        P(rows),
        P(rows),
        P(rows, "tensor"),
        P(rows, "tensor"),
        P(rows, "tensor"),
        P("tensor", rows),
        P(rows, None),
        P("expert", "dp", "tensor"),
        P("expert", "tensor", "dp"),
        P(rows, None),
    )
    out_specs = (
        P(rows, None),
        P(rows, None),
        P(rows),
        P(rows),
        P(rows),
        P(rows),
        P(rows, "tensor"),
        P(rows, "tensor"),
        P(rows, "tensor"),
        P("tensor", rows),
        P(rows, None),
        P("expert", "dp", "tensor"),
        P("expert", "tensor", "dp"),
    )
    return jax.shard_map(
        on_device, mesh=mesh, in_specs=in_specs, out_specs=out_specs, check_vma=False
    )
```
